128 devices in a mesh: cp: 32 (over z, y, x_lo), fsdp: 4 (over x_hi, core).
Axes of the slice: x: 4 (x_hi: 2, x_lo: 2; x = x_hi * 2 + x_lo), y: 4, z: 4, core: 2. Of those that a mesh axis runs over, the one named last changes fastest.
Arguments:
- query_states: bfloat16 [4, 4096, 1024], P('fsdp', 'cp'), may hold values from -32 to 32
- key_states: bfloat16 [4, 4096, 1024], P('fsdp', 'cp'), may hold values from -32 to 32
- value_states: bfloat16 [4, 4096, 1024], P('fsdp', 'cp'), may hold values from -6 to 6
- span_order: int32 [64], replicated, may hold values from 0 to 63, as said below
- block_mask: int32 [64, 64], replicated, may hold values from 0 to 1, as said below
- output_weight: bfloat16 [1024, 2048], P(('cp', 'fsdp')), may hold values from -0.1875 to 0.1875
- upstream: bfloat16 [4, 4096, 2048], P('fsdp', 'cp'), may hold values from -6 to 6
Outputs:
- projected: bfloat16 [4, 4096, 2048], P('fsdp', 'cp')
- query_gradient: bfloat16 [4, 4096, 1024], P('fsdp', 'cp')
- key_gradient: bfloat16 [4, 4096, 1024], P('fsdp', 'cp')
- value_gradient: bfloat16 [4, 4096, 1024], P('fsdp', 'cp')
- weight_gradient: float32 [1024, 2048], P(('cp', 'fsdp'))
The draws below stay inside these ranges and needn't reach their ends.
Inputs may be any that keep to these rules, and one draw needn't show every extreme that they name: `span_order`: entries 2 d and 2 d + 1 hold positions p and 63 - p; every position appears once. `block_mask`: the diagonal is 1.
All inputs are finite; a program needn't handle non-finite values.
Results may differ from the reference program's by a relative error of at most 0.024.
Values may be sent and summed in bfloat16 or wider, within the bound.
No kernel may reach another device: no remote copies, remote signals or barrier semaphores. Data moves between devices by JAX's collectives and lax.ppermute only.
A program may use at most 128 MiB of HBM per device.

```python
import jax
import jax.numpy as jnp
from jax import lax

D = 2048
HEADS = 8
HEAD = 128
TOK_DEV = 128
HD = 1024
CH = 64
NCH = 64
LEN = 4096
SEQS = 4
N_CP = 32


def base_draw(key, salt):
    subkey = jax.random.fold_in(key, salt)
    values = jnp.clip(5.0 * jax.random.normal(subkey, (SEQS, LEN, HEADS * HEAD), jnp.float32), -32.0, 32.0)
    return values


def draw_query_states(key, part):
    values = base_draw(key, 11)
    return values.astype(jnp.bfloat16)


def draw_key_states(key, part):
    values = base_draw(key, 23)
    return values.astype(jnp.bfloat16)


def draw_span_order(key, part):
    pair_count = NCH // 2
    shuffled = jax.random.permutation(key, pair_count)
    paired = jnp.stack([shuffled, NCH - 1 - shuffled], axis=1).reshape(NCH)
    return paired.astype(jnp.int32)


def draw_block_mask(key, part):
    random_bits = jax.random.randint(key, (NCH, NCH), 0, 2)
    diagonal = jnp.arange(NCH)[:, None] == jnp.arange(NCH)[None, :]
    return jnp.where(diagonal, 1, random_bits).astype(jnp.int32)


def block_scale(rng, extent, pieces, least, top_value):
    def one(dim, blocks):
        draws = jax.random.uniform(jax.random.fold_in(jax.random.fold_in(rng, 6), dim), (blocks,), jnp.float32, least / len(pieces), top_value / len(pieces))
        return jnp.repeat(jnp.exp(draws), extent[dim] // blocks).reshape((-1,) + (1,) * (len(extent) - dim - 1))

    factor_of = one(*pieces[0])
    for cut in pieces[1:]:
        factor_of = factor_of * one(*cut)
    return factor_of


def normal_values(rng, dims, width, most, shards=(), kind=jnp.bfloat16):
    values = width * jax.random.normal(rng, dims, jnp.float32)
    if shards:
        values = values * block_scale(rng, dims, shards, -0.22, 0.18)
    return jnp.clip(values, -most, most).astype(kind)


def setup_inputs(seed: int = 0) -> dict:
    splits = jax.random.split(jax.random.key(seed), 8)
    query_states = draw_query_states(jax.random.fold_in(splits[7], 71), 0)
    key_states = draw_key_states(jax.random.fold_in(splits[7], 71), 0)
    value_states = normal_values(splits[2], (SEQS, LEN, HD), 1.0, 6.0, ((0, 4), (1, 32)))
    span_order = draw_span_order(jax.random.fold_in(splits[7], 71), 0)
    block_mask = draw_block_mask(jax.random.fold_in(splits[7], 71), 0)
    output_weight = normal_values(splits[5], (HD, D), HD ** -0.5, 0.1875, ((0, 128),))
    upstream = normal_values(splits[6], (SEQS, LEN, D), 1.0, 6.0, ((0, 4), (1, 32)))
    return {"query_states": query_states, "key_states": key_states, "value_states": value_states, "span_order": span_order, "block_mask": block_mask, "output_weight": output_weight, "upstream": upstream}


def reference(query_states, key_states, value_states, span_order, block_mask, output_weight, upstream):
    span_rows = CH
    positions = (span_order[:, None] * span_rows + jnp.arange(span_rows, dtype=jnp.int32)[None, :]).reshape(-1)
    onehot = (span_order[:, None] == jnp.arange(NCH, dtype=jnp.int32)[None, :]).astype(jnp.float32)
    span_ok = jnp.dot(jnp.dot(onehot, block_mask.astype(jnp.float32)), onehot.T) > 0.5
    row_span = jnp.arange(LEN, dtype=jnp.int32) // span_rows
    score_scale = 1.0 / HEAD

    def one_sequence(arrays):
        queries, key_all, value_all, grad_all = arrays
        key_f32 = key_all.astype(jnp.float32).reshape(LEN, HEADS, HEAD)
        value_f32 = value_all.astype(jnp.float32).reshape(LEN, HEADS, HEAD)

        def block_step(carry, step_index):
            key_sum, value_sum, weight_sum = carry
            begin_row = step_index * TOK_DEV
            query_block = lax.dynamic_slice_in_dim(queries, begin_row, TOK_DEV)
            grad_rows = lax.dynamic_slice_in_dim(grad_all, begin_row, TOK_DEV)
            query_pos = lax.dynamic_slice_in_dim(positions, begin_row, TOK_DEV)
            query_span = lax.dynamic_slice_in_dim(row_span, begin_row, TOK_DEV)
            allowed = span_ok[query_span][:, row_span] & (positions[None, :] <= query_pos[:, None])
            query_f32 = query_block.astype(jnp.float32).reshape(TOK_DEV, HEADS, HEAD)
            scores = jnp.einsum('qhd,khd->hqk', query_f32, key_f32) * score_scale
            masked = jnp.where(allowed[None], scores, -jnp.inf)
            row_max = masked.max(-1)
            exp_terms = jnp.where(allowed[None], jnp.exp(scores - row_max[..., None]), 0.0)
            log_total = row_max + jnp.log(exp_terms.sum(-1))
            probability = jnp.where(allowed[None], jnp.exp(scores - log_total[..., None]), 0.0)
            probability_low = lax.optimization_barrier(probability.astype(jnp.bfloat16))
            attended = jnp.einsum('hqk,khd->qhd', probability_low.astype(jnp.float32), value_f32)
            attended = lax.optimization_barrier(attended.reshape(TOK_DEV, HD).astype(jnp.bfloat16))
            projected = jnp.dot(attended, output_weight, preferred_element_type=jnp.float32).astype(jnp.bfloat16)
            grad_attended = jnp.dot(grad_rows, output_weight.T, preferred_element_type=jnp.float32).astype(jnp.bfloat16)
            grad_attended = lax.optimization_barrier(grad_attended)
            grad_f32 = grad_attended.astype(jnp.float32).reshape(TOK_DEV, HEADS, HEAD)
            row_delta = (grad_f32 * attended.astype(jnp.float32).reshape(TOK_DEV, HEADS, HEAD)).sum(-1)
            dprob = jnp.einsum('qhd,khd->hqk', grad_f32, value_f32)
            dscores = (probability * (dprob - row_delta.T[..., None]) * score_scale).astype(jnp.bfloat16)
            dscores_f32 = lax.optimization_barrier(dscores).astype(jnp.float32)
            query_grad = jnp.einsum('hqk,khd->qhd', dscores_f32, key_f32).reshape(TOK_DEV, HD).astype(jnp.bfloat16)
            key_piece = jnp.einsum('hqk,qhd->khd', dscores_f32, query_f32).astype(jnp.bfloat16)
            value_piece = jnp.einsum('hqk,qhd->khd', probability_low.astype(jnp.float32), grad_f32).astype(jnp.bfloat16)
            weight_piece = jnp.dot(attended.T, grad_rows, preferred_element_type=jnp.float32).astype(jnp.bfloat16)
            key_piece, value_piece, weight_piece = lax.optimization_barrier((key_piece, value_piece, weight_piece))
            updated = (key_sum + key_piece.astype(jnp.float32), value_sum + value_piece.astype(jnp.float32),
                       weight_sum + weight_piece.astype(jnp.float32))
            return updated, (projected, query_grad)

        start_sums = (jnp.zeros((LEN, HEADS, HEAD), jnp.float32), jnp.zeros((LEN, HEADS, HEAD), jnp.float32),
                      jnp.zeros((HD, D), jnp.float32))
        sums_out, rows_out = lax.scan(block_step, start_sums, jnp.arange(N_CP, dtype=jnp.int32))
        key_sum, value_sum, weight_sum = sums_out
        projected, query_grad = rows_out
        return (projected.reshape(LEN, D), query_grad.reshape(LEN, HD),
                key_sum.reshape(LEN, HD).astype(jnp.bfloat16), value_sum.reshape(LEN, HD).astype(jnp.bfloat16),
                weight_sum)

    projected, query_gradient, key_gradient, value_gradient, weight_sums = lax.map(
        one_sequence, (query_states, key_states, value_states, upstream))
    return projected, query_gradient, key_gradient, value_gradient, weight_sums.sum(0)
```

```python
import functools

import jax
import jax.numpy as jnp
from jax import lax
from jax.experimental import pallas as pl
from jax.experimental.pallas import tpu as pltpu
from jax.sharding import Mesh, PartitionSpec as P

HEADS = 8
HEAD = 128
SPAN = 64
UNITS = 16
ROWS = UNITS * SPAN
TILE = 256
LOW = -1e30
SCALE = 1.0 / HEAD
F32 = jnp.float32
BF16 = jnp.bfloat16
NT = (((1,), (1,)), ((), ()))
NN = (((1,), (0,)), ((), ()))
TN = (((0,), (0,)), ((), ()))


def dot(a, b, dims):
    return lax.dot_general(a, b, dims, preferred_element_type=F32)


def span_hot(first_span):
    span = lax.broadcasted_iota(jnp.int32, (TILE, HEAD), 0) // SPAN + first_span
    lane = lax.broadcasted_iota(jnp.int32, (TILE, HEAD), 1)
    return (span == lane).astype(F32).astype(BF16)


def query_wide(query, first_span):
    return jnp.concatenate([query * BF16(SCALE), span_hot(first_span)], axis=1)


def spread_bias(bias):
    return jnp.broadcast_to(bias[:, None, :], (UNITS, SPAN, HEAD)).reshape(ROWS, HEAD).astype(BF16)


def later_in_span():
    key = lax.broadcasted_iota(jnp.int32, (TILE, TILE), 0)
    query = lax.broadcasted_iota(jnp.int32, (TILE, TILE), 1)
    return (key // SPAN == query // SPAN) & (key > query)


def forward_body(first, *refs):
    if first:
        q_ref, kv0_ref, kv1_ref, bias_ref, o_ref, m_ref, l_ref, ka_ref, s_ref = refs
    else:
        (q_ref, kv0_ref, kv1_ref, bias_ref, o0_ref, m0_ref, l0_ref, att_ref, lse_ref, ka_ref, s_ref) = refs
    step = pl.program_id(0)

    @pl.when(step == 0)
    def _():
        for c, kv_ref in enumerate((kv0_ref, kv1_ref)):
            rows = pl.ds(c * ROWS, ROWS)
            ka_ref[rows, :HEAD] = kv_ref[:, :HEAD]
            ka_ref[rows, HEAD:] = spread_bias(bias_ref[c * UNITS : (c + 1) * UNITS, :])

    qa = query_wide(q_ref[...], step * (TILE // SPAN))
    for c in range(2):
        rows = pl.ds(c * ROWS, ROWS)
        s_ref[rows, :] = dot(ka_ref[rows, :], qa, NT)
    if first:
        rows = pl.ds(pl.multiple_of(step * TILE, TILE), TILE)
        s_ref[rows, :] = jnp.where(later_in_span(), LOW, s_ref[rows, :])
    top = jnp.max(s_ref[...], axis=0, keepdims=True)
    if not first:
        top = jnp.maximum(top, m0_ref[...])
    weights = jnp.exp(s_ref[...] - top)
    total = jnp.sum(weights, axis=0, keepdims=True)
    low = weights.astype(BF16)
    out = dot(kv0_ref[:, HEAD:], low[:ROWS], TN) + dot(kv1_ref[:, HEAD:], low[ROWS:], TN)
    if first:
        o_ref[...] = out
        m_ref[...] = top
        l_ref[...] = total
    else:
        fade = jnp.exp(m0_ref[...] - top)
        total = total + l0_ref[...] * fade
        out = (out + o0_ref[...] * fade) / total
        att_ref[...] = out.T.astype(BF16)
        lse_ref[...] = top + jnp.log(total)


def tile_spec(cols):
    return pl.BlockSpec((TILE, cols), lambda i: (i, 0))


def row_spec(rows):
    return pl.BlockSpec((rows, TILE), lambda i: (0, i))


def whole(rows, cols):
    return pl.BlockSpec((rows, cols), lambda i: (0, 0))


def cost(matmuls, pairs):
    return pl.CostEstimate(
        flops=matmuls * 2 * pairs * 2 * HEAD, bytes_accessed=4 << 20, transcendentals=pairs
    )


def forward(first, q, kv0, kv1, bias, *carry):
    stat = jax.ShapeDtypeStruct((1, ROWS), F32)
    if first:
        outs = [jax.ShapeDtypeStruct((HEAD, ROWS), F32), stat, stat]
        out_specs = [row_spec(HEAD), row_spec(1), row_spec(1)]
        carry_specs = []
    else:
        outs = [jax.ShapeDtypeStruct((ROWS, HEAD), BF16), stat]
        out_specs = [tile_spec(HEAD), row_spec(1)]
        carry_specs = [row_spec(HEAD), row_spec(1), row_spec(1)]
    return pl.pallas_call(
        functools.partial(forward_body, first),
        out_shape=outs,
        grid=(ROWS // TILE,),
        in_specs=[
            tile_spec(HEAD),
            whole(ROWS, 2 * HEAD),
            whole(ROWS, 2 * HEAD),
            whole(2 * UNITS, HEAD),
            *carry_specs,
        ],
        out_specs=out_specs,
        scratch_shapes=[
            pltpu.VMEM((2 * ROWS, 2 * HEAD), BF16),
            pltpu.VMEM((2 * ROWS, TILE), F32),
        ],
        cost_estimate=cost(2, 2 * ROWS * ROWS),
        compiler_params=pltpu.CompilerParams(vmem_limit_bytes=40 << 20),
        name="forward_a" if first else "forward_b",
    )(q, kv0, kv1, bias, *carry)


def delta_body(g_ref, att_ref, d_ref):
    product = g_ref[...].astype(F32) * att_ref[...].astype(F32)
    d_ref[...] = jnp.sum(product.T, axis=0, keepdims=True)


def row_delta(g, att):
    return pl.pallas_call(
        delta_body,
        out_shape=jax.ShapeDtypeStruct((1, ROWS), F32),
        in_specs=[pl.BlockSpec(memory_space=pltpu.VMEM)] * 2,
        out_specs=pl.BlockSpec(memory_space=pltpu.VMEM),
        name="delta",
    )(g, att)


def query_body(q_ref, g_ref, lse_ref, delta_ref, kv0, kv1, kv2, kv3, bias_ref, dq_ref, ka_ref, s_ref):
    step = pl.program_id(0)
    chunks = (kv0, kv1, kv2, kv3)

    @pl.when(step == 0)
    def _():
        for c, kv_ref in enumerate(chunks):
            rows = pl.ds(c * ROWS, ROWS)
            ka_ref[rows, :HEAD] = kv_ref[:, :HEAD]
            ka_ref[rows, HEAD:] = spread_bias(bias_ref[c * UNITS : (c + 1) * UNITS, :])

    qa = query_wide(q_ref[...], step * (TILE // SPAN))
    g = g_ref[...]
    lse = lse_ref[...]
    delta = delta_ref[...]
    total = jnp.zeros((HEAD, TILE), F32)
    for c, kv_ref in enumerate(chunks):
        s_ref[...] = dot(ka_ref[pl.ds(c * ROWS, ROWS), :], qa, NT)
        if c == 0:
            rows = pl.ds(pl.multiple_of(step * TILE, TILE), TILE)
            s_ref[rows, :] = jnp.where(later_in_span(), LOW, s_ref[rows, :])
        prob = jnp.exp(s_ref[...] - lse)
        dprob = dot(kv_ref[:, HEAD:], g, NT)
        ds = (prob * (dprob - delta)).astype(BF16)
        total += dot(kv_ref[:, :HEAD], ds, TN)
    dq_ref[...] = (total * SCALE).T.astype(BF16)


def query_grad(q, g, lse, delta, kvs, bias):
    return pl.pallas_call(
        query_body,
        out_shape=jax.ShapeDtypeStruct((ROWS, HEAD), BF16),
        grid=(ROWS // TILE,),
        in_specs=[
            tile_spec(HEAD),
            tile_spec(HEAD),
            row_spec(1),
            row_spec(1),
            *[whole(ROWS, 2 * HEAD)] * 4,
            whole(4 * UNITS, HEAD),
        ],
        out_specs=tile_spec(HEAD),
        scratch_shapes=[
            pltpu.VMEM((4 * ROWS, 2 * HEAD), BF16),
            pltpu.VMEM((ROWS, TILE), F32),
        ],
        cost_estimate=cost(3, 4 * ROWS * ROWS),
        compiler_params=pltpu.CompilerParams(vmem_limit_bytes=40 << 20),
        name="query_grad",
    )(q, g, lse, delta, *kvs, bias)


def key_body(*refs):
    kv_ref, bias_ref = refs[:2]
    qs, gs, stats = refs[2:6], refs[6:10], refs[10:14]
    dk_ref, dv_ref, ka_ref, s_ref, dk_acc, dv_acc = refs[14:]
    ka_ref[:, :HEAD] = kv_ref[:, :HEAD]
    ka_ref[:, HEAD:] = spread_bias(bias_ref[:UNITS, :])
    dk_acc[...] = jnp.zeros_like(dk_acc)
    dv_acc[...] = jnp.zeros_like(dv_acc)
    for c in range(4):

        def tile(i, _, c=c):
            rows = pl.ds(pl.multiple_of(i * TILE, TILE), TILE)
            q = qs[c][rows, :]
            g = gs[c][rows, :]
            lse = stats[c][0:1, rows]
            delta = stats[c][1:2, rows]
            qa = query_wide(q, i * (TILE // SPAN) + c * UNITS)
            s_ref[...] = dot(ka_ref[...], qa, NT)
            if c == 0:
                s_ref[rows, :] = jnp.where(later_in_span(), LOW, s_ref[rows, :])
            prob = jnp.exp(s_ref[...] - lse)
            dprob = dot(kv_ref[:, HEAD:], g, NT)
            ds = (prob * (dprob - delta)).astype(BF16)
            dv_acc[...] += dot(prob.astype(BF16), g, NN)
            dk_acc[...] += dot(ds, q, NN)
            return 0

        lax.fori_loop(0, ROWS // TILE, tile, 0)
    dk_ref[...] = (dk_acc[...] * SCALE).astype(BF16)
    dv_ref[...] = dv_acc[...].astype(BF16)


def key_grad(kv, bias, qs, gs, stats):
    in_vmem = pl.BlockSpec(memory_space=pltpu.VMEM)
    return pl.pallas_call(
        key_body,
        out_shape=[jax.ShapeDtypeStruct((ROWS, HEAD), BF16)] * 2,
        in_specs=[in_vmem] * 14,
        out_specs=[in_vmem] * 2,
        scratch_shapes=[
            pltpu.VMEM((ROWS, 2 * HEAD), BF16),
            pltpu.VMEM((ROWS, TILE), F32),
            pltpu.VMEM((ROWS, HEAD), F32),
            pltpu.VMEM((ROWS, HEAD), F32),
        ],
        cost_estimate=cost(4, 4 * ROWS * ROWS),
        compiler_params=pltpu.CompilerParams(vmem_limit_bytes=40 << 20),
        name="key_grad",
    )(kv, bias, *qs, *gs, *stats)


ZY = ("z", "y")
CHIPS = ("z", "y", "xl", "xh")
SWAP = [(0, 1), (1, 0)]


def other_core(x):
    return lax.ppermute(x, "core", SWAP)


def other_chip(x):
    return lax.ppermute(x, "xl", SWAP)


def everyone(x):
    far = other_chip(x)
    return x, other_core(x), far, other_core(far)


def exchange(x, axes):
    return lax.all_to_all(x, axes, 0, 0, tiled=True)


def in_order(first, own, peer):
    return jnp.stack([jnp.where(first, own, peer), jnp.where(first, peer, own)])


def span_bias(span_order, block_mask, xl, core):
    count = span_order.shape[0]
    row = jnp.arange(count, dtype=jnp.int32)
    owner, unit = row // UNITS, row % UNITS
    row_xl = xl ^ (owner // 2)
    half = core ^ (owner % 2) ^ ((unit // 4 + unit % 4) % 2)
    storage = 2 * (2 * unit + row_xl) + half
    held = (storage[:, None] == jnp.arange(count, dtype=jnp.int32)[None, :]).astype(jnp.int32)
    position = jnp.sum(held * span_order[None, :], axis=1)
    hot = (position[:, None] == jnp.arange(count, dtype=jnp.int32)[None, :]).astype(F32)
    pairs = jnp.dot(hot, jnp.dot(block_mask.astype(F32).T, hot.T))
    allowed = (pairs > 0.5) & (position[:, None] <= position[None, :])
    bias = jnp.where(allowed, 0.0, LOW).astype(F32)
    return jnp.pad(bias, ((0, 0), (0, HEAD - count)))


def by_unit(rows, kinds):
    split = rows.reshape(2, SPAN, kinds, HEADS, HEAD)
    return split.transpose(0, 3, 1, 2, 4).reshape(UNITS, SPAN, kinds * HEAD)


def by_row(blocks, kinds):
    split = blocks.reshape(2, HEADS, SPAN, kinds, HEAD)
    return split.transpose(0, 2, 3, 1, 4).reshape(2, SPAN, kinds * HEADS * HEAD)


def local(query_states, key_states, value_states, span_order, block_mask, output_weight, upstream):
    z, y, xl, core = (lax.axis_index(a) for a in ("z", "y", "xl", "core"))
    first_core = core == 0
    half = core ^ ((z + y) % 2)

    def share(rows):
        halves = rows.reshape(2, SPAN, -1)
        own = lax.dynamic_index_in_dim(halves, half, 0, False)
        peer = other_core(lax.dynamic_index_in_dim(halves, 1 - half, 0, False))
        return in_order(first_core, own, peer)

    def unshare(both):
        own = lax.dynamic_index_in_dim(both, core, 0, False)
        peer = other_core(lax.dynamic_index_in_dim(both, 1 - core, 0, False))
        return in_order(half == 0, own, peer).reshape(2 * SPAN, -1)

    states = share(jnp.concatenate([query_states[0], key_states[0], value_states[0]], axis=1))
    up = share(upstream[0]).reshape(2 * SPAN, -1)
    bias = span_bias(span_order, block_mask, xl, core)

    blocks = exchange(by_unit(states, 3), ZY).reshape(ROWS, 3 * HEAD)
    q = blocks[:, :HEAD]
    kvs = everyone(blocks[:, HEAD:])

    copies = jnp.broadcast_to(output_weight[None], (64, *output_weight.shape))
    weight_own = exchange(copies, CHIPS)
    weight_peer = other_core(weight_own)
    weight = in_order(first_core, weight_own, weight_peer).transpose(1, 0, 2, 3)
    weight = weight.reshape(HEADS * HEAD, -1)

    partial = forward(True, q, kvs[0], kvs[1], bias[: 2 * UNITS])
    attended, lse = forward(False, q, kvs[2], kvs[3], bias[2 * UNITS :], *partial)

    grad_rows = dot(up, weight, NT).astype(BF16).reshape(2, SPAN, -1)
    g = exchange(by_unit(grad_rows, 1), ZY).reshape(ROWS, HEAD)
    gs = everyone(g)
    qs = everyone(q)
    attended_rows = by_row(exchange(attended.reshape(UNITS, SPAN, HEAD), ZY), 1)
    attended_rows = attended_rows.reshape(2 * SPAN, -1)
    delta = row_delta(g, attended)
    stats = everyone(jnp.concatenate([lse, delta], axis=0))

    query_out = query_grad(q, g, lse, delta, kvs, bias)

    projected = dot(attended_rows, weight, NN).astype(BF16).reshape(2, SPAN, -1)
    projected = unshare(projected)
    term = dot(attended_rows, up, TN).astype(BF16).reshape(64, 2, 8, -1)
    term_own = lax.dynamic_index_in_dim(term, core, 1, False)
    term_peer = other_core(lax.dynamic_index_in_dim(term, 1 - core, 1, False))
    pair = (term_own.astype(F32) + term_peer.astype(F32)).astype(BF16)
    weight_gradient = jnp.sum(exchange(pair, CHIPS).astype(F32), axis=0)

    key_out, value_out = key_grad(kvs[0], bias, qs, gs, stats)
    grads = jnp.concatenate([query_out, key_out, value_out], axis=1).reshape(UNITS, SPAN, -1)
    grads = unshare(by_row(exchange(grads, ZY), 3))
    query_gradient, key_gradient, value_gradient = jnp.split(grads, 3, axis=1)
    return (
        projected[None],
        query_gradient[None],
        key_gradient[None],
        value_gradient[None],
        weight_gradient,
    )


def solution(mesh):
    axes = ("z", "y", "xl", "xh", "core")
    fine = Mesh(mesh.devices.reshape(4, 4, 2, 2, 2), axes)
    rows = P(("xh", "core"), ("z", "y", "xl"), None)
    return jax.shard_map(
        local,
        mesh=fine,
        in_specs=(rows, rows, rows, P(), P(), P(axes, None), rows),
        out_specs=(rows, rows, rows, rows, P(axes, None)),
        check_vma=False,
    )
```

```python
import functools

import jax
import jax.numpy as jnp
from jax import lax
from jax.experimental import pallas as pl
from jax.experimental.pallas import tpu as pltpu
from jax.sharding import Mesh, PartitionSpec as P

HEADS = 8
HEAD = 128
SPAN = 64
UNITS = 16
ROWS = UNITS * SPAN
TILE = 256
LOW = -1e30
SCALE = 1.0 / HEAD
F32 = jnp.float32
BF16 = jnp.bfloat16
NT = (((1,), (1,)), ((), ()))
NN = (((1,), (0,)), ((), ()))
TN = (((0,), (0,)), ((), ()))


def dot(a, b, dims):
    return lax.dot_general(a, b, dims, preferred_element_type=F32)


def span_hot(first_span):
    span = lax.broadcasted_iota(jnp.int32, (TILE, HEAD), 0) // SPAN + first_span
    lane = lax.broadcasted_iota(jnp.int32, (TILE, HEAD), 1)
    return (span == lane).astype(F32).astype(BF16)


def query_wide(query, first_span):
    return jnp.concatenate([query * BF16(SCALE), span_hot(first_span)], axis=1)


def spread_bias(bias):
    return jnp.broadcast_to(bias[:, None, :], (UNITS, SPAN, HEAD)).reshape(ROWS, HEAD).astype(BF16)


def later_in_span():
    key = lax.broadcasted_iota(jnp.int32, (TILE, TILE), 0)
    query = lax.broadcasted_iota(jnp.int32, (TILE, TILE), 1)
    return (key // SPAN == query // SPAN) & (key > query)


def forward_body(first, *refs):
    if first:
        q_ref, kv0_ref, kv1_ref, bias_ref, o_ref, m_ref, l_ref, ka_ref, s_ref = refs
    else:
        (q_ref, kv0_ref, kv1_ref, bias_ref, o0_ref, m0_ref, l0_ref, att_ref, lse_ref, ka_ref, s_ref) = refs
    step = pl.program_id(0)

    @pl.when(step == 0)
    def _():
        for c, kv_ref in enumerate((kv0_ref, kv1_ref)):
            rows = pl.ds(c * ROWS, ROWS)
            ka_ref[rows, :HEAD] = kv_ref[:, :HEAD]
            ka_ref[rows, HEAD:] = spread_bias(bias_ref[c * UNITS : (c + 1) * UNITS, :])

    qa = query_wide(q_ref[...], step * (TILE // SPAN))
    for c in range(2):
        rows = pl.ds(c * ROWS, ROWS)
        s_ref[rows, :] = dot(ka_ref[rows, :], qa, NT)
    if first:
        rows = pl.ds(pl.multiple_of(step * TILE, TILE), TILE)
        s_ref[rows, :] = jnp.where(later_in_span(), LOW, s_ref[rows, :])
    top = jnp.max(s_ref[...], axis=0, keepdims=True)
    if not first:
        top = jnp.maximum(top, m0_ref[...])
    weights = jnp.exp(s_ref[...] - top)
    total = jnp.sum(weights, axis=0, keepdims=True)
    low = weights.astype(BF16)
    out = dot(kv0_ref[:, HEAD:], low[:ROWS], TN) + dot(kv1_ref[:, HEAD:], low[ROWS:], TN)
    if first:
        o_ref[...] = out
        m_ref[...] = top
        l_ref[...] = total
    else:
        fade = jnp.exp(m0_ref[...] - top)
        total = total + l0_ref[...] * fade
        out = (out + o0_ref[...] * fade) / total
        att_ref[...] = out.T.astype(BF16)
        lse_ref[...] = top + jnp.log(total)


def tile_spec(cols):
    return pl.BlockSpec((TILE, cols), lambda i: (i, 0))


def row_spec(rows):
    return pl.BlockSpec((rows, TILE), lambda i: (0, i))


def whole(rows, cols):
    return pl.BlockSpec((rows, cols), lambda i: (0, 0))


def cost(matmuls, pairs):
    return pl.CostEstimate(
        flops=matmuls * 2 * pairs * 2 * HEAD, bytes_accessed=4 << 20, transcendentals=pairs
    )


def forward(first, q, kv0, kv1, bias, *carry):
    stat = jax.ShapeDtypeStruct((1, ROWS), F32)
    if first:
        outs = [jax.ShapeDtypeStruct((HEAD, ROWS), F32), stat, stat]
        out_specs = [row_spec(HEAD), row_spec(1), row_spec(1)]
        carry_specs = []
    else:
        outs = [jax.ShapeDtypeStruct((ROWS, HEAD), BF16), stat]
        out_specs = [tile_spec(HEAD), row_spec(1)]
        carry_specs = [row_spec(HEAD), row_spec(1), row_spec(1)]
    return pl.pallas_call(
        functools.partial(forward_body, first),
        out_shape=outs,
        grid=(ROWS // TILE,),
        in_specs=[
            tile_spec(HEAD),
            whole(ROWS, 2 * HEAD),
            whole(ROWS, 2 * HEAD),
            whole(2 * UNITS, HEAD),
            *carry_specs,
        ],
        out_specs=out_specs,
        scratch_shapes=[
            pltpu.VMEM((2 * ROWS, 2 * HEAD), BF16),
            pltpu.VMEM((2 * ROWS, TILE), F32),
        ],
        cost_estimate=cost(2, 2 * ROWS * ROWS),
        compiler_params=pltpu.CompilerParams(vmem_limit_bytes=40 << 20),
        name="forward_a" if first else "forward_b",
    )(q, kv0, kv1, bias, *carry)


def delta_body(g_ref, att_ref, d_ref):
    product = g_ref[...].astype(F32) * att_ref[...].astype(F32)
    d_ref[...] = jnp.sum(product.T, axis=0, keepdims=True)


def row_delta(g, att):
    return pl.pallas_call(
        delta_body,
        out_shape=jax.ShapeDtypeStruct((1, ROWS), F32),
        in_specs=[pl.BlockSpec(memory_space=pltpu.VMEM)] * 2,
        out_specs=pl.BlockSpec(memory_space=pltpu.VMEM),
        name="delta",
    )(g, att)


def query_body(q_ref, g_ref, lse_ref, delta_ref, kv0, kv1, kv2, kv3, bias_ref, dq_ref, ka_ref, s_ref):
    step = pl.program_id(0)
    chunks = (kv0, kv1, kv2, kv3)

    @pl.when(step == 0)
    def _():
        for c, kv_ref in enumerate(chunks):
            rows = pl.ds(c * ROWS, ROWS)
            ka_ref[rows, :HEAD] = kv_ref[:, :HEAD]
            ka_ref[rows, HEAD:] = spread_bias(bias_ref[c * UNITS : (c + 1) * UNITS, :])

    qa = query_wide(q_ref[...], step * (TILE // SPAN))
    g = g_ref[...]
    lse = lse_ref[...]
    delta = delta_ref[...]
    total = jnp.zeros((HEAD, TILE), F32)
    for c, kv_ref in enumerate(chunks):
        s_ref[...] = dot(ka_ref[pl.ds(c * ROWS, ROWS), :], qa, NT)
        if c == 0:
            rows = pl.ds(pl.multiple_of(step * TILE, TILE), TILE)
            s_ref[rows, :] = jnp.where(later_in_span(), LOW, s_ref[rows, :])
        prob = jnp.exp(s_ref[...] - lse)
        dprob = dot(kv_ref[:, HEAD:], g, NT)
        ds = (prob * (dprob - delta)).astype(BF16)
        total += dot(kv_ref[:, :HEAD], ds, TN)
    dq_ref[...] = (total * SCALE).T.astype(BF16)


def query_grad(q, g, lse, delta, kvs, bias):
    return pl.pallas_call(
        query_body,
        out_shape=jax.ShapeDtypeStruct((ROWS, HEAD), BF16),
        grid=(ROWS // TILE,),
        in_specs=[
            tile_spec(HEAD),
            tile_spec(HEAD),
            row_spec(1),
            row_spec(1),
            *[whole(ROWS, 2 * HEAD)] * 4,
            whole(4 * UNITS, HEAD),
        ],
        out_specs=tile_spec(HEAD),
        scratch_shapes=[
            pltpu.VMEM((4 * ROWS, 2 * HEAD), BF16),
            pltpu.VMEM((ROWS, TILE), F32),
        ],
        cost_estimate=cost(3, 4 * ROWS * ROWS),
        compiler_params=pltpu.CompilerParams(vmem_limit_bytes=40 << 20),
        name="query_grad",
    )(q, g, lse, delta, *kvs, bias)


def key_body(*refs):
    kv_ref, bias_ref = refs[:2]
    qs, gs, stats = refs[2:6], refs[6:10], refs[10:14]
    dk_ref, dv_ref, ka_ref, s_ref, dk_acc, dv_acc = refs[14:]
    ka_ref[:, :HEAD] = kv_ref[:, :HEAD]
    ka_ref[:, HEAD:] = spread_bias(bias_ref[:UNITS, :])
    dk_acc[...] = jnp.zeros_like(dk_acc)
    dv_acc[...] = jnp.zeros_like(dv_acc)
    for c in range(4):

        def tile(i, _, c=c):
            rows = pl.ds(pl.multiple_of(i * TILE, TILE), TILE)
            q = qs[c][rows, :]
            g = gs[c][rows, :]
            lse = stats[c][0:1, rows]
            delta = stats[c][1:2, rows]
            qa = query_wide(q, i * (TILE // SPAN) + c * UNITS)
            s_ref[...] = dot(ka_ref[...], qa, NT)
            if c == 0:
                s_ref[rows, :] = jnp.where(later_in_span(), LOW, s_ref[rows, :])
            prob = jnp.exp(s_ref[...] - lse)
            dprob = dot(kv_ref[:, HEAD:], g, NT)
            ds = (prob * (dprob - delta)).astype(BF16)
            dv_acc[...] += dot(prob.astype(BF16), g, NN)
            dk_acc[...] += dot(ds, q, NN)
            return 0

        lax.fori_loop(0, ROWS // TILE, tile, 0)
    dk_ref[...] = (dk_acc[...] * SCALE).astype(BF16)
    dv_ref[...] = dv_acc[...].astype(BF16)


def key_grad(kv, bias, qs, gs, stats):
    in_vmem = pl.BlockSpec(memory_space=pltpu.VMEM)
    return pl.pallas_call(
        key_body,
        out_shape=[jax.ShapeDtypeStruct((ROWS, HEAD), BF16)] * 2,
        in_specs=[in_vmem] * 14,
        out_specs=[in_vmem] * 2,
        scratch_shapes=[
            pltpu.VMEM((ROWS, 2 * HEAD), BF16),
            pltpu.VMEM((ROWS, TILE), F32),
            pltpu.VMEM((ROWS, HEAD), F32),
            pltpu.VMEM((ROWS, HEAD), F32),
        ],
        cost_estimate=cost(4, 4 * ROWS * ROWS),
        compiler_params=pltpu.CompilerParams(vmem_limit_bytes=40 << 20),
        name="key_grad",
    )(kv, bias, *qs, *gs, *stats)


ZY = ("z", "y")
CHIPS = ("z", "y", "xl", "xh")
SWAP = [(0, 1), (1, 0)]


def other_core(x):
    return lax.ppermute(x, "core", SWAP)


def other_chip(x):
    return lax.ppermute(x, "xl", SWAP)


def everyone(x):
    far = other_chip(x)
    return x, other_core(x), far, other_core(far)


def exchange(x, axes):
    return lax.all_to_all(x, axes, 0, 0, tiled=True)


def in_order(first, own, peer):
    return jnp.stack([jnp.where(first, own, peer), jnp.where(first, peer, own)])


def span_bias(span_order, block_mask, xl, core):
    count = span_order.shape[0]
    row = jnp.arange(count, dtype=jnp.int32)
    owner, unit = row // UNITS, row % UNITS
    row_xl = xl ^ (owner // 2)
    half = core ^ (owner % 2) ^ ((unit // 4 + unit % 4) % 2)
    storage = 2 * (2 * unit + row_xl) + half
    held = (storage[:, None] == jnp.arange(count, dtype=jnp.int32)[None, :]).astype(jnp.int32)
    position = jnp.sum(held * span_order[None, :], axis=1)
    hot = (position[:, None] == jnp.arange(count, dtype=jnp.int32)[None, :]).astype(F32)
    pairs = jnp.dot(hot, jnp.dot(block_mask.astype(F32).T, hot.T))
    allowed = (pairs > 0.5) & (position[:, None] <= position[None, :])
    bias = jnp.where(allowed, 0.0, LOW).astype(F32)
    return jnp.pad(bias, ((0, 0), (0, HEAD - count)))


def by_unit(rows, kinds):
    split = rows.reshape(2, SPAN, kinds, HEADS, HEAD)
    return split.transpose(0, 3, 1, 2, 4).reshape(UNITS, SPAN, kinds * HEAD)


def by_row(blocks, kinds):
    split = blocks.reshape(2, HEADS, SPAN, kinds, HEAD)
    return split.transpose(0, 2, 3, 1, 4).reshape(2, SPAN, kinds * HEADS * HEAD)


def side_by_side(first, own, peer):
    return jnp.concatenate([jnp.where(first, own, peer), jnp.where(first, peer, own)], axis=-1)


def from_chips(x):
    place = 2 * lax.axis_index("xl") + lax.axis_index("xh")
    held = [x] + [
        lax.ppermute(x, ("xl", "xh"), [(k, k ^ step) for k in range(4)]) for step in (1, 2, 3)
    ]
    low, high = place % 2 == 1, place >= 2
    pairs = [
        (jnp.where(low, held[k + 1], held[k]), jnp.where(low, held[k], held[k + 1])) for k in (0, 2)
    ]
    front = [jnp.where(high, pairs[1][k], pairs[0][k]) for k in (0, 1)]
    back = [jnp.where(high, pairs[0][k], pairs[1][k]) for k in (0, 1)]
    return jnp.stack(front + back, axis=1)


def sum_to_chips(x):
    place = 2 * lax.axis_index("xl") + lax.axis_index("xh")
    total = lax.dynamic_index_in_dim(x, place, 1, False).astype(F32)
    for step in (1, 2, 3):
        part = lax.dynamic_index_in_dim(x, place ^ step, 1, False)
        sent = lax.ppermute(part, ("xl", "xh"), [(k, k ^ step) for k in range(4)])
        total = total + sent.astype(F32)
    return total.astype(x.dtype)


def local(query_states, key_states, value_states, span_order, block_mask, output_weight, upstream):
    z, y, xl, core = (lax.axis_index(a) for a in ("z", "y", "xl", "core"))
    first_core = core == 0
    half = core ^ ((z + y) % 2)
    cols = output_weight.shape[1] // 2

    def mine(x, axis):
        return lax.dynamic_index_in_dim(x, core, axis, False)

    def theirs(x, axis):
        return lax.dynamic_index_in_dim(x, 1 - core, axis, False)

    def share(rows):
        halves = rows.reshape(2, SPAN, -1)
        own = lax.dynamic_index_in_dim(halves, half, 0, False)
        peer = other_core(lax.dynamic_index_in_dim(halves, 1 - half, 0, False))
        return in_order(first_core, own, peer)

    def unshare(both):
        own = mine(both, 0)
        peer = other_core(theirs(both, 0))
        return in_order(half == 0, own, peer).reshape(2 * SPAN, -1)

    weight_cols = output_weight.reshape(-1, 2, cols)
    weight_rows = in_order(first_core, mine(weight_cols, 1), other_core(theirs(weight_cols, 1)))
    weight_rows = weight_rows.reshape(-1, cols)
    copies = jnp.broadcast_to(weight_rows[None], (UNITS, *weight_rows.shape))
    states = share(jnp.concatenate([query_states[0], key_states[0], value_states[0]], axis=1))
    weight_rows = exchange(copies, ZY)
    sent, weight_rows = lax.optimization_barrier((by_unit(states, 3), weight_rows))
    weight = from_chips(weight_rows)
    blocks = exchange(sent, ZY).reshape(ROWS, 3 * HEAD)
    bias = span_bias(span_order, block_mask, xl, core)

    up_cols = upstream[0].reshape(2 * SPAN, 2, cols)
    up = in_order(first_core, mine(up_cols, 1), other_core(theirs(up_cols, 1)))
    up = up.reshape(2, 2, SPAN, cols)
    up = in_order(half == 0, up[:, 0], up[:, 1]).reshape(4 * SPAN, cols)

    q = blocks[:, :HEAD]
    kvs = everyone(blocks[:, HEAD:])
    partial = forward(True, q, kvs[0], kvs[1], bias[: 2 * UNITS])

    weight = weight.reshape(HEADS * HEAD, cols)
    grad_rows = dot(up, weight, NT)
    grad_rows = grad_rows[: 2 * SPAN] + other_core(grad_rows[2 * SPAN :])
    grad_rows = grad_rows.astype(BF16).reshape(2, SPAN, -1)
    g = exchange(by_unit(grad_rows, 1), ZY).reshape(ROWS, HEAD)
    gs = everyone(g)
    qs = everyone(q)

    attended, lse = forward(False, q, kvs[2], kvs[3], bias[2 * UNITS :], *partial)
    attended, g = lax.optimization_barrier((attended, g))
    delta = row_delta(g, attended)
    stats = everyone(jnp.concatenate([lse, delta], axis=0))
    query_out = query_grad(q, g, lse, delta, kvs, bias)

    attended_rows = by_row(exchange(attended.reshape(UNITS, SPAN, HEAD), ZY), 1)
    attended_rows = jnp.stack([attended_rows, other_core(attended_rows)]).reshape(4 * SPAN, -1)
    term = dot(attended_rows, up, TN).astype(BF16).reshape(UNITS, 4, 16, cols)
    term, key_side = lax.optimization_barrier((term, kvs[0]))
    term = sum_to_chips(term)
    projected = dot(attended_rows, weight, NN).astype(BF16).reshape(2, 2, SPAN, cols)
    own, peer = mine(projected, 1), other_core(theirs(projected, 1))
    own = in_order(half == 0, own[0], own[1]).reshape(2 * SPAN, cols)
    peer = in_order(half == 0, peer[1], peer[0]).reshape(2 * SPAN, cols)
    projected = side_by_side(first_core, own, peer)

    key_out, value_out = key_grad(key_side, bias, qs, gs, stats)
    grads = jnp.concatenate([query_out, key_out, value_out], axis=1).reshape(UNITS, SPAN, -1)
    grads, term = lax.optimization_barrier((exchange(grads, ZY), term))
    summed = jnp.sum(exchange(term, ZY).astype(F32), axis=0).reshape(2, -1, cols)
    weight_gradient = side_by_side(first_core, mine(summed, 0), other_core(theirs(summed, 0)))
    grads = unshare(by_row(grads, 3))
    query_gradient, key_gradient, value_gradient = jnp.split(grads, 3, axis=1)
    return (
        projected[None],
        query_gradient[None],
        key_gradient[None],
        value_gradient[None],
        weight_gradient,
    )


def solution(mesh):
    axes = ("z", "y", "xl", "xh", "core")
    fine = Mesh(mesh.devices.reshape(4, 4, 2, 2, 2), axes)
    rows = P(("xh", "core"), ("z", "y", "xl"), None)
    return jax.shard_map(
        local,
        mesh=fine,
        in_specs=(rows, rows, rows, P(), P(), P(axes, None), rows),
        out_specs=(rows, rows, rows, rows, P(axes, None)),
        check_vma=False,
    )
```

```python
import functools

import jax
import jax.numpy as jnp
from jax import lax
from jax.experimental import pallas as pl
from jax.experimental.pallas import tpu as pltpu
from jax.sharding import Mesh, PartitionSpec as P

HEADS = 8
HEAD = 128
SPAN = 64
UNITS = 16
ROWS = UNITS * SPAN
TILE = 256
LOW = -1e30
SCALE = 1.0 / HEAD
F32 = jnp.float32
BF16 = jnp.bfloat16
NT = (((1,), (1,)), ((), ()))
NN = (((1,), (0,)), ((), ()))
TN = (((0,), (0,)), ((), ()))


def dot(a, b, dims):
    return lax.dot_general(a, b, dims, preferred_element_type=F32)


def span_hot(first_span):
    span = lax.broadcasted_iota(jnp.int32, (TILE, HEAD), 0) // SPAN + first_span
    lane = lax.broadcasted_iota(jnp.int32, (TILE, HEAD), 1)
    return (span == lane).astype(F32).astype(BF16)


def query_wide(query, first_span):
    return jnp.concatenate([query * BF16(SCALE), span_hot(first_span)], axis=1)


def spread_bias(bias):
    return jnp.broadcast_to(bias[:, None, :], (UNITS, SPAN, HEAD)).reshape(ROWS, HEAD).astype(BF16)


def later_in_span():
    key = lax.broadcasted_iota(jnp.int32, (TILE, TILE), 0)
    query = lax.broadcasted_iota(jnp.int32, (TILE, TILE), 1)
    return (key // SPAN == query // SPAN) & (key > query)


def forward_body(first, *refs):
    if first:
        q_ref, kv0_ref, kv1_ref, bias_ref, o_ref, m_ref, l_ref, ka_ref, s_ref = refs
    else:
        (q_ref, kv0_ref, kv1_ref, bias_ref, o0_ref, m0_ref, l0_ref, att_ref, lse_ref, ka_ref, s_ref) = refs
    step = pl.program_id(0)

    @pl.when(step == 0)
    def _():
        for c, kv_ref in enumerate((kv0_ref, kv1_ref)):
            rows = pl.ds(c * ROWS, ROWS)
            ka_ref[rows, :HEAD] = kv_ref[:, :HEAD]
            ka_ref[rows, HEAD:] = spread_bias(bias_ref[c * UNITS : (c + 1) * UNITS, :])

    qa = query_wide(q_ref[...], step * (TILE // SPAN))
    for c in range(2):
        rows = pl.ds(c * ROWS, ROWS)
        s_ref[rows, :] = dot(ka_ref[rows, :], qa, NT)
    if first:
        rows = pl.ds(pl.multiple_of(step * TILE, TILE), TILE)
        s_ref[rows, :] = jnp.where(later_in_span(), LOW, s_ref[rows, :])
    top = jnp.max(s_ref[...], axis=0, keepdims=True)
    if not first:
        top = jnp.maximum(top, m0_ref[...])
    weights = jnp.exp(s_ref[...] - top)
    total = jnp.sum(weights, axis=0, keepdims=True)
    low = weights.astype(BF16)
    out = dot(kv0_ref[:, HEAD:], low[:ROWS], TN) + dot(kv1_ref[:, HEAD:], low[ROWS:], TN)
    if first:
        o_ref[...] = out
        m_ref[...] = top
        l_ref[...] = total
    else:
        fade = jnp.exp(m0_ref[...] - top)
        total = total + l0_ref[...] * fade
        out = (out + o0_ref[...] * fade) / total
        att_ref[...] = out.T.astype(BF16)
        lse_ref[...] = top + jnp.log(total)


def tile_spec(cols):
    return pl.BlockSpec((TILE, cols), lambda i: (i, 0))


def row_spec(rows):
    return pl.BlockSpec((rows, TILE), lambda i: (0, i))


def whole(rows, cols):
    return pl.BlockSpec((rows, cols), lambda i: (0, 0))


def cost(matmuls, pairs):
    return pl.CostEstimate(
        flops=matmuls * 2 * pairs * 2 * HEAD, bytes_accessed=4 << 20, transcendentals=pairs
    )


def forward(first, q, kv0, kv1, bias, *carry):
    stat = jax.ShapeDtypeStruct((1, ROWS), F32)
    if first:
        outs = [jax.ShapeDtypeStruct((HEAD, ROWS), F32), stat, stat]
        out_specs = [row_spec(HEAD), row_spec(1), row_spec(1)]
        carry_specs = []
    else:
        outs = [jax.ShapeDtypeStruct((ROWS, HEAD), BF16), stat]
        out_specs = [tile_spec(HEAD), row_spec(1)]
        carry_specs = [row_spec(HEAD), row_spec(1), row_spec(1)]
    return pl.pallas_call(
        functools.partial(forward_body, first),
        out_shape=outs,
        grid=(ROWS // TILE,),
        in_specs=[
            tile_spec(HEAD),
            whole(ROWS, 2 * HEAD),
            whole(ROWS, 2 * HEAD),
            whole(2 * UNITS, HEAD),
            *carry_specs,
        ],
        out_specs=out_specs,
        scratch_shapes=[
            pltpu.VMEM((2 * ROWS, 2 * HEAD), BF16),
            pltpu.VMEM((2 * ROWS, TILE), F32),
        ],
        cost_estimate=cost(2, 2 * ROWS * ROWS),
        compiler_params=pltpu.CompilerParams(vmem_limit_bytes=40 << 20),
        name="forward_a" if first else "forward_b",
    )(q, kv0, kv1, bias, *carry)


def delta_body(g_ref, att_ref, d_ref):
    product = g_ref[...].astype(F32) * att_ref[...].astype(F32)
    d_ref[...] = jnp.sum(product.T, axis=0, keepdims=True)


def row_delta(g, att):
    return pl.pallas_call(
        delta_body,
        out_shape=jax.ShapeDtypeStruct((1, ROWS), F32),
        in_specs=[pl.BlockSpec(memory_space=pltpu.VMEM)] * 2,
        out_specs=pl.BlockSpec(memory_space=pltpu.VMEM),
        name="delta",
    )(g, att)


def query_body(q_ref, g_ref, lse_ref, delta_ref, kv0, kv1, kv2, kv3, bias_ref, dq_ref, ka_ref, s_ref):
    step = pl.program_id(0)
    chunks = (kv0, kv1, kv2, kv3)

    @pl.when(step == 0)
    def _():
        for c, kv_ref in enumerate(chunks):
            rows = pl.ds(c * ROWS, ROWS)
            ka_ref[rows, :HEAD] = kv_ref[:, :HEAD]
            ka_ref[rows, HEAD:] = spread_bias(bias_ref[c * UNITS : (c + 1) * UNITS, :])

    qa = query_wide(q_ref[...], step * (TILE // SPAN))
    g = g_ref[...]
    lse = lse_ref[...]
    delta = delta_ref[...]
    total = jnp.zeros((HEAD, TILE), F32)
    for c, kv_ref in enumerate(chunks):
        s_ref[...] = dot(ka_ref[pl.ds(c * ROWS, ROWS), :], qa, NT)
        if c == 0:
            rows = pl.ds(pl.multiple_of(step * TILE, TILE), TILE)
            s_ref[rows, :] = jnp.where(later_in_span(), LOW, s_ref[rows, :])
        prob = jnp.exp(s_ref[...] - lse)
        dprob = dot(kv_ref[:, HEAD:], g, NT)
        ds = (prob * (dprob - delta)).astype(BF16)
        total += dot(kv_ref[:, :HEAD], ds, TN)
    dq_ref[...] = (total * SCALE).T.astype(BF16)


def query_grad(q, g, lse, delta, kvs, bias):
    return pl.pallas_call(
        query_body,
        out_shape=jax.ShapeDtypeStruct((ROWS, HEAD), BF16),
        grid=(ROWS // TILE,),
        in_specs=[
            tile_spec(HEAD),
            tile_spec(HEAD),
            row_spec(1),
            row_spec(1),
            *[whole(ROWS, 2 * HEAD)] * 4,
            whole(4 * UNITS, HEAD),
        ],
        out_specs=tile_spec(HEAD),
        scratch_shapes=[
            pltpu.VMEM((4 * ROWS, 2 * HEAD), BF16),
            pltpu.VMEM((ROWS, TILE), F32),
        ],
        cost_estimate=cost(3, 4 * ROWS * ROWS),
        compiler_params=pltpu.CompilerParams(vmem_limit_bytes=40 << 20),
        name="query_grad",
    )(q, g, lse, delta, *kvs, bias)


def key_body(*refs):
    kv_ref, bias_ref = refs[:2]
    pairs, stats = refs[2:6], refs[6]
    dk_ref, dv_ref, ka_ref, s_ref, dk_acc, dv_acc = refs[7:]
    ka_ref[:, :HEAD] = kv_ref[:, :HEAD]
    ka_ref[:, HEAD:] = spread_bias(bias_ref[:UNITS, :])
    dk_acc[...] = jnp.zeros_like(dk_acc)
    dv_acc[...] = jnp.zeros_like(dv_acc)
    for c in range(4):

        def tile(i, _, c=c):
            rows = pl.ds(pl.multiple_of(i * TILE, TILE), TILE)
            q = pairs[c][rows, :HEAD]
            g = pairs[c][rows, HEAD:]
            lse = stats[2 * c : 2 * c + 1, rows]
            delta = stats[2 * c + 1 : 2 * c + 2, rows]
            qa = query_wide(q, i * (TILE // SPAN) + c * UNITS)
            s_ref[...] = dot(ka_ref[...], qa, NT)
            if c == 0:
                s_ref[rows, :] = jnp.where(later_in_span(), LOW, s_ref[rows, :])
            prob = jnp.exp(s_ref[...] - lse)
            dprob = dot(kv_ref[:, HEAD:], g, NT)
            ds = (prob * (dprob - delta)).astype(BF16)
            dv_acc[...] += dot(prob.astype(BF16), g, NN)
            dk_acc[...] += dot(ds, q, NN)
            return 0

        lax.fori_loop(0, ROWS // TILE, tile, 0)
    dk_ref[...] = (dk_acc[...] * SCALE).astype(BF16)
    dv_ref[...] = dv_acc[...].astype(BF16)


def key_grad(kv, bias, pairs, stats):
    in_vmem = pl.BlockSpec(memory_space=pltpu.VMEM)
    return pl.pallas_call(
        key_body,
        out_shape=[jax.ShapeDtypeStruct((ROWS, HEAD), BF16)] * 2,
        in_specs=[in_vmem] * 7,
        out_specs=[in_vmem] * 2,
        scratch_shapes=[
            pltpu.VMEM((ROWS, 2 * HEAD), BF16),
            pltpu.VMEM((ROWS, TILE), F32),
            pltpu.VMEM((ROWS, HEAD), F32),
            pltpu.VMEM((ROWS, HEAD), F32),
        ],
        cost_estimate=cost(4, 4 * ROWS * ROWS),
        compiler_params=pltpu.CompilerParams(vmem_limit_bytes=40 << 20),
        name="key_grad",
    )(kv, bias, *pairs, stats)


ZY = ("z", "y")
CHIPS = ("z", "y", "xl", "xh")
SWAP = [(0, 1), (1, 0)]


def other_core(x):
    return lax.ppermute(x, "core", SWAP)


def other_chip(x):
    return lax.ppermute(x, "xl", SWAP)


def everyone(x):
    far = other_chip(x)
    return x, other_core(x), far, other_core(far)


def exchange(x, axes):
    return lax.all_to_all(x, axes, 0, 0, tiled=True)


def in_order(first, own, peer):
    return jnp.stack([jnp.where(first, own, peer), jnp.where(first, peer, own)])


def span_bias(span_order, block_mask, xl, core):
    count = span_order.shape[0]
    row = jnp.arange(count, dtype=jnp.int32)
    owner, unit = row // UNITS, row % UNITS
    row_xl = xl ^ (owner // 2)
    half = core ^ (owner % 2) ^ ((unit // 4 + unit % 4) % 2)
    storage = 2 * (2 * unit + row_xl) + half
    held = (storage[:, None] == jnp.arange(count, dtype=jnp.int32)[None, :]).astype(jnp.int32)
    position = jnp.sum(held * span_order[None, :], axis=1)
    hot = (position[:, None] == jnp.arange(count, dtype=jnp.int32)[None, :]).astype(F32)
    pairs = jnp.dot(hot, jnp.dot(block_mask.astype(F32).T, hot.T))
    allowed = (pairs > 0.5) & (position[:, None] <= position[None, :])
    bias = jnp.where(allowed, 0.0, LOW).astype(F32)
    return jnp.pad(bias, ((0, 0), (0, HEAD - count)))


def by_unit(rows, kinds):
    split = rows.reshape(2, SPAN, kinds, HEADS, HEAD)
    return split.transpose(0, 3, 1, 2, 4).reshape(UNITS, SPAN, kinds * HEAD)


def by_row(blocks, kinds):
    split = blocks.reshape(2, HEADS, SPAN, kinds, HEAD)
    return split.transpose(0, 2, 3, 1, 4).reshape(2, SPAN, kinds * HEADS * HEAD)


def side_by_side(first, own, peer):
    return jnp.concatenate([jnp.where(first, own, peer), jnp.where(first, peer, own)], axis=-1)


def to_narrow(x):
    return jnp.concatenate(jnp.split(x, 4, axis=-1), axis=-2)


def from_narrow(x):
    return jnp.concatenate(jnp.split(x, 4, axis=-2), axis=-1)


def chip_place():
    return 2 * lax.axis_index("xl") + lax.axis_index("xh")


def chip_copies(parts):
    return [
        lax.ppermute(part, ("xl", "xh"), [(k, k ^ step) for k in range(4)])
        for step, part in zip((1, 2, 3), parts)
    ]


def weight_body(place_ref, *refs):
    parts, out_ref = refs[:4], refs[4]
    for step in range(4):
        chip = place_ref[0] ^ step
        for c in range(4):
            rows = parts[step][:, c * 16 : (c + 1) * 16, :]
            out_ref[:, chip, :, c * 256 : (c + 1) * 256] = rows


def weight_whole(place, parts):
    in_vmem = pl.BlockSpec(memory_space=pltpu.VMEM)
    return pl.pallas_call(
        weight_body,
        out_shape=jax.ShapeDtypeStruct((UNITS, 4, 16, 1024), BF16),
        in_specs=[pl.BlockSpec(memory_space=pltpu.SMEM)] + [in_vmem] * 4,
        out_specs=in_vmem,
        cost_estimate=pl.CostEstimate(flops=0, bytes_accessed=4 << 20, transcendentals=0),
        compiler_params=pltpu.CompilerParams(vmem_limit_bytes=24 << 20),
        name="weight_whole",
    )(place, *parts)


def term_body(place_ref, att_ref, up_ref, *refs):
    outs, sum_ref = refs[:4], refs[4]
    for c in range(4):
        cols = slice(c * 256, (c + 1) * 256)
        sum_ref[...] = dot(att_ref[...], up_ref[:, cols], TN).astype(BF16).reshape(sum_ref.shape)
        for step in range(4):
            outs[step][:, c * 16 : (c + 1) * 16, :] = sum_ref[:, place_ref[0] ^ step]


def weight_terms(place, att, up):
    in_vmem = pl.BlockSpec(memory_space=pltpu.VMEM)
    return pl.pallas_call(
        term_body,
        out_shape=[jax.ShapeDtypeStruct((UNITS, SPAN, 256), BF16)] * 4,
        in_specs=[pl.BlockSpec(memory_space=pltpu.SMEM)] + [in_vmem] * 2,
        out_specs=[in_vmem] * 4,
        scratch_shapes=[pltpu.VMEM((UNITS, 4, 16, 256), BF16)],
        cost_estimate=pl.CostEstimate(
            flops=2 * 256 * 1024 * 1024, bytes_accessed=4 << 20, transcendentals=0
        ),
        compiler_params=pltpu.CompilerParams(vmem_limit_bytes=24 << 20),
        name="weight_terms",
    )(place, att, up)


def local(query_states, key_states, value_states, span_order, block_mask, output_weight, upstream):
    z, y, xl, core = (lax.axis_index(a) for a in ("z", "y", "xl", "core"))
    first_core = core == 0
    half = core ^ ((z + y) % 2)
    cols = output_weight.shape[1] // 2

    def mine(x, axis):
        return lax.dynamic_index_in_dim(x, core, axis, False)

    def theirs(x, axis):
        return lax.dynamic_index_in_dim(x, 1 - core, axis, False)

    def share(rows):
        halves = rows.reshape(2, SPAN, -1)
        own = lax.dynamic_index_in_dim(halves, half, 0, False)
        peer = other_core(lax.dynamic_index_in_dim(halves, 1 - half, 0, False))
        return in_order(first_core, own, peer)

    def unshare(both):
        own = mine(both, 0)
        peer = other_core(theirs(both, 0))
        return in_order(half == 0, own, peer).reshape(2 * SPAN, -1)

    weight_cols = output_weight.reshape(-1, 2, cols)
    weight_rows = in_order(first_core, mine(weight_cols, 1), other_core(theirs(weight_cols, 1)))
    weight_rows = to_narrow(weight_rows.reshape(-1, cols))
    copies = jnp.broadcast_to(weight_rows[None], (UNITS, *weight_rows.shape))
    states = share(jnp.concatenate([query_states[0], key_states[0], value_states[0]], axis=1))
    blocks = exchange(jnp.concatenate([by_unit(states, 3), copies], axis=2), ZY)
    q = blocks[:, :, :HEAD].reshape(ROWS, HEAD)
    own_kv = blocks[:, :, HEAD : 3 * HEAD].reshape(ROWS, 2 * HEAD)
    far_kv = other_chip(own_kv)
    near_kv = other_core(own_kv)
    weight_own = blocks[:, :, 3 * HEAD :]
    weight_others = chip_copies([weight_own] * 3)
    place = chip_place().reshape(1)
    bias = span_bias(span_order, block_mask, xl, core)

    up_cols = upstream[0].reshape(2 * SPAN, 2, cols)
    up = in_order(first_core, mine(up_cols, 1), other_core(theirs(up_cols, 1)))
    up = up.reshape(2, 2, SPAN, cols)
    up = in_order(half == 0, up[:, 0], up[:, 1]).reshape(4 * SPAN, cols)

    partial = forward(True, q, own_kv, near_kv, bias[: 2 * UNITS])
    far_kv, *partial = lax.optimization_barrier((far_kv, *partial))
    kvs = (own_kv, near_kv, far_kv, other_core(far_kv))

    attended, lse = forward(False, q, kvs[2], kvs[3], bias[2 * UNITS :], *partial)
    attended_units = exchange(attended.reshape(UNITS, SPAN, HEAD), ZY)
    attended_units, *weight_others = lax.optimization_barrier((attended_units, *weight_others))
    weight = weight_whole(place, [weight_own, *weight_others]).reshape(HEADS * HEAD, cols)
    grad_rows = dot(up, weight, NT)
    grad_rows = grad_rows[: 2 * SPAN] + other_core(grad_rows[2 * SPAN :])
    grad_rows = grad_rows.astype(BF16).reshape(2, SPAN, -1)
    g = exchange(by_unit(grad_rows, 1), ZY).reshape(ROWS, HEAD)

    attended_rows = by_row(attended_units, 1)
    attended_rows = jnp.stack([attended_rows, other_core(attended_rows)]).reshape(4 * SPAN, -1)
    terms = weight_terms(place, attended_rows, up)
    *terms, g = lax.optimization_barrier((*terms, g))
    pairs = everyone(jnp.concatenate([q, g], axis=1))
    others = chip_copies(terms[1:])
    projected = dot(attended_rows, weight, NN).astype(BF16).reshape(2, 2, SPAN, cols)
    own, peer = mine(projected, 1), other_core(theirs(projected, 1))
    own = in_order(half == 0, own[0], own[1]).reshape(2 * SPAN, cols)
    peer = in_order(half == 0, peer[1], peer[0]).reshape(2 * SPAN, cols)
    projected = side_by_side(first_core, own, peer)

    delta = row_delta(g, attended)
    stats = jnp.concatenate([lse, delta], axis=0)
    stats = jnp.concatenate([stats, other_core(stats)], axis=0)
    stats = jnp.concatenate([stats, other_chip(stats)], axis=0)
    query_out = query_grad(q, g, lse, delta, kvs, bias)
    key_out, value_out = key_grad(own_kv, bias, pairs, stats)
    key_out, *others = lax.optimization_barrier((key_out, *others))
    term = sum((x.astype(F32) for x in others), terms[0].astype(F32)).astype(BF16)
    grads = [x.reshape(UNITS, SPAN, HEAD) for x in (query_out, key_out, value_out)]
    grads = exchange(jnp.concatenate([*grads, term], axis=2), ZY)
    summed = jnp.sum(grads[:, :, 3 * HEAD :].astype(F32), axis=0)
    summed = from_narrow(summed).reshape(2, -1, cols)
    grads = grads[:, :, : 3 * HEAD]
    weight_gradient = side_by_side(first_core, mine(summed, 0), other_core(theirs(summed, 0)))
    grads = unshare(by_row(grads, 3))
    query_gradient, key_gradient, value_gradient = jnp.split(grads, 3, axis=1)
    return (
        projected[None],
        query_gradient[None],
        key_gradient[None],
        value_gradient[None],
        weight_gradient,
    )


def solution(mesh):
    axes = ("z", "y", "xl", "xh", "core")
    fine = Mesh(mesh.devices.reshape(4, 4, 2, 2, 2), axes)
    rows = P(("xh", "core"), ("z", "y", "xl"), None)
    return jax.shard_map(
        local,
        mesh=fine,
        in_specs=(rows, rows, rows, P(), P(), P(axes, None), rows),
        out_specs=(rows, rows, rows, rows, P(axes, None)),
        check_vma=False,
    )
```

```python
import functools

import jax
import jax.numpy as jnp
from jax import lax
from jax.experimental import pallas as pl
from jax.experimental.pallas import tpu as pltpu
from jax.sharding import Mesh, PartitionSpec as P

HEADS = 8
HEAD = 128
SPAN = 64
UNITS = 16
ROWS = UNITS * SPAN
TILE = 256
LOW = -1e30
SCALE = 1.0 / HEAD
F32 = jnp.float32
BF16 = jnp.bfloat16
NT = (((1,), (1,)), ((), ()))
NN = (((1,), (0,)), ((), ()))
TN = (((0,), (0,)), ((), ()))


def dot(a, b, dims):
    return lax.dot_general(a, b, dims, preferred_element_type=F32)


def span_hot(first_span):
    span = lax.broadcasted_iota(jnp.int32, (TILE, HEAD), 0) // SPAN + first_span
    lane = lax.broadcasted_iota(jnp.int32, (TILE, HEAD), 1)
    return (span == lane).astype(F32).astype(BF16)


def query_wide(query, first_span):
    return jnp.concatenate([query * BF16(SCALE), span_hot(first_span)], axis=1)


def spread_bias(bias):
    return jnp.broadcast_to(bias[:, None, :], (UNITS, SPAN, HEAD)).reshape(ROWS, HEAD).astype(BF16)


def fill_keys(chunks, bias_ref, ka_ref):
    for c, kv_ref in enumerate(chunks):
        rows = pl.ds(c * ROWS, ROWS)
        ka_ref[rows, :HEAD] = kv_ref[:, :HEAD]
        ka_ref[rows, HEAD:] = spread_bias(bias_ref[c * UNITS : (c + 1) * UNITS, :])


def later_in_span():
    key = lax.broadcasted_iota(jnp.int32, (TILE, TILE), 0)
    query = lax.broadcasted_iota(jnp.int32, (TILE, TILE), 1)
    return (key // SPAN == query // SPAN) & (key > query)


def forward_body(q_ref, kv0, kv1, kv2, kv3, bias_ref, att_ref, lse_ref, ka_ref, s_ref):
    step = pl.program_id(0)
    chunks = (kv0, kv1, kv2, kv3)

    @pl.when(step == 0)
    def _():
        fill_keys(chunks, bias_ref, ka_ref)

    qa = query_wide(q_ref[...], step * (TILE // SPAN))
    top = None
    for c in range(4):
        rows = pl.ds(c * ROWS, ROWS)
        s_ref[rows, :] = dot(ka_ref[rows, :], qa, NT)
        if c == 0:
            own = pl.ds(pl.multiple_of(step * TILE, TILE), TILE)
            s_ref[own, :] = jnp.where(later_in_span(), LOW, s_ref[own, :])
        chunk_top = jnp.max(s_ref[rows, :], axis=0, keepdims=True)
        top = chunk_top if c == 0 else jnp.maximum(top, chunk_top)
    total = jnp.zeros((1, TILE), F32)
    out = jnp.zeros((HEAD, TILE), F32)
    for c, kv_ref in enumerate(chunks):
        weights = jnp.exp(s_ref[pl.ds(c * ROWS, ROWS), :] - top)
        total += jnp.sum(weights, axis=0, keepdims=True)
        out += dot(kv_ref[:, HEAD:], weights.astype(BF16), TN)
    att_ref[...] = (out / total).T.astype(BF16)
    lse_ref[...] = top + jnp.log(total)


def tile_spec(cols):
    return pl.BlockSpec((TILE, cols), lambda i: (i, 0))


def row_spec(rows):
    return pl.BlockSpec((rows, TILE), lambda i: (0, i))


def cost(matmuls, pairs):
    return pl.CostEstimate(
        flops=matmuls * 2 * pairs * 2 * HEAD, bytes_accessed=4 << 20, transcendentals=pairs
    )


def once(*shape):
    return pl.BlockSpec(shape, lambda i: (0,) * len(shape), pipeline_mode=pl.Buffered(1))


def forward(q, kvs, bias):
    return pl.pallas_call(
        forward_body,
        out_shape=[
            jax.ShapeDtypeStruct((ROWS, HEAD), BF16),
            jax.ShapeDtypeStruct((1, ROWS), F32),
        ],
        grid=(ROWS // TILE,),
        in_specs=[tile_spec(HEAD), *[once(ROWS, 2 * HEAD)] * 4, once(4 * UNITS, HEAD)],
        out_specs=[tile_spec(HEAD), row_spec(1)],
        scratch_shapes=[
            pltpu.VMEM((4 * ROWS, 2 * HEAD), BF16),
            pltpu.VMEM((4 * ROWS, TILE), F32),
        ],
        cost_estimate=cost(2, 4 * ROWS * ROWS),
        compiler_params=pltpu.CompilerParams(vmem_limit_bytes=24 << 20),
        name="forward",
    )(q, *kvs, bias)


def delta_body(g_ref, att_ref, d_ref):
    product = g_ref[...].astype(F32) * att_ref[...].astype(F32)
    d_ref[...] = jnp.sum(product.T, axis=0, keepdims=True)


def row_delta(g, att):
    return pl.pallas_call(
        delta_body,
        out_shape=jax.ShapeDtypeStruct((1, ROWS), F32),
        grid=(ROWS // TILE,),
        in_specs=[tile_spec(HEAD)] * 2,
        out_specs=row_spec(1),
        cost_estimate=pl.CostEstimate(flops=0, bytes_accessed=1 << 20, transcendentals=0),
        name="delta",
    )(g, att)


def query_body(q_ref, g_ref, lse_ref, delta_ref, kv0, kv1, kv2, kv3, bias_ref, dq_ref, ka_ref, s_ref):
    step = pl.program_id(0)
    chunks = (kv0, kv1, kv2, kv3)

    @pl.when(step == 0)
    def _():
        fill_keys(chunks, bias_ref, ka_ref)

    qa = query_wide(q_ref[...], step * (TILE // SPAN))
    g = g_ref[...]
    lse = lse_ref[...]
    delta = delta_ref[...]
    total = jnp.zeros((HEAD, TILE), F32)
    for c, kv_ref in enumerate(chunks):
        s_ref[...] = dot(ka_ref[pl.ds(c * ROWS, ROWS), :], qa, NT)
        if c == 0:
            rows = pl.ds(pl.multiple_of(step * TILE, TILE), TILE)
            s_ref[rows, :] = jnp.where(later_in_span(), LOW, s_ref[rows, :])
        prob = jnp.exp(s_ref[...] - lse)
        dprob = dot(kv_ref[:, HEAD:], g, NT)
        ds = (prob * (dprob - delta)).astype(BF16)
        total += dot(kv_ref[:, :HEAD], ds, TN)
    dq_ref[...] = (total * SCALE).T.astype(BF16)


def query_grad(q, g, lse, delta, kvs, bias):
    return pl.pallas_call(
        query_body,
        out_shape=jax.ShapeDtypeStruct((ROWS, HEAD), BF16),
        grid=(ROWS // TILE,),
        in_specs=[
            tile_spec(HEAD),
            tile_spec(HEAD),
            row_spec(1),
            row_spec(1),
            *[once(ROWS, 2 * HEAD)] * 4,
            once(4 * UNITS, HEAD),
        ],
        out_specs=tile_spec(HEAD),
        scratch_shapes=[
            pltpu.VMEM((4 * ROWS, 2 * HEAD), BF16),
            pltpu.VMEM((ROWS, TILE), F32),
        ],
        cost_estimate=cost(3, 4 * ROWS * ROWS),
        compiler_params=pltpu.CompilerParams(vmem_limit_bytes=16 << 20),
        name="query_grad",
    )(q, g, lse, delta, *kvs, bias)


def key_body(*refs):
    kv_ref, bias_ref = refs[:2]
    qs, gs, stats = refs[2:6], refs[6:10], refs[10]
    dk_ref, dv_ref, ka_ref, s_ref, dk_acc, dv_acc = refs[11:]
    ka_ref[:, :HEAD] = kv_ref[:, :HEAD]
    ka_ref[:, HEAD:] = spread_bias(bias_ref[:UNITS, :])
    dk_acc[...] = jnp.zeros_like(dk_acc)
    dv_acc[...] = jnp.zeros_like(dv_acc)
    for c in range(4):

        def tile(i, _, c=c):
            rows = pl.ds(pl.multiple_of(i * TILE, TILE), TILE)
            q = qs[c][rows, :]
            g = gs[c][rows, :]
            lse = stats[2 * c : 2 * c + 1, rows]
            delta = stats[2 * c + 1 : 2 * c + 2, rows]
            qa = query_wide(q, i * (TILE // SPAN) + c * UNITS)
            s_ref[...] = dot(ka_ref[...], qa, NT)
            if c == 0:
                s_ref[rows, :] = jnp.where(later_in_span(), LOW, s_ref[rows, :])
            prob = jnp.exp(s_ref[...] - lse)
            dprob = dot(kv_ref[:, HEAD:], g, NT)
            ds = (prob * (dprob - delta)).astype(BF16)
            dv_acc[...] += dot(prob.astype(BF16), g, NN)
            dk_acc[...] += dot(ds, q, NN)
            return 0

        lax.fori_loop(0, ROWS // TILE, tile, 0)
    dk_ref[...] = (dk_acc[...] * SCALE).astype(BF16)
    dv_ref[...] = dv_acc[...].astype(BF16)


def key_grad(kv, bias, qs, gs, stats):
    return pl.pallas_call(
        key_body,
        out_shape=[jax.ShapeDtypeStruct((ROWS, HEAD), BF16)] * 2,
        grid=(1,),
        in_specs=[
            once(ROWS, 2 * HEAD),
            once(4 * UNITS, HEAD),
            *[once(ROWS, HEAD)] * 8,
            once(8, ROWS),
        ],
        out_specs=[once(ROWS, HEAD)] * 2,
        scratch_shapes=[
            pltpu.VMEM((ROWS, 2 * HEAD), BF16),
            pltpu.VMEM((ROWS, TILE), F32),
            pltpu.VMEM((ROWS, HEAD), F32),
            pltpu.VMEM((ROWS, HEAD), F32),
        ],
        cost_estimate=cost(4, 4 * ROWS * ROWS),
        compiler_params=pltpu.CompilerParams(vmem_limit_bytes=16 << 20),
        name="key_grad",
    )(kv, bias, *qs, *gs, stats)


ZY = ("z", "y")
CHIPS = ("z", "y", "xl", "xh")
SWAP = [(0, 1), (1, 0)]


def other_core(x):
    return lax.ppermute(x, "core", SWAP)


def other_chip(x):
    return lax.ppermute(x, "xl", SWAP)


def everyone(x):
    far = other_chip(x)
    return x, other_core(x), far, other_core(far)


def exchange(x, axes):
    return lax.all_to_all(x, axes, 0, 0, tiled=True)


def in_order(first, own, peer):
    return jnp.stack([jnp.where(first, own, peer), jnp.where(first, peer, own)])


def span_bias(span_order, block_mask, xl, core):
    count = span_order.shape[0]
    row = jnp.arange(count, dtype=jnp.int32)
    owner, unit = row // UNITS, row % UNITS
    row_xl = xl ^ (owner // 2)
    half = core ^ (owner % 2) ^ ((unit // 4 + unit % 4) % 2)
    storage = 2 * (2 * unit + row_xl) + half
    held = (storage[:, None] == jnp.arange(count, dtype=jnp.int32)[None, :]).astype(jnp.int32)
    position = jnp.sum(held * span_order[None, :], axis=1)
    hot = (position[:, None] == jnp.arange(count, dtype=jnp.int32)[None, :]).astype(F32)
    pairs = jnp.dot(hot, jnp.dot(block_mask.astype(F32).T, hot.T))
    allowed = (pairs > 0.5) & (position[:, None] <= position[None, :])
    bias = jnp.where(allowed, 0.0, LOW).astype(F32)
    return jnp.pad(bias, ((0, 0), (0, HEAD - count)))


def by_unit(rows, kinds):
    split = rows.reshape(2, SPAN, kinds, HEADS, HEAD)
    return split.transpose(0, 3, 1, 2, 4).reshape(UNITS, SPAN, kinds * HEAD)


def by_row(blocks, kinds):
    split = blocks.reshape(2, HEADS, SPAN, kinds, HEAD)
    return split.transpose(0, 2, 3, 1, 4).reshape(2, SPAN, kinds * HEADS * HEAD)


def side_by_side(first, own, peer):
    return jnp.concatenate([jnp.where(first, own, peer), jnp.where(first, peer, own)], axis=-1)


def to_narrow(x):
    return jnp.concatenate(jnp.split(x, 2, axis=-1), axis=-2)


def from_narrow(x):
    return jnp.concatenate(jnp.split(x, 2, axis=-2), axis=-1)


def across(x):
    return lax.ppermute(x, ("xl", "xh"), [(k, k ^ 3) for k in range(4)])


def weight_body(xl_ref, own_ref, other_ref, out_ref):
    for flip, part in enumerate((own_ref, other_ref)):
        for c in range(2):
            rows = part[:, c * 32 : (c + 1) * 32, :]
            out_ref[:, xl_ref[0] ^ flip, :, c * 512 : (c + 1) * 512] = rows


def weight_whole(xl, own, other):
    return pl.pallas_call(
        weight_body,
        out_shape=jax.ShapeDtypeStruct((UNITS, 2, 32, 1024), BF16),
        grid=(1,),
        in_specs=[pl.BlockSpec(memory_space=pltpu.SMEM)] + [once(UNITS, SPAN, 512)] * 2,
        out_specs=once(UNITS, 2, 32, 1024),
        cost_estimate=pl.CostEstimate(flops=0, bytes_accessed=4 << 20, transcendentals=0),
        compiler_params=pltpu.CompilerParams(vmem_limit_bytes=12 << 20),
        name="weight_whole",
    )(xl, own, other)


def term_body(xl_ref, att_ref, up_ref, own_ref, other_ref, sum_ref):
    for c in range(2):
        cols = slice(c * 512, (c + 1) * 512)
        sum_ref[...] = dot(att_ref[...], up_ref[:, cols], TN).astype(BF16).reshape(sum_ref.shape)
        for flip, part in enumerate((own_ref, other_ref)):
            part[:, c * 32 : (c + 1) * 32, :] = sum_ref[:, xl_ref[0] ^ flip]


def weight_terms(xl, att, up):
    return pl.pallas_call(
        term_body,
        out_shape=[jax.ShapeDtypeStruct((UNITS, SPAN, 512), BF16)] * 2,
        grid=(1,),
        in_specs=[pl.BlockSpec(memory_space=pltpu.SMEM), once(256, 1024), once(256, 1024)],
        out_specs=[once(UNITS, SPAN, 512)] * 2,
        scratch_shapes=[pltpu.VMEM((UNITS, 2, 32, 512), BF16)],
        cost_estimate=pl.CostEstimate(
            flops=2 * 256 * 1024 * 1024, bytes_accessed=4 << 20, transcendentals=0
        ),
        compiler_params=pltpu.CompilerParams(vmem_limit_bytes=16 << 20),
        name="weight_terms",
    )(xl, att, up)


def local(query_states, key_states, value_states, span_order, block_mask, output_weight, upstream):
    z, y, xl, xh, core = (lax.axis_index(a) for a in ("z", "y", "xl", "xh", "core"))
    first_core = core == 0
    half = core ^ ((z + y) % 2)
    cols = output_weight.shape[1] // 2

    def mine(x, axis):
        return lax.dynamic_index_in_dim(x, core, axis, False)

    def theirs(x, axis):
        return lax.dynamic_index_in_dim(x, 1 - core, axis, False)

    def share(rows):
        halves = rows.reshape(2, SPAN, -1)
        own = lax.dynamic_index_in_dim(halves, half, 0, False)
        peer = other_core(lax.dynamic_index_in_dim(halves, 1 - half, 0, False))
        return in_order(first_core, own, peer)

    def unshare(both):
        own = mine(both, 0)
        peer = other_core(theirs(both, 0))
        return in_order(half == 0, own, peer).reshape(2 * SPAN, -1)

    weight_cols = output_weight.reshape(-1, 2, cols)
    weight_rows = in_order(first_core, mine(weight_cols, 1), other_core(theirs(weight_cols, 1)))
    weight_rows = weight_rows.reshape(-1, cols)
    weight_rows = in_order(xh == 0, weight_rows, lax.ppermute(weight_rows, "xh", SWAP))
    weight_rows = to_narrow(weight_rows.reshape(-1, cols))
    copies = jnp.broadcast_to(weight_rows[None], (UNITS, *weight_rows.shape))
    states = share(jnp.concatenate([query_states[0], key_states[0], value_states[0]], axis=1))
    blocks = exchange(jnp.concatenate([by_unit(states, 3), copies], axis=2), ZY)
    q = blocks[:, :, :HEAD].reshape(ROWS, HEAD)
    own_kv = blocks[:, :, HEAD : 3 * HEAD].reshape(ROWS, 2 * HEAD)
    far_kv = other_chip(own_kv)
    weight_own = blocks[:, :, 3 * HEAD :]
    weight_other = across(weight_own)
    kvs = (own_kv, other_core(own_kv), far_kv, other_core(far_kv))
    bias = span_bias(span_order, block_mask, xl, core)

    up_cols = upstream[0].reshape(2 * SPAN, 2, cols)
    up = in_order(first_core, mine(up_cols, 1), other_core(theirs(up_cols, 1)))
    up = up.reshape(2, 2, SPAN, cols)
    up = in_order(half == 0, up[:, 0], up[:, 1]).reshape(4 * SPAN, cols)

    attended, lse = forward(q, kvs, bias)

    place, lse = lax.optimization_barrier((xl.reshape(1), lse))
    weight = weight_whole(place, weight_own, weight_other).reshape(HEADS * HEAD, cols)
    grad_rows = dot(up, weight, NT)
    grad_rows = grad_rows[: 2 * SPAN] + other_core(grad_rows[2 * SPAN :])
    grad_rows = grad_rows.astype(BF16).reshape(2, SPAN, -1)
    crossing = jnp.concatenate(
        [attended.reshape(UNITS, SPAN, HEAD), by_unit(grad_rows, 1)], axis=2
    )
    crossed = exchange(crossing, ZY)
    qs = everyone(q)
    g = crossed[:, :, HEAD:].reshape(ROWS, HEAD)
    delta = row_delta(g, attended)
    stats = jnp.concatenate([lse, delta], axis=0)
    stats = jnp.concatenate([stats, other_core(stats)], axis=0)
    stats_far = other_chip(stats)
    gs = everyone(g)

    attended_rows = by_row(crossed[:, :, :HEAD], 1)
    attended_rows = jnp.stack([attended_rows, other_core(attended_rows)]).reshape(4 * SPAN, -1)
    place, stats_far = lax.optimization_barrier((xl.reshape(1), stats_far))
    stats = jnp.concatenate([stats, stats_far], axis=0)
    term_own, term_sent = weight_terms(place, attended_rows, up)
    term_other = across(term_sent)
    projected = dot(attended_rows, weight, NN).astype(BF16).reshape(2, 2, SPAN, cols)
    own, peer = mine(projected, 1), other_core(theirs(projected, 1))
    own = in_order(half == 0, own[0], own[1]).reshape(2 * SPAN, cols)
    peer = in_order(half == 0, peer[1], peer[0]).reshape(2 * SPAN, cols)
    projected = side_by_side(first_core, own, peer)

    query_out = query_grad(q, g, lse, delta, kvs, bias)
    key_out, value_out = key_grad(own_kv, bias, qs, gs, stats)
    term = (term_own.astype(F32) + term_other.astype(F32)).astype(BF16)
    grads = [x.reshape(UNITS, SPAN, HEAD) for x in (query_out, key_out, value_out)]
    grads = exchange(jnp.concatenate([*grads, term], axis=2), ZY)
    summed = jnp.sum(grads[:, :, 3 * HEAD :].astype(F32), axis=0)
    summed = from_narrow(summed).reshape(2, 16, cols)
    partner = lax.ppermute(lax.dynamic_index_in_dim(summed, 1 - xh, 0, False), "xh", SWAP)
    summed = (lax.dynamic_index_in_dim(summed, xh, 0, False) + partner).reshape(2, -1, cols)
    grads = grads[:, :, : 3 * HEAD]
    weight_gradient = side_by_side(first_core, mine(summed, 0), other_core(theirs(summed, 0)))
    grads = unshare(by_row(grads, 3))
    query_gradient, key_gradient, value_gradient = jnp.split(grads, 3, axis=1)
    return (
        projected[None],
        query_gradient[None],
        key_gradient[None],
        value_gradient[None],
        weight_gradient,
    )


def solution(mesh):
    axes = ("z", "y", "xl", "xh", "core")
    fine = Mesh(mesh.devices.reshape(4, 4, 2, 2, 2), axes)
    rows = P(("xh", "core"), ("z", "y", "xl"), None)
    return jax.shard_map(
        local,
        mesh=fine,
        in_specs=(rows, rows, rows, P(), P(), P(axes, None), rows),
        out_specs=(rows, rows, rows, rows, P(axes, None)),
        check_vma=False,
    )
```

```python
import functools

import jax
import jax.numpy as jnp
from jax import lax
from jax.experimental import pallas as pl
from jax.experimental.pallas import tpu as pltpu
from jax.sharding import Mesh, PartitionSpec as P

HEADS = 8
HEAD = 128
SPAN = 64
UNITS = 16
ROWS = UNITS * SPAN
TILE = 256
LOW = -1e30
SCALE = 1.0 / HEAD
F32 = jnp.float32
BF16 = jnp.bfloat16
NT = (((1,), (1,)), ((), ()))
NN = (((1,), (0,)), ((), ()))
TN = (((0,), (0,)), ((), ()))


def dot(a, b, dims):
    return lax.dot_general(a, b, dims, preferred_element_type=F32)


def span_hot(first_span):
    span = lax.broadcasted_iota(jnp.int32, (TILE, HEAD), 0) // SPAN + first_span
    lane = lax.broadcasted_iota(jnp.int32, (TILE, HEAD), 1)
    return (span == lane).astype(F32).astype(BF16)


def query_wide(query, first_span):
    return jnp.concatenate([query * BF16(SCALE), span_hot(first_span)], axis=1)


def spread_bias(bias):
    return jnp.broadcast_to(bias[:, None, :], (UNITS, SPAN, HEAD)).reshape(ROWS, HEAD).astype(BF16)


def fill_keys(chunks, bias_ref, ka_ref):
    for c, kv_ref in enumerate(chunks):
        rows = pl.ds(c * ROWS, ROWS)
        ka_ref[rows, :HEAD] = kv_ref[:, :HEAD]
        ka_ref[rows, HEAD:] = spread_bias(bias_ref[c * UNITS : (c + 1) * UNITS, :])


def later_in_span():
    key = lax.broadcasted_iota(jnp.int32, (TILE, TILE), 0)
    query = lax.broadcasted_iota(jnp.int32, (TILE, TILE), 1)
    return (key // SPAN == query // SPAN) & (key > query)


def forward_body(q_ref, kv0, kv1, kv2, kv3, bias_ref, att_ref, lse_ref, ka_ref, s_ref):
    step = pl.program_id(0)
    chunks = (kv0, kv1, kv2, kv3)

    @pl.when(step == 0)
    def _():
        fill_keys(chunks, bias_ref, ka_ref)

    qa = query_wide(q_ref[...], step * (TILE // SPAN))
    top = None
    for c in range(4):
        rows = pl.ds(c * ROWS, ROWS)
        s_ref[rows, :] = dot(ka_ref[rows, :], qa, NT)
        if c == 0:
            own = pl.ds(pl.multiple_of(step * TILE, TILE), TILE)
            s_ref[own, :] = jnp.where(later_in_span(), LOW, s_ref[own, :])
        chunk_top = jnp.max(s_ref[rows, :], axis=0, keepdims=True)
        top = chunk_top if c == 0 else jnp.maximum(top, chunk_top)
    total = jnp.zeros((1, TILE), F32)
    out = jnp.zeros((HEAD, TILE), F32)
    for c, kv_ref in enumerate(chunks):
        weights = jnp.exp(s_ref[pl.ds(c * ROWS, ROWS), :] - top)
        total += jnp.sum(weights, axis=0, keepdims=True)
        out += dot(kv_ref[:, HEAD:], weights.astype(BF16), TN)
    att_ref[...] = (out / total).T.astype(BF16)
    lse_ref[...] = top + jnp.log(total)


def tile_spec(cols):
    return pl.BlockSpec((TILE, cols), lambda i: (i, 0))


def row_spec(rows):
    return pl.BlockSpec((rows, TILE), lambda i: (0, i))


def cost(matmuls, pairs):
    return pl.CostEstimate(
        flops=matmuls * 2 * pairs * 2 * HEAD, bytes_accessed=4 << 20, transcendentals=pairs
    )


def once(*shape):
    return pl.BlockSpec(shape, lambda i: (0,) * len(shape), pipeline_mode=pl.Buffered(1))


def forward(q, kvs, bias):
    return pl.pallas_call(
        forward_body,
        out_shape=[
            jax.ShapeDtypeStruct((ROWS, HEAD), BF16),
            jax.ShapeDtypeStruct((1, ROWS), F32),
        ],
        grid=(ROWS // TILE,),
        in_specs=[tile_spec(HEAD), *[once(ROWS, 2 * HEAD)] * 4, once(4 * UNITS, HEAD)],
        out_specs=[tile_spec(HEAD), row_spec(1)],
        scratch_shapes=[
            pltpu.VMEM((4 * ROWS, 2 * HEAD), BF16),
            pltpu.VMEM((4 * ROWS, TILE), F32),
        ],
        cost_estimate=cost(2, 4 * ROWS * ROWS),
        compiler_params=pltpu.CompilerParams(vmem_limit_bytes=24 << 20),
        name="forward",
    )(q, *kvs, bias)


def row_delta(g, att):
    return jnp.sum((g.astype(F32) * att.astype(F32)).T, axis=0, keepdims=True)


def query_body(q_ref, g_ref, att_ref, lse_ref, kv0, kv1, kv2, kv3, bias_ref, dq_ref, ka_ref, s_ref):
    step = pl.program_id(0)
    chunks = (kv0, kv1, kv2, kv3)

    @pl.when(step == 0)
    def _():
        fill_keys(chunks, bias_ref, ka_ref)

    qa = query_wide(q_ref[...], step * (TILE // SPAN))
    g = g_ref[...]
    lse = lse_ref[...]
    delta = row_delta(g, att_ref[...])
    total = jnp.zeros((HEAD, TILE), F32)
    for c, kv_ref in enumerate(chunks):
        s_ref[...] = dot(ka_ref[pl.ds(c * ROWS, ROWS), :], qa, NT)
        if c == 0:
            rows = pl.ds(pl.multiple_of(step * TILE, TILE), TILE)
            s_ref[rows, :] = jnp.where(later_in_span(), LOW, s_ref[rows, :])
        prob = jnp.exp(s_ref[...] - lse)
        dprob = dot(kv_ref[:, HEAD:], g, NT)
        ds = (prob * (dprob - delta)).astype(BF16)
        total += dot(kv_ref[:, :HEAD], ds, TN)
    dq_ref[...] = (total * SCALE).T.astype(BF16)


def query_grad(q, g, att, lse, kvs, bias):
    return pl.pallas_call(
        query_body,
        out_shape=jax.ShapeDtypeStruct((ROWS, HEAD), BF16),
        grid=(ROWS // TILE,),
        in_specs=[
            tile_spec(HEAD),
            tile_spec(HEAD),
            tile_spec(HEAD),
            row_spec(1),
            *[once(ROWS, 2 * HEAD)] * 4,
            once(4 * UNITS, HEAD),
        ],
        out_specs=tile_spec(HEAD),
        scratch_shapes=[
            pltpu.VMEM((4 * ROWS, 2 * HEAD), BF16),
            pltpu.VMEM((ROWS, TILE), F32),
        ],
        cost_estimate=cost(3, 4 * ROWS * ROWS),
        compiler_params=pltpu.CompilerParams(vmem_limit_bytes=16 << 20),
        name="query_grad",
    )(q, g, att, lse, *kvs, bias)


def key_body(*refs):
    kv_ref, bias_ref = refs[:2]
    pairs, gs, lses = refs[2:6], refs[6:10], refs[10]
    dk_ref, dv_ref, ka_ref, s_ref, dk_acc, dv_acc = refs[11:]
    ka_ref[:, :HEAD] = kv_ref[:, :HEAD]
    ka_ref[:, HEAD:] = spread_bias(bias_ref[:UNITS, :])
    dk_acc[...] = jnp.zeros_like(dk_acc)
    dv_acc[...] = jnp.zeros_like(dv_acc)
    for c in range(4):

        def tile(i, _, c=c):
            rows = pl.ds(pl.multiple_of(i * TILE, TILE), TILE)
            q = pairs[c][rows, :HEAD]
            g = gs[c][rows, :]
            lse = lses[c : c + 1, rows]
            delta = row_delta(g, pairs[c][rows, HEAD:])
            qa = query_wide(q, i * (TILE // SPAN) + c * UNITS)
            s_ref[...] = dot(ka_ref[...], qa, NT)
            if c == 0:
                s_ref[rows, :] = jnp.where(later_in_span(), LOW, s_ref[rows, :])
            prob = jnp.exp(s_ref[...] - lse)
            dprob = dot(kv_ref[:, HEAD:], g, NT)
            ds = (prob * (dprob - delta)).astype(BF16)
            dv_acc[...] += dot(prob.astype(BF16), g, NN)
            dk_acc[...] += dot(ds, q, NN)
            return 0

        lax.fori_loop(0, ROWS // TILE, tile, 0)
    dk_ref[...] = (dk_acc[...] * SCALE).astype(BF16)
    dv_ref[...] = dv_acc[...].astype(BF16)


def key_grad(kv, bias, pairs, gs, lses):
    return pl.pallas_call(
        key_body,
        out_shape=[jax.ShapeDtypeStruct((ROWS, HEAD), BF16)] * 2,
        grid=(1,),
        in_specs=[
            once(ROWS, 2 * HEAD),
            once(4 * UNITS, HEAD),
            *[once(ROWS, 2 * HEAD)] * 4,
            *[once(ROWS, HEAD)] * 4,
            once(4, ROWS),
        ],
        out_specs=[once(ROWS, HEAD)] * 2,
        scratch_shapes=[
            pltpu.VMEM((ROWS, 2 * HEAD), BF16),
            pltpu.VMEM((ROWS, TILE), F32),
            pltpu.VMEM((ROWS, HEAD), F32),
            pltpu.VMEM((ROWS, HEAD), F32),
        ],
        cost_estimate=cost(4, 4 * ROWS * ROWS),
        compiler_params=pltpu.CompilerParams(vmem_limit_bytes=16 << 20),
        name="key_grad",
    )(kv, bias, *pairs, *gs, lses)


ZY = ("z", "y")
CHIPS = ("z", "y", "xl", "xh")
SWAP = [(0, 1), (1, 0)]


def other_core(x):
    return lax.ppermute(x, "core", SWAP)


def other_chip(x):
    return lax.ppermute(x, "xl", SWAP)


def everyone(x):
    far = other_chip(x)
    return x, other_core(x), far, other_core(far)


def exchange(x, axes):
    return lax.all_to_all(x, axes, 0, 0, tiled=True)


def in_order(first, own, peer):
    return jnp.stack([jnp.where(first, own, peer), jnp.where(first, peer, own)])


def span_bias(span_order, block_mask, xl, core):
    count = span_order.shape[0]
    row = jnp.arange(count, dtype=jnp.int32)
    owner, unit = row // UNITS, row % UNITS
    row_xl = xl ^ (owner // 2)
    half = core ^ (owner % 2) ^ ((unit // 4 + unit % 4) % 2)
    storage = 2 * (2 * unit + row_xl) + half
    held = (storage[:, None] == jnp.arange(count, dtype=jnp.int32)[None, :]).astype(jnp.int32)
    position = jnp.sum(held * span_order[None, :], axis=1)
    hot = (position[:, None] == jnp.arange(count, dtype=jnp.int32)[None, :]).astype(F32)
    pairs = jnp.dot(hot, jnp.dot(block_mask.astype(F32).T, hot.T))
    allowed = (pairs > 0.5) & (position[:, None] <= position[None, :])
    bias = jnp.where(allowed, 0.0, LOW).astype(F32)
    return jnp.pad(bias, ((0, 0), (0, HEAD - count)))


def side_by_side(first, own, peer):
    return jnp.concatenate([jnp.where(first, own, peer), jnp.where(first, peer, own)], axis=-1)


def across(x):
    return lax.ppermute(x, ("xl", "xh"), [(k, k ^ 3) for k in range(4)])


def weight_body(xl_ref, own_ref, other_ref, out_ref):
    for flip, part in enumerate((own_ref, other_ref)):
        for c in range(2):
            rows = part[:, c * 32 : (c + 1) * 32, :]
            out_ref[:, xl_ref[0] ^ flip, :, c * 512 : (c + 1) * 512] = rows


def weight_whole(xl, own, other):
    return pl.pallas_call(
        weight_body,
        out_shape=jax.ShapeDtypeStruct((UNITS, 2, 32, 1024), BF16),
        grid=(1,),
        in_specs=[pl.BlockSpec(memory_space=pltpu.SMEM)] + [once(UNITS, SPAN, 512)] * 2,
        out_specs=once(UNITS, 2, 32, 1024),
        cost_estimate=pl.CostEstimate(flops=0, bytes_accessed=4 << 20, transcendentals=0),
        compiler_params=pltpu.CompilerParams(vmem_limit_bytes=12 << 20),
        name="weight_whole",
    )(xl, own, other)


def term_body(own_ref, peer_ref, up_ref, out_ref):
    att = jnp.concatenate([own_ref[...], peer_ref[...]], axis=0)
    for c in range(2):
        cols = slice(c * 512, (c + 1) * 512)
        out_ref[:, cols] = dot(att, up_ref[:, cols], TN).astype(BF16)


def weight_terms(own, peer, up):
    return pl.pallas_call(
        term_body,
        out_shape=jax.ShapeDtypeStruct((1024, 1024), BF16),
        grid=(1,),
        in_specs=[once(128, 1024), once(128, 1024), once(256, 1024)],
        out_specs=once(1024, 1024),
        cost_estimate=pl.CostEstimate(
            flops=2 * 256 * 1024 * 1024, bytes_accessed=4 << 20, transcendentals=0
        ),
        compiler_params=pltpu.CompilerParams(vmem_limit_bytes=16 << 20),
        name="weight_terms",
    )(own, peer, up)


IN_SMEM = pl.BlockSpec(memory_space=pltpu.SMEM)


def move(body, name, outs, scalars, *arrays):
    return pl.pallas_call(
        body,
        out_shape=[jax.ShapeDtypeStruct(shape, BF16) for shape in outs],
        grid=(1,),
        in_specs=[IN_SMEM] * len(scalars) + [once(*x.shape) for x in arrays],
        out_specs=[once(*shape) for shape in outs],
        cost_estimate=pl.CostEstimate(flops=0, bytes_accessed=4 << 20, transcendentals=0),
        compiler_params=pltpu.CompilerParams(vmem_limit_bytes=12 << 20),
        name=name,
    )(*scalars, *arrays)


def head_cols(h):
    return slice(h * HEAD, (h + 1) * HEAD)


def span_rows(half):
    return pl.ds(pl.multiple_of(half * SPAN, SPAN), SPAN)


def cut_body(half_ref, q_ref, k_ref, v_ref, own_ref, sent_ref):
    for side, out in enumerate((own_ref, sent_ref)):
        rows = span_rows(half_ref[0] ^ side)
        for t, x in enumerate((q_ref, k_ref, v_ref)):
            for h in range(HEADS):
                out[h, :, head_cols(t)] = x[rows, head_cols(h)]


def fill_body(core_ref, xh_ref, own_ref, peer_ref, w0, w1, w2, w3, out_ref):
    core, xh = core_ref[0], xh_ref[0]
    out_ref[pl.ds(core * HEADS, HEADS), :, : 3 * HEAD] = own_ref[...]
    out_ref[pl.ds((1 - core) * HEADS, HEADS), :, : 3 * HEAD] = peer_ref[...]
    first, mine_first = core == 0, xh == 0
    w = [x[...].astype(F32) for x in (w0, w1, w2, w3)]
    near = [jnp.where(first, w[0], w[1]), jnp.where(first, w[1], w[0])]
    far = [jnp.where(first, w[2], w[3]), jnp.where(first, w[3], w[2])]
    front = [jnp.where(mine_first, a, b) for a, b in zip(near, far)]
    back = [jnp.where(mine_first, b, a) for a, b in zip(near, far)]
    rows = jnp.concatenate(front + back, axis=0).astype(BF16)
    for c in range(2):
        part = rows[:, c * 512 : (c + 1) * 512]
        for unit in range(UNITS):
            out_ref[unit, c * 32 : (c + 1) * 32, 3 * HEAD :] = part


def split_body(x_ref, q_ref, kv_ref, w_ref):
    x = x_ref[...]
    q_ref[...] = x[:, :, :HEAD].reshape(ROWS, HEAD)
    kv_ref[...] = x[:, :, HEAD : 3 * HEAD].reshape(ROWS, 2 * HEAD)
    w_ref[...] = x[:, :, 3 * HEAD :]


def cross_body(att_ref, own_ref, peer_ref, out_ref):
    for s in range(2):
        for h in range(HEADS):
            unit, rows = s * HEADS + h, slice(s * SPAN, (s + 1) * SPAN)
            out_ref[unit, :, :HEAD] = att_ref[unit * SPAN : (unit + 1) * SPAN, :]
            total = own_ref[rows, head_cols(h)] + peer_ref[rows, head_cols(h)]
            out_ref[unit, :, HEAD:] = total.astype(BF16)


def land_body(x_ref, att_ref, g_ref):
    g_ref[...] = x_ref[:, :, HEAD:].reshape(ROWS, HEAD)
    for s in range(2):
        for h in range(HEADS):
            att_ref[s * SPAN : (s + 1) * SPAN, head_cols(h)] = x_ref[s * HEADS + h, :, :HEAD]


def final_body(core_ref, half_ref, own_ref, peer_ref, dq_ref, dk_ref, dv_ref):
    core, half = core_ref[0], half_ref[0]
    for t, out in enumerate((dq_ref, dk_ref, dv_ref)):
        for h in range(HEADS):
            out[span_rows(half), head_cols(h)] = own_ref[core * HEADS + h, :, head_cols(t)]
            out[span_rows(1 - half), head_cols(h)] = peer_ref[h, :, head_cols(t)]


def local(query_states, key_states, value_states, span_order, block_mask, output_weight, upstream):
    z, y, xl, xh, core = (lax.axis_index(a) for a in ("z", "y", "xl", "xh", "core"))
    first_core = core == 0
    half = core ^ ((z + y) % 2)
    core_1, xl_1, xh_1, half_1 = (x.reshape(1) for x in (core, xl, xh, half))
    cols = output_weight.shape[1] // 2

    def by_core(x):
        left, right = x[..., :cols], x[..., cols:]
        return jnp.where(first_core, left, right), jnp.where(first_core, right, left)

    weight_mine, weight_theirs = by_core(output_weight)
    weight_rows = [
        weight_mine,
        other_core(weight_theirs),
        lax.ppermute(weight_mine, "xh", SWAP),
        lax.ppermute(weight_theirs, ("xh", "core"), [(k, 3 - k) for k in range(4)]),
    ]
    unit_rows = (HEADS, SPAN, 3 * HEAD)
    own, sent = move(
        cut_body,
        "cut",
        [unit_rows] * 2,
        [half_1],
        query_states[0],
        key_states[0],
        value_states[0],
    )
    (blocks,) = move(
        fill_body,
        "fill",
        [(UNITS, SPAN, 3 * HEAD + 512)],
        [core_1, xh_1],
        own,
        other_core(sent),
        *weight_rows,
    )
    blocks = exchange(blocks, ZY)
    q, own_kv, weight_own = move(
        split_body,
        "split",
        [(ROWS, HEAD), (ROWS, 2 * HEAD), (UNITS, SPAN, 512)],
        [],
        blocks,
    )
    far_kv = other_chip(own_kv)
    weight_other = across(weight_own)
    kvs = (own_kv, other_core(own_kv), far_kv, other_core(far_kv))
    bias = span_bias(span_order, block_mask, xl, core)

    up_mine, up_theirs = by_core(upstream[0])
    up = in_order(first_core, up_mine, other_core(up_theirs)).reshape(2, 2, SPAN, cols)
    up = in_order(half == 0, up[:, 0], up[:, 1]).reshape(4 * SPAN, cols)

    attended, lse = forward(q, kvs, bias)

    place, lse = lax.optimization_barrier((xl_1, lse))
    weight = weight_whole(place, weight_own, weight_other).reshape(HEADS * HEAD, cols)
    grad_rows = dot(up, weight, NT)
    grad_own, grad_sent = grad_rows[: 2 * SPAN], grad_rows[2 * SPAN :]
    (crossing,) = move(
        cross_body, "cross", [(UNITS, SPAN, 2 * HEAD)], [], attended, grad_own, other_core(grad_sent)
    )
    crossed = exchange(crossing, ZY)
    pairs = everyone(jnp.concatenate([q, attended], axis=1))
    lses = jnp.concatenate([lse, other_core(lse)], axis=0)
    lses = jnp.concatenate([lses, other_chip(lses)], axis=0)

    att_own, g = move(land_body, "land", [(2 * SPAN, HEADS * HEAD), (ROWS, HEAD)], [], crossed)
    gs = everyone(g)
    att_peer = other_core(att_own)
    term = weight_terms(att_own, att_peer, up).reshape(UNITS, SPAN, cols)
    term = exchange(term, ZY)

    query_out = query_grad(q, g, attended, lse, kvs, bias)
    key_out, value_out = key_grad(own_kv, bias, pairs, gs, lses)
    grads = [x.reshape(UNITS, SPAN, HEAD) for x in (query_out, key_out, value_out)]
    grads = exchange(jnp.concatenate(grads, axis=2), ZY)

    def project(att):
        return dot(att, weight, NN).astype(BF16).reshape(2, SPAN, cols)

    own, peer = project(att_own), project(att_peer)
    kept = [lax.dynamic_index_in_dim(x, core, 0, False) for x in (own, peer)]
    gone = jnp.stack([lax.dynamic_index_in_dim(x, 1 - core, 0, False) for x in (own, peer)])
    gone = other_core(gone)
    own = in_order(half == 0, kept[0], kept[1]).reshape(2 * SPAN, cols)
    peer = in_order(half == 0, gone[1], gone[0]).reshape(2 * SPAN, cols)
    projected = side_by_side(first_core, own, peer)

    summed = jnp.sum(term.astype(F32), axis=0).reshape(4, 16, cols)
    chip = 2 * xl + xh
    total = lax.dynamic_index_in_dim(summed, chip, 0, False)
    for step in (1, 2, 3):
        part = lax.dynamic_index_in_dim(summed, chip ^ step, 0, False)
        total = total + lax.ppermute(part, ("xl", "xh"), [(k, k ^ step) for k in range(4)])
    total = total.reshape(2, -1, cols)
    own = lax.dynamic_index_in_dim(total, core, 0, False)
    peer = other_core(lax.dynamic_index_in_dim(total, 1 - core, 0, False))
    weight_gradient = side_by_side(first_core, own, peer)

    peer = other_core(lax.dynamic_slice_in_dim(grads, (1 - core) * HEADS, HEADS, 0))
    own_rows = (2 * SPAN, HEADS * HEAD)
    query_gradient, key_gradient, value_gradient = move(
        final_body, "final", [own_rows] * 3, [core_1, half_1], grads, peer
    )
    return (
        projected[None],
        query_gradient[None],
        key_gradient[None],
        value_gradient[None],
        weight_gradient,
    )


def solution(mesh):
    axes = ("z", "y", "xl", "xh", "core")
    fine = Mesh(mesh.devices.reshape(4, 4, 2, 2, 2), axes)
    rows = P(("xh", "core"), ("z", "y", "xl"), None)
    return jax.shard_map(
        local,
        mesh=fine,
        in_specs=(rows, rows, rows, P(), P(), P(axes, None), rows),
        out_specs=(rows, rows, rows, rows, P(axes, None)),
        check_vma=False,
    )
```

```python
import functools

import jax
import jax.numpy as jnp
from jax import lax
from jax.experimental import pallas as pl
from jax.experimental.pallas import tpu as pltpu
from jax.sharding import Mesh, PartitionSpec as P

HEADS = 8
HEAD = 128
SPAN = 64
UNITS = 16
MANY = 12
ROWS = UNITS * SPAN
TILE = 256
LOW = -1e30
GRANT = 16 << 20
SCALE = 1.0 / HEAD
F32 = jnp.float32
BF16 = jnp.bfloat16
NT = (((1,), (1,)), ((), ()))
NN = (((1,), (0,)), ((), ()))
TN = (((0,), (0,)), ((), ()))


def in_hbm(x):
    return pltpu.with_memory_space_constraint(x, pltpu.HBM)


def dot(a, b, dims):
    return lax.dot_general(a, b, dims, preferred_element_type=F32)


def span_hot(first_span):
    span = lax.broadcasted_iota(jnp.int32, (TILE, HEAD), 0) // SPAN + first_span
    lane = lax.broadcasted_iota(jnp.int32, (TILE, HEAD), 1)
    return (span == lane).astype(F32).astype(BF16)


def query_wide(query, first_span):
    return jnp.concatenate([query * BF16(SCALE), span_hot(first_span)], axis=1)


def spread_bias(bias):
    return jnp.broadcast_to(bias[:, None, :], (UNITS, SPAN, HEAD)).reshape(ROWS, HEAD).astype(BF16)


def fill_keys(chunks, bias_ref, ka_ref, first_chunk=0):
    for c, kv_ref in enumerate(chunks):
        rows = pl.ds(c * ROWS, ROWS)
        spans = slice((first_chunk + c) * UNITS, (first_chunk + c + 1) * UNITS)
        ka_ref[rows, :HEAD] = kv_ref[:, :HEAD]
        ka_ref[rows, HEAD:] = spread_bias(bias_ref[spans, :])


def later_in_span():
    key = lax.broadcasted_iota(jnp.int32, (TILE, TILE), 0)
    query = lax.broadcasted_iota(jnp.int32, (TILE, TILE), 1)
    return (key // SPAN == query // SPAN) & (key > query)


def forward_body(first, *refs):
    if first:
        q_ref, kv0, kv1, bias_ref, o_ref, m_ref, l_ref, ka_ref, s_ref = refs
    else:
        q_ref, kv0, kv1, bias_ref, o0_ref, m0_ref, l0_ref, pair_ref, lse_ref, ka_ref, s_ref = refs
    step = pl.program_id(0)
    chunks = (kv0, kv1)

    @pl.when(step == 0)
    def _():
        fill_keys(chunks, bias_ref, ka_ref, 0 if first else 2)

    q = q_ref[...]
    qa = query_wide(q, step * (TILE // SPAN))
    top = None if first else m0_ref[...]
    for c in range(2):
        rows = pl.ds(c * ROWS, ROWS)
        s_ref[rows, :] = dot(ka_ref[rows, :], qa, NT)
        if first and c == 0:
            own = pl.ds(pl.multiple_of(step * TILE, TILE), TILE)
            s_ref[own, :] = jnp.where(later_in_span(), LOW, s_ref[own, :])
        chunk_top = jnp.max(s_ref[rows, :], axis=0, keepdims=True)
        top = chunk_top if top is None else jnp.maximum(top, chunk_top)
    total = jnp.zeros((1, TILE), F32)
    out = jnp.zeros((HEAD, TILE), F32)
    for c, kv_ref in enumerate(chunks):
        weights = jnp.exp(s_ref[pl.ds(c * ROWS, ROWS), :] - top)
        total += jnp.sum(weights, axis=0, keepdims=True)
        out += dot(kv_ref[:, HEAD:], weights.astype(BF16), TN)
    if first:
        o_ref[...] = out
        m_ref[...] = top
        l_ref[...] = total
    else:
        fade = jnp.exp(m0_ref[...] - top)
        total += l0_ref[...] * fade
        out = (out + o0_ref[...] * fade) / total
        pair_ref[:, :HEAD] = q
        pair_ref[:, HEAD:] = out.T.astype(BF16)
        lse_ref[...] = top + jnp.log(total)


def tile_spec(cols):
    return pl.BlockSpec((TILE, cols), lambda i: (i, 0))


def row_spec(rows):
    return pl.BlockSpec((rows, TILE), lambda i: (0, i))


def cost(matmuls, pairs):
    return pl.CostEstimate(
        flops=matmuls * 2 * pairs * 2 * HEAD, bytes_accessed=4 << 20, transcendentals=pairs
    )


def once(*shape):
    return pl.BlockSpec(shape, lambda i: (0,) * len(shape), pipeline_mode=pl.Buffered(1))


def forward(first, q, kvs, bias, *carry):
    stat = jax.ShapeDtypeStruct((1, ROWS), F32)
    if first:
        outs = [pltpu.HBM((HEAD, ROWS), F32), stat, stat]
        out_specs = [row_spec(HEAD), row_spec(1), row_spec(1)]
    else:
        outs = [pltpu.HBM((ROWS, 2 * HEAD), BF16), stat]
        out_specs = [tile_spec(2 * HEAD), row_spec(1)]
    return pl.pallas_call(
        functools.partial(forward_body, first),
        out_shape=outs,
        grid=(ROWS // TILE,),
        in_specs=[
            tile_spec(HEAD),
            *[once(ROWS, 2 * HEAD)] * 2,
            once(4 * UNITS, HEAD),
            *[row_spec(x.shape[0]) for x in carry],
        ],
        out_specs=out_specs,
        scratch_shapes=[
            pltpu.VMEM((2 * ROWS, 2 * HEAD), BF16),
            pltpu.VMEM((2 * ROWS, TILE), F32),
        ],
        cost_estimate=cost(2, 2 * ROWS * ROWS),
        compiler_params=pltpu.CompilerParams(vmem_limit_bytes=GRANT),
        name="forward_near" if first else "forward_far",
    )(q, *kvs, bias, *carry)


def row_delta(g, att):
    return jnp.sum((g.astype(F32) * att.astype(F32)).T, axis=0, keepdims=True)


def query_body(pair_ref, g_ref, lse_ref, far_ref, kv0, kv1, kv2, kv3, bias_ref, dq_ref, ka_ref, s_ref):
    step = pl.program_id(0)
    chunks = (kv0, kv1, kv2, kv3)

    @pl.when(step == 0)
    def _():
        fill_keys(chunks, bias_ref, ka_ref)

    qa = query_wide(pair_ref[:, :HEAD], step * (TILE // SPAN))
    g = g_ref[...]
    lse = lse_ref[...]
    delta = row_delta(g, pair_ref[:, HEAD:])
    total = jnp.zeros((HEAD, TILE), F32)
    for c, kv_ref in enumerate(chunks):
        s_ref[...] = dot(ka_ref[pl.ds(c * ROWS, ROWS), :], qa, NT)
        if c == 0:
            rows = pl.ds(pl.multiple_of(step * TILE, TILE), TILE)
            s_ref[rows, :] = jnp.where(later_in_span(), LOW, s_ref[rows, :])
        prob = jnp.exp(s_ref[...] - lse)
        dprob = dot(kv_ref[:, HEAD:], g, NT)
        ds = (prob * (dprob - delta)).astype(BF16)
        total += dot(kv_ref[:, :HEAD], ds, TN)
    dq_ref[...] = (total * SCALE).T.astype(BF16)


def query_grad(pair, g, lse, far, kvs, bias):
    return pl.pallas_call(
        query_body,
        out_shape=jax.ShapeDtypeStruct((ROWS, HEAD), BF16),
        grid=(ROWS // TILE,),
        in_specs=[
            tile_spec(2 * HEAD),
            tile_spec(HEAD),
            row_spec(1),
            pl.BlockSpec(memory_space=pl.ANY),
            *[once(ROWS, 2 * HEAD)] * 4,
            once(4 * UNITS, HEAD),
        ],
        out_specs=tile_spec(HEAD),
        scratch_shapes=[
            pltpu.VMEM((4 * ROWS, 2 * HEAD), BF16),
            pltpu.VMEM((ROWS, TILE), F32),
        ],
        cost_estimate=cost(3, 4 * ROWS * ROWS),
        compiler_params=pltpu.CompilerParams(vmem_limit_bytes=GRANT),
        name="query_grad",
    )(pair, g, lse, far, *kvs, bias)


def key_body(*refs):
    kv_ref, bias_ref = refs[:2]
    pairs, gs, lses = refs[2:6], refs[6:10], refs[10]
    dk_ref, dv_ref, ka_ref, s_ref, dk_acc, dv_acc = refs[11:]
    ka_ref[:, :HEAD] = kv_ref[:, :HEAD]
    ka_ref[:, HEAD:] = spread_bias(bias_ref[:UNITS, :])
    dk_acc[...] = jnp.zeros_like(dk_acc)
    dv_acc[...] = jnp.zeros_like(dv_acc)
    for c in range(4):

        def tile(i, _, c=c):
            rows = pl.ds(pl.multiple_of(i * TILE, TILE), TILE)
            q = pairs[c][rows, :HEAD]
            g = gs[c][rows, :]
            lse = lses[c : c + 1, rows]
            delta = row_delta(g, pairs[c][rows, HEAD:])
            qa = query_wide(q, i * (TILE // SPAN) + c * UNITS)
            s_ref[...] = dot(ka_ref[...], qa, NT)
            if c == 0:
                s_ref[rows, :] = jnp.where(later_in_span(), LOW, s_ref[rows, :])
            prob = jnp.exp(s_ref[...] - lse)
            dprob = dot(kv_ref[:, HEAD:], g, NT)
            ds = (prob * (dprob - delta)).astype(BF16)
            dv_acc[...] += dot(prob.astype(BF16), g, NN)
            dk_acc[...] += dot(ds, q, NN)
            return 0

        lax.fori_loop(0, ROWS // TILE, tile, 0)
    dk_ref[...] = (dk_acc[...] * SCALE).astype(BF16)
    dv_ref[...] = dv_acc[...].astype(BF16)


def key_grad(kv, bias, pairs, gs, lses):
    return pl.pallas_call(
        key_body,
        out_shape=[jax.ShapeDtypeStruct((ROWS, HEAD), BF16)] * 2,
        grid=(1,),
        in_specs=[
            once(ROWS, 2 * HEAD),
            once(4 * UNITS, HEAD),
            *[once(ROWS, 2 * HEAD)] * 4,
            *[once(ROWS, HEAD)] * 4,
            once(4, ROWS),
        ],
        out_specs=[once(ROWS, HEAD)] * 2,
        scratch_shapes=[
            pltpu.VMEM((ROWS, 2 * HEAD), BF16),
            pltpu.VMEM((ROWS, TILE), F32),
            pltpu.VMEM((ROWS, HEAD), F32),
            pltpu.VMEM((ROWS, HEAD), F32),
        ],
        cost_estimate=cost(4, 4 * ROWS * ROWS),
        compiler_params=pltpu.CompilerParams(vmem_limit_bytes=GRANT),
        name="key_grad",
    )(kv, bias, *pairs, *gs, lses)


ZY = ("z", "y")
CHIPS = ("z", "y", "xl", "xh")
SWAP = [(0, 1), (1, 0)]


def other_core(x):
    return lax.ppermute(x, "core", SWAP)


def other_chip(x):
    return lax.ppermute(x, "xl", SWAP)


def everyone(x):
    far = other_chip(x)
    return x, other_core(x), far, other_core(far)


def exchange(x, axes):
    return lax.all_to_all(x, axes, 0, 0, tiled=True)


def in_order(first, own, peer):
    return jnp.stack([jnp.where(first, own, peer), jnp.where(first, peer, own)])


def span_bias(span_order, block_mask, xl, core):
    count = span_order.shape[0]
    row = jnp.arange(count, dtype=jnp.int32)
    owner, unit = row // UNITS, row % UNITS
    row_xl = xl ^ (owner // 2)
    half = core ^ (owner % 2) ^ ((unit // 4 + unit % 4) % 2)
    storage = 2 * (2 * unit + row_xl) + half
    held = (storage[:, None] == jnp.arange(count, dtype=jnp.int32)[None, :]).astype(jnp.int32)
    position = jnp.sum(held * span_order[None, :], axis=1)
    hot = (position[:, None] == jnp.arange(count, dtype=jnp.int32)[None, :]).astype(F32)
    pairs = jnp.dot(hot, jnp.dot(block_mask.astype(F32).T, hot.T))
    allowed = (pairs > 0.5) & (position[:, None] <= position[None, :])
    bias = jnp.where(allowed, 0.0, LOW).astype(F32)
    return jnp.pad(bias, ((0, 0), (0, HEAD - count)))


def side_by_side(first, own, peer):
    return jnp.concatenate([jnp.where(first, own, peer), jnp.where(first, peer, own)], axis=-1)


def across(x):
    return lax.ppermute(x, ("xl", "xh"), [(k, k ^ 3) for k in range(4)])


def weight_body(xl_ref, own0, own1, other0, other1, out_ref):
    for flip, pieces in enumerate(((own0, own1), (other0, other1))):
        for units, part in zip((slice(0, MANY), slice(MANY, UNITS)), pieces):
            for c in range(2):
                rows = part[:, c * 32 : (c + 1) * 32, :]
                out_ref[units, xl_ref[0] ^ flip, :, c * 512 : (c + 1) * 512] = rows


def weight_whole(xl, own, other):
    return pl.pallas_call(
        weight_body,
        out_shape=pltpu.HBM((UNITS, 2, 32, 1024), BF16),
        grid=(1,),
        in_specs=[pl.BlockSpec(memory_space=pltpu.SMEM)] + [once(*x.shape) for x in (*own, *other)],
        out_specs=once(UNITS, 2, 32, 1024),
        cost_estimate=pl.CostEstimate(flops=0, bytes_accessed=4 << 20, transcendentals=0),
        compiler_params=pltpu.CompilerParams(vmem_limit_bytes=GRANT),
        name="weight_whole",
    )(xl, *own, *other)


def term_body(own_ref, peer_ref, up_ref, out_ref):
    att = jnp.concatenate([own_ref[...], peer_ref[...]], axis=0)
    for c in range(2):
        cols = slice(c * 512, (c + 1) * 512)
        out_ref[:, cols] = dot(att, up_ref[:, cols], TN).astype(BF16)


def weight_terms(own, peer, up):
    return pl.pallas_call(
        term_body,
        out_shape=pltpu.HBM((1024, 1024), BF16),
        grid=(1,),
        in_specs=[once(128, 1024), once(128, 1024), once(256, 1024)],
        out_specs=once(1024, 1024),
        cost_estimate=pl.CostEstimate(
            flops=2 * 256 * 1024 * 1024, bytes_accessed=4 << 20, transcendentals=0
        ),
        compiler_params=pltpu.CompilerParams(vmem_limit_bytes=GRANT),
        name="weight_terms",
    )(own, peer, up)


IN_SMEM = pl.BlockSpec(memory_space=pltpu.SMEM)


def move(body, name, outs, scalars, *arrays, space=jax.ShapeDtypeStruct):
    return pl.pallas_call(
        body,
        out_shape=[space(shape, BF16) for shape in outs],
        grid=(1,),
        in_specs=[IN_SMEM] * len(scalars) + [once(*x.shape) for x in arrays],
        out_specs=[once(*shape) for shape in outs],
        cost_estimate=pl.CostEstimate(flops=0, bytes_accessed=4 << 20, transcendentals=0),
        compiler_params=pltpu.CompilerParams(vmem_limit_bytes=GRANT),
        name=name,
    )(*scalars, *arrays)


def head_cols(h):
    return slice(h * HEAD, (h + 1) * HEAD)


def span_rows(half):
    return pl.ds(pl.multiple_of(half * SPAN, SPAN), SPAN)


def cut_body(half_ref, q_ref, k_ref, v_ref, own_ref, sent_ref):
    for side, out in enumerate((own_ref, sent_ref)):
        rows = span_rows(half_ref[0] ^ side)
        for t, x in enumerate((q_ref, k_ref, v_ref)):
            for h in range(HEADS):
                out[h, :, head_cols(t)] = x[rows, head_cols(h)]


def fill_body(core_ref, xh_ref, own_ref, peer_ref, w0, w1, w2, w3, out_ref):
    core, xh = core_ref[0], xh_ref[0]
    out_ref[pl.ds(core * HEADS, HEADS), :, : 3 * HEAD] = own_ref[...]
    out_ref[pl.ds((1 - core) * HEADS, HEADS), :, : 3 * HEAD] = peer_ref[...]
    first, mine_first = core == 0, xh == 0
    w = [x[...].astype(F32) for x in (w0, w1, w2, w3)]
    near = [jnp.where(first, w[0], w[1]), jnp.where(first, w[1], w[0])]
    far = [jnp.where(first, w[2], w[3]), jnp.where(first, w[3], w[2])]
    front = [jnp.where(mine_first, a, b) for a, b in zip(near, far)]
    back = [jnp.where(mine_first, b, a) for a, b in zip(near, far)]
    rows = jnp.concatenate(front + back, axis=0).astype(BF16)
    for c in range(2):
        part = rows[:, c * 512 : (c + 1) * 512]
        for unit in range(UNITS):
            out_ref[unit, c * 32 : (c + 1) * 32, 3 * HEAD :] = part


def split_body(x_ref, q_ref, kv_ref, w0_ref, w1_ref):
    x = x_ref[...]
    q_ref[...] = x[:, :, :HEAD].reshape(ROWS, HEAD)
    kv_ref[...] = x[:, :, HEAD : 3 * HEAD].reshape(ROWS, 2 * HEAD)
    w0_ref[...] = x[:MANY, :, 3 * HEAD :]
    w1_ref[...] = x[MANY:, :, 3 * HEAD :]


def cross_body(pair_ref, own_ref, peer_ref, lses_ref, out_ref):
    for s in range(2):
        for h in range(HEADS):
            unit, rows = s * HEADS + h, slice(s * SPAN, (s + 1) * SPAN)
            out_ref[unit, :, :HEAD] = pair_ref[unit * SPAN : (unit + 1) * SPAN, HEAD:]
            total = own_ref[rows, head_cols(h)] + peer_ref[rows, head_cols(h)]
            out_ref[unit, :, HEAD:] = total.astype(BF16)


def land_body(x_ref, att_ref, g_ref):
    g_ref[...] = x_ref[:, :, HEAD:].reshape(ROWS, HEAD)
    for s in range(2):
        for h in range(HEADS):
            att_ref[s * SPAN : (s + 1) * SPAN, head_cols(h)] = x_ref[s * HEADS + h, :, :HEAD]


def final_body(core_ref, half_ref, own_ref, peer_ref, dq_ref, dk_ref, dv_ref):
    core, half = core_ref[0], half_ref[0]
    for t, out in enumerate((dq_ref, dk_ref, dv_ref)):
        for h in range(HEADS):
            out[span_rows(half), head_cols(h)] = own_ref[core * HEADS + h, :, head_cols(t)]
            out[span_rows(1 - half), head_cols(h)] = peer_ref[h, :, head_cols(t)]


def local(query_states, key_states, value_states, span_order, block_mask, output_weight, upstream):
    z, y, xl, xh, core = (lax.axis_index(a) for a in ("z", "y", "xl", "xh", "core"))
    first_core = core == 0
    half = core ^ ((z + y) % 2)
    core_1, xl_1, xh_1, half_1 = (x.reshape(1) for x in (core, xl, xh, half))
    cols = output_weight.shape[1] // 2

    def by_core(x):
        left, right = x[..., :cols], x[..., cols:]
        return jnp.where(first_core, left, right), jnp.where(first_core, right, left)

    weight_mine, weight_theirs = by_core(output_weight)
    weight_rows = [
        weight_mine,
        other_core(weight_theirs),
        lax.ppermute(weight_mine, "xh", SWAP),
        lax.ppermute(weight_theirs, ("xh", "core"), [(k, 3 - k) for k in range(4)]),
    ]
    unit_rows = (HEADS, SPAN, 3 * HEAD)
    own, sent = move(
        cut_body,
        "cut",
        [unit_rows] * 2,
        [half_1],
        in_hbm(query_states[0]),
        in_hbm(key_states[0]),
        in_hbm(value_states[0]),
        space=pltpu.HBM,
    )
    (blocks,) = move(
        fill_body,
        "fill",
        [(UNITS, SPAN, 3 * HEAD + 512)],
        [core_1, xh_1],
        in_hbm(own),
        other_core(sent),
        *weight_rows,
    )
    blocks = exchange(blocks, ZY)
    q, own_kv, *weight_own = move(
        split_body,
        "split",
        [(ROWS, HEAD), (ROWS, 2 * HEAD), (MANY, SPAN, 512), (UNITS - MANY, SPAN, 512)],
        [],
        blocks,
        space=pltpu.HBM,
    )
    far_kv = other_chip(own_kv)
    weight_other = [across(weight_own[0]), other_chip(weight_own[1])]
    near_kv = other_core(own_kv)
    bias = span_bias(span_order, block_mask, xl, core)

    up_mine, up_theirs = by_core(upstream[0])
    up = in_order(first_core, up_mine, other_core(up_theirs)).reshape(2, 2, SPAN, cols)
    up = in_order(half == 0, up[:, 0], up[:, 1]).reshape(4 * SPAN, cols)

    out, top, total = forward(True, in_hbm(q), (in_hbm(own_kv), near_kv), bias)
    far_kv, total = lax.optimization_barrier((far_kv, total))
    kvs = (own_kv, near_kv, far_kv, other_core(far_kv))
    pair, lse = forward(False, in_hbm(q), kvs[2:], bias, in_hbm(out), top, total)
    lses = jnp.concatenate([lse, other_core(lse)], axis=0)
    lses = jnp.concatenate([lses, other_chip(lses)], axis=0)

    place, lse = lax.optimization_barrier((xl_1, lse))
    weight = weight_whole(place, [in_hbm(x) for x in weight_own], weight_other).reshape(HEADS * HEAD, cols)
    grad_rows = dot(up, weight, NT)
    grad_own, grad_sent = grad_rows[: 2 * SPAN], grad_rows[2 * SPAN :]
    (crossing,) = move(
        cross_body,
        "cross",
        [(UNITS, SPAN, 2 * HEAD)],
        [],
        in_hbm(pair),
        grad_own,
        other_core(grad_sent),
        lses,
    )
    crossed = exchange(crossing, ZY)
    pairs = everyone(pair)

    att_own, g = move(
        land_body,
        "land",
        [(2 * SPAN, HEADS * HEAD), (ROWS, HEAD)],
        [],
        crossed,
        space=pltpu.HBM,
    )
    gs = everyone(g)
    att_peer = other_core(att_own)
    term = weight_terms(att_own, att_peer, up).reshape(UNITS, SPAN, cols)
    term = exchange(term, ZY)

    query_out = query_grad(in_hbm(pair), in_hbm(g), lse, pairs[2], [in_hbm(x) for x in kvs], bias)
    key_out, value_out = key_grad(in_hbm(own_kv), bias, pairs, gs, lses)
    grads = [x.reshape(UNITS, SPAN, HEAD) for x in (query_out, key_out, value_out)]
    grads = exchange(jnp.concatenate(grads, axis=2), ZY)

    def project(att):
        return dot(att, weight, NN).astype(BF16).reshape(2, SPAN, cols)

    own, peer = project(att_own), project(att_peer)
    kept = [lax.dynamic_index_in_dim(x, core, 0, False) for x in (own, peer)]
    gone = jnp.stack([lax.dynamic_index_in_dim(x, 1 - core, 0, False) for x in (own, peer)])
    gone = other_core(gone)
    own = in_order(half == 0, kept[0], kept[1]).reshape(2 * SPAN, cols)
    peer = in_order(half == 0, gone[1], gone[0]).reshape(2 * SPAN, cols)
    projected = side_by_side(first_core, own, peer)

    summed = jnp.sum(term.astype(F32), axis=0).reshape(4, 16, cols)
    chip = 2 * xl + xh
    total = lax.dynamic_index_in_dim(summed, chip, 0, False)
    for step in (1, 2, 3):
        part = lax.dynamic_index_in_dim(summed, chip ^ step, 0, False)
        total = total + lax.ppermute(part, ("xl", "xh"), [(k, k ^ step) for k in range(4)])
    total = total.reshape(2, -1, cols)
    own = lax.dynamic_index_in_dim(total, core, 0, False)
    peer = other_core(lax.dynamic_index_in_dim(total, 1 - core, 0, False))
    weight_gradient = side_by_side(first_core, own, peer)

    peer = other_core(lax.dynamic_slice_in_dim(grads, (1 - core) * HEADS, HEADS, 0))
    own_rows = (2 * SPAN, HEADS * HEAD)
    query_gradient, key_gradient, value_gradient = move(
        final_body, "final", [own_rows] * 3, [core_1, half_1], grads, peer
    )
    return (
        projected[None],
        query_gradient[None],
        key_gradient[None],
        value_gradient[None],
        weight_gradient,
    )


def solution(mesh):
    axes = ("z", "y", "xl", "xh", "core")
    fine = Mesh(mesh.devices.reshape(4, 4, 2, 2, 2), axes)
    rows = P(("xh", "core"), ("z", "y", "xl"), None)
    return jax.shard_map(
        local,
        mesh=fine,
        in_specs=(rows, rows, rows, P(), P(), P(axes, None), rows),
        out_specs=(rows, rows, rows, rows, P(axes, None)),
        check_vma=False,
    )
```

```python
import functools

import jax
import jax.numpy as jnp
from jax import lax
from jax.experimental import pallas as pl
from jax.experimental.pallas import tpu as pltpu
from jax.sharding import Mesh, PartitionSpec as P

HEADS = 8
HEAD = 128
SPAN = 64
UNITS = 16
MANY = 12
ROWS = UNITS * SPAN
TILE = 256
LOW = -1e30
GRANT = 16 << 20
WIDE_GRANT = 32 << 20
SCALE = 1.0 / HEAD
F32 = jnp.float32
BF16 = jnp.bfloat16
NT = (((1,), (1,)), ((), ()))
NN = (((1,), (0,)), ((), ()))
TN = (((0,), (0,)), ((), ()))


def in_hbm(x):
    return pltpu.with_memory_space_constraint(x, pltpu.HBM)


def dot(a, b, dims):
    return lax.dot_general(a, b, dims, preferred_element_type=F32)


def span_hot(first_span):
    span = lax.broadcasted_iota(jnp.int32, (TILE, HEAD), 0) // SPAN + first_span
    lane = lax.broadcasted_iota(jnp.int32, (TILE, HEAD), 1)
    return (span == lane).astype(F32).astype(BF16)


def query_wide(query, first_span):
    return jnp.concatenate([query * BF16(SCALE), span_hot(first_span)], axis=1)


def spread_bias(bias):
    return jnp.broadcast_to(bias[:, None, :], (UNITS, SPAN, HEAD)).reshape(ROWS, HEAD).astype(BF16)


def fill_keys(chunks, bias_ref, ka_ref, first_chunk=0):
    for c, kv_ref in enumerate(chunks):
        rows = pl.ds(c * ROWS, ROWS)
        spans = slice((first_chunk + c) * UNITS, (first_chunk + c + 1) * UNITS)
        ka_ref[rows, :HEAD] = kv_ref[:, :HEAD]
        ka_ref[rows, HEAD:] = spread_bias(bias_ref[spans, :])


def later_in_span():
    key = lax.broadcasted_iota(jnp.int32, (TILE, TILE), 0)
    query = lax.broadcasted_iota(jnp.int32, (TILE, TILE), 1)
    return (key // SPAN == query // SPAN) & (key > query)


def forward_body(first, *refs):
    if first:
        q_ref, kv0, kv1, bias_ref, o_ref, m_ref, l_ref, ka_ref, s_ref = refs
    else:
        q_ref, kv0, kv1, bias_ref, o0_ref, m0_ref, l0_ref, pair_ref, lse_ref, ka_ref, s_ref = refs
    step = pl.program_id(0)
    chunks = (kv0, kv1)

    @pl.when(step == 0)
    def _():
        fill_keys(chunks, bias_ref, ka_ref, 0 if first else 2)

    q = q_ref[...]
    qa = query_wide(q, step * (TILE // SPAN))
    top = None if first else m0_ref[...]
    for c in range(2):
        rows = pl.ds(c * ROWS, ROWS)
        s_ref[rows, :] = dot(ka_ref[rows, :], qa, NT)
        if first and c == 0:
            own = pl.ds(pl.multiple_of(step * TILE, TILE), TILE)
            s_ref[own, :] = jnp.where(later_in_span(), LOW, s_ref[own, :])
        chunk_top = jnp.max(s_ref[rows, :], axis=0, keepdims=True)
        top = chunk_top if top is None else jnp.maximum(top, chunk_top)
    total = jnp.zeros((1, TILE), F32)
    out = jnp.zeros((HEAD, TILE), F32)
    for c, kv_ref in enumerate(chunks):
        weights = jnp.exp(s_ref[pl.ds(c * ROWS, ROWS), :] - top)
        total += jnp.sum(weights, axis=0, keepdims=True)
        out += dot(kv_ref[:, HEAD:], weights.astype(BF16), TN)
    if first:
        o_ref[...] = out
        m_ref[...] = top
        l_ref[...] = total
    else:
        fade = jnp.exp(m0_ref[...] - top)
        total += l0_ref[...] * fade
        out = (out + o0_ref[...] * fade) / total
        pair_ref[:, :HEAD] = q
        pair_ref[:, HEAD:] = out.T.astype(BF16)
        lse_ref[...] = top + jnp.log(total)


def tile_spec(cols):
    return pl.BlockSpec((TILE, cols), lambda i: (i, 0))


def row_spec(rows):
    return pl.BlockSpec((rows, TILE), lambda i: (0, i))


def cost(matmuls, pairs):
    return pl.CostEstimate(
        flops=matmuls * 2 * pairs * 2 * HEAD, bytes_accessed=4 << 20, transcendentals=pairs
    )


def once(*shape):
    return pl.BlockSpec(shape, lambda i: (0,) * len(shape), pipeline_mode=pl.Buffered(1))


def forward(first, q, kvs, bias, *carry):
    stat = jax.ShapeDtypeStruct((1, ROWS), F32)
    if first:
        outs = [pltpu.HBM((HEAD, ROWS), F32), stat, stat]
        out_specs = [row_spec(HEAD), row_spec(1), row_spec(1)]
    else:
        outs = [pltpu.HBM((ROWS, 2 * HEAD), BF16), stat]
        out_specs = [tile_spec(2 * HEAD), row_spec(1)]
    return pl.pallas_call(
        functools.partial(forward_body, first),
        out_shape=outs,
        grid=(ROWS // TILE,),
        in_specs=[
            tile_spec(HEAD),
            *[once(ROWS, 2 * HEAD)] * 2,
            once(4 * UNITS, HEAD),
            *[row_spec(x.shape[0]) for x in carry],
        ],
        out_specs=out_specs,
        scratch_shapes=[
            pltpu.VMEM((2 * ROWS, 2 * HEAD), BF16),
            pltpu.VMEM((2 * ROWS, TILE), F32),
        ],
        cost_estimate=cost(2, 2 * ROWS * ROWS),
        compiler_params=pltpu.CompilerParams(vmem_limit_bytes=GRANT),
        name="forward_near" if first else "forward_far",
    )(q, *kvs, bias, *carry)


def row_delta(g, att):
    return jnp.sum((g.astype(F32) * att.astype(F32)).T, axis=0, keepdims=True)


def query_body(pair_ref, g_ref, lse_ref, far_ref, kv0, kv1, kv2, kv3, bias_ref, dq_ref, ka_ref, s_ref):
    step = pl.program_id(0)
    chunks = (kv0, kv1, kv2, kv3)

    @pl.when(step == 0)
    def _():
        fill_keys(chunks, bias_ref, ka_ref)

    qa = query_wide(pair_ref[:, :HEAD], step * (TILE // SPAN))
    g = g_ref[...]
    lse = lse_ref[...]
    delta = row_delta(g, pair_ref[:, HEAD:])
    own = pl.ds(pl.multiple_of(step * TILE, TILE), TILE)
    s_ref[...] = dot(ka_ref[pl.ds(0, ROWS), :], qa, NT)
    s_ref[own, :] = jnp.where(later_in_span(), LOW, s_ref[own, :])
    total = jnp.zeros((HEAD, TILE), F32)
    for c, kv_ref in enumerate(chunks):
        scores = dot(ka_ref[pl.ds(c * ROWS, ROWS), :], qa, NT) if c else s_ref[...]
        prob = jnp.exp(scores - lse)
        dprob = dot(kv_ref[:, HEAD:], g, NT)
        ds = (prob * (dprob - delta)).astype(BF16)
        total += dot(kv_ref[:, :HEAD], ds, TN)
    dq_ref[...] = (total * SCALE).T.astype(BF16)


def query_grad(pair, g, lse, far, kvs, bias):
    return pl.pallas_call(
        query_body,
        out_shape=jax.ShapeDtypeStruct((ROWS, HEAD), BF16),
        grid=(ROWS // TILE,),
        in_specs=[
            tile_spec(2 * HEAD),
            tile_spec(HEAD),
            row_spec(1),
            pl.BlockSpec(memory_space=pl.ANY),
            *[once(ROWS, 2 * HEAD)] * 4,
            once(4 * UNITS, HEAD),
        ],
        out_specs=tile_spec(HEAD),
        scratch_shapes=[
            pltpu.VMEM((4 * ROWS, 2 * HEAD), BF16),
            pltpu.VMEM((ROWS, TILE), F32),
        ],
        cost_estimate=cost(3, 4 * ROWS * ROWS),
        compiler_params=pltpu.CompilerParams(vmem_limit_bytes=WIDE_GRANT),
        name="query_grad",
    )(pair, g, lse, far, *kvs, bias)


def key_body(*refs):
    kv_ref, bias_ref = refs[:2]
    pairs, gs, lses = refs[2:6], refs[6:10], refs[10]
    dk_ref, dv_ref, ka_ref, s_ref, dk_acc, dv_acc = refs[11:]
    ka_ref[:, :HEAD] = kv_ref[:, :HEAD]
    ka_ref[:, HEAD:] = spread_bias(bias_ref[:UNITS, :])
    dk_acc[...] = jnp.zeros_like(dk_acc)
    dv_acc[...] = jnp.zeros_like(dv_acc)

    def tile(i, _):
        rows = pl.ds(pl.multiple_of(i * TILE, TILE), TILE)
        dk = jnp.zeros((ROWS, HEAD), F32)
        dv = jnp.zeros((ROWS, HEAD), F32)
        for c in range(4):
            q = pairs[c][rows, :HEAD]
            g = gs[c][rows, :]
            lse = lses[c : c + 1, rows]
            delta = row_delta(g, pairs[c][rows, HEAD:])
            qa = query_wide(q, i * (TILE // SPAN) + c * UNITS)
            scores = dot(ka_ref[...], qa, NT)
            if c == 0:
                s_ref[...] = scores
                s_ref[rows, :] = jnp.where(later_in_span(), LOW, s_ref[rows, :])
                scores = s_ref[...]
            prob = jnp.exp(scores - lse)
            dprob = dot(kv_ref[:, HEAD:], g, NT)
            ds = (prob * (dprob - delta)).astype(BF16)
            dv += dot(prob.astype(BF16), g, NN)
            dk += dot(ds, q, NN)
        dk_acc[...] += dk
        dv_acc[...] += dv
        return 0

    lax.fori_loop(0, ROWS // TILE, tile, 0)
    dk_ref[...] = (dk_acc[...] * SCALE).astype(BF16)
    dv_ref[...] = dv_acc[...].astype(BF16)


def key_grad(kv, bias, pairs, gs, lses):
    return pl.pallas_call(
        key_body,
        out_shape=[jax.ShapeDtypeStruct((ROWS, HEAD), BF16)] * 2,
        grid=(1,),
        in_specs=[
            once(ROWS, 2 * HEAD),
            once(4 * UNITS, HEAD),
            *[once(ROWS, 2 * HEAD)] * 4,
            *[once(ROWS, HEAD)] * 4,
            once(4, ROWS),
        ],
        out_specs=[once(ROWS, HEAD)] * 2,
        scratch_shapes=[
            pltpu.VMEM((ROWS, 2 * HEAD), BF16),
            pltpu.VMEM((ROWS, TILE), F32),
            pltpu.VMEM((ROWS, HEAD), F32),
            pltpu.VMEM((ROWS, HEAD), F32),
        ],
        cost_estimate=cost(4, 4 * ROWS * ROWS),
        compiler_params=pltpu.CompilerParams(vmem_limit_bytes=WIDE_GRANT),
        name="key_grad",
    )(kv, bias, *pairs, *gs, lses)


ZY = ("z", "y")
CHIPS = ("z", "y", "xl", "xh")
SWAP = [(0, 1), (1, 0)]


def other_core(x):
    return lax.ppermute(x, "core", SWAP)


def other_chip(x):
    return lax.ppermute(x, "xl", SWAP)


def everyone(x):
    far = other_chip(x)
    return x, other_core(x), far, other_core(far)


def exchange(x, axes):
    return lax.all_to_all(x, axes, 0, 0, tiled=True)


def in_order(first, own, peer):
    return jnp.stack([jnp.where(first, own, peer), jnp.where(first, peer, own)])


def span_bias(span_order, block_mask, xl, core):
    count = span_order.shape[0]
    row = jnp.arange(count, dtype=jnp.int32)
    owner, unit = row // UNITS, row % UNITS
    row_xl = xl ^ (owner // 2)
    half = core ^ (owner % 2) ^ ((unit // 4 + unit % 4) % 2)
    storage = 2 * (2 * unit + row_xl) + half
    held = (storage[:, None] == jnp.arange(count, dtype=jnp.int32)[None, :]).astype(jnp.int32)
    position = jnp.sum(held * span_order[None, :], axis=1)
    hot = (position[:, None] == jnp.arange(count, dtype=jnp.int32)[None, :]).astype(F32)
    pairs = jnp.dot(hot, jnp.dot(block_mask.astype(F32).T, hot.T))
    allowed = (pairs > 0.5) & (position[:, None] <= position[None, :])
    bias = jnp.where(allowed, 0.0, LOW).astype(F32)
    return jnp.pad(bias, ((0, 0), (0, HEAD - count)))


def side_by_side(first, own, peer):
    return jnp.concatenate([jnp.where(first, own, peer), jnp.where(first, peer, own)], axis=-1)


def across(x):
    return lax.ppermute(x, ("xl", "xh"), [(k, k ^ 3) for k in range(4)])


def weight_body(xl_ref, own0, own1, other0, other1, up_ref, out_ref, keep_ref, send_ref, w_ref):
    for flip, pieces in enumerate(((own0, own1), (other0, other1))):
        for units, part in zip((slice(0, MANY), slice(MANY, UNITS)), pieces):
            for c in range(2):
                rows = part[:, c * 32 : (c + 1) * 32, :]
                w_ref[units, xl_ref[0] ^ flip, :, c * 512 : (c + 1) * 512] = rows
    weight = w_ref[...].reshape(1024, 1024)
    out_ref[...] = weight
    for rows, out in ((slice(0, 128), keep_ref), (slice(128, 256), send_ref)):
        out[...] = dot(up_ref[rows, :], weight, NT)


def weight_whole(xl, own, other, up):
    return pl.pallas_call(
        weight_body,
        out_shape=[
            pltpu.HBM((1024, 1024), BF16),
            jax.ShapeDtypeStruct((128, 1024), F32),
            jax.ShapeDtypeStruct((128, 1024), F32),
        ],
        grid=(1,),
        in_specs=[pl.BlockSpec(memory_space=pltpu.SMEM)]
        + [once(*x.shape) for x in (*own, *other, up)],
        out_specs=[once(1024, 1024), once(128, 1024), once(128, 1024)],
        scratch_shapes=[pltpu.VMEM((UNITS, 2, 32, 1024), BF16)],
        cost_estimate=pl.CostEstimate(
            flops=2 * 256 * 1024 * 1024, bytes_accessed=4 << 20, transcendentals=0
        ),
        compiler_params=pltpu.CompilerParams(vmem_limit_bytes=GRANT),
        name="weight_whole",
    )(xl, *own, *other, up)


def term_body(own_ref, peer_ref, up_ref, out_ref):
    att = jnp.concatenate([own_ref[...], peer_ref[...]], axis=0)
    for c in range(2):
        cols = slice(c * 512, (c + 1) * 512)
        out_ref[:, cols] = dot(att, up_ref[:, cols], TN).astype(BF16)


def weight_terms(own, peer, up):
    return pl.pallas_call(
        term_body,
        out_shape=pltpu.HBM((1024, 1024), BF16),
        grid=(1,),
        in_specs=[once(128, 1024), once(128, 1024), once(256, 1024)],
        out_specs=once(1024, 1024),
        cost_estimate=pl.CostEstimate(
            flops=2 * 256 * 1024 * 1024, bytes_accessed=4 << 20, transcendentals=0
        ),
        compiler_params=pltpu.CompilerParams(vmem_limit_bytes=GRANT),
        name="weight_terms",
    )(own, peer, up)


IN_SMEM = pl.BlockSpec(memory_space=pltpu.SMEM)


def move(body, name, outs, scalars, *arrays, space=jax.ShapeDtypeStruct):
    spaces = space if isinstance(space, list) else [space] * len(outs)
    return pl.pallas_call(
        body,
        out_shape=[make(shape, BF16) for make, shape in zip(spaces, outs)],
        grid=(1,),
        in_specs=[IN_SMEM] * len(scalars) + [once(*x.shape) for x in arrays],
        out_specs=[once(*shape) for shape in outs],
        cost_estimate=pl.CostEstimate(flops=0, bytes_accessed=4 << 20, transcendentals=0),
        compiler_params=pltpu.CompilerParams(vmem_limit_bytes=GRANT),
        name=name,
    )(*scalars, *arrays)


def head_cols(h):
    return slice(h * HEAD, (h + 1) * HEAD)


def span_rows(half):
    return pl.ds(pl.multiple_of(half * SPAN, SPAN), SPAN)


def cut_body(half_ref, q_ref, k_ref, v_ref, own_ref, sent_ref):
    for side, out in enumerate((own_ref, sent_ref)):
        rows = span_rows(half_ref[0] ^ side)
        for t, x in enumerate((q_ref, k_ref, v_ref)):
            for h in range(HEADS):
                out[h, :, head_cols(t)] = x[rows, head_cols(h)]


def fill_body(core_ref, xh_ref, own_ref, peer_ref, w0, w1, w2, w3, out_ref):
    core, xh = core_ref[0], xh_ref[0]
    out_ref[pl.ds(core * HEADS, HEADS), :, : 3 * HEAD] = own_ref[...]
    out_ref[pl.ds((1 - core) * HEADS, HEADS), :, : 3 * HEAD] = peer_ref[...]
    first, mine_first = core == 0, xh == 0
    w = [jnp.where(first, x[:, :1024], x[:, 1024:]).astype(F32) for x in (w0, w1, w2, w3)]
    near = [jnp.where(first, w[0], w[1]), jnp.where(first, w[1], w[0])]
    far = [jnp.where(first, w[2], w[3]), jnp.where(first, w[3], w[2])]
    front = [jnp.where(mine_first, a, b) for a, b in zip(near, far)]
    back = [jnp.where(mine_first, b, a) for a, b in zip(near, far)]
    rows = jnp.concatenate(front + back, axis=0).astype(BF16)
    for c in range(2):
        part = rows[:, c * 512 : (c + 1) * 512]
        for unit in range(UNITS):
            out_ref[unit, c * 32 : (c + 1) * 32, 3 * HEAD :] = part


def split_body(x_ref, q_ref, kv_ref, w0_ref, w1_ref):
    x = x_ref[...]
    q_ref[...] = x[:, :, :HEAD].reshape(ROWS, HEAD)
    kv_ref[...] = x[:, :, HEAD : 3 * HEAD].reshape(ROWS, 2 * HEAD)
    w0_ref[...] = x[:MANY, :, 3 * HEAD :]
    w1_ref[...] = x[MANY:, :, 3 * HEAD :]


def cross_body(pair_ref, own_ref, peer_ref, out_ref):
    for s in range(2):
        for h in range(HEADS):
            unit, rows = s * HEADS + h, slice(s * SPAN, (s + 1) * SPAN)
            out_ref[unit, :, :HEAD] = pair_ref[unit * SPAN : (unit + 1) * SPAN, HEAD:]
            total = own_ref[rows, head_cols(h)] + peer_ref[rows, head_cols(h)]
            out_ref[unit, :, HEAD:] = total.astype(BF16)


def land_body(x_ref, lses_ref, att_ref, g_ref):
    g_ref[...] = x_ref[:, :, HEAD:].reshape(ROWS, HEAD)
    for s in range(2):
        for h in range(HEADS):
            att_ref[s * SPAN : (s + 1) * SPAN, head_cols(h)] = x_ref[s * HEADS + h, :, :HEAD]


def final_body(core_ref, half_ref, own_ref, peer_ref, dq_ref, dk_ref, dv_ref):
    core, half = core_ref[0], half_ref[0]
    for t, out in enumerate((dq_ref, dk_ref, dv_ref)):
        for h in range(HEADS):
            out[span_rows(half), head_cols(h)] = own_ref[core * HEADS + h, :, head_cols(t)]
            out[span_rows(1 - half), head_cols(h)] = peer_ref[h, :, head_cols(t)]


def local(query_states, key_states, value_states, span_order, block_mask, output_weight, upstream):
    z, y, xl, xh, core = (lax.axis_index(a) for a in ("z", "y", "xl", "xh", "core"))
    first_core = core == 0
    half = core ^ ((z + y) % 2)
    core_1, xl_1, xh_1, half_1 = (x.reshape(1) for x in (core, xl, xh, half))
    cols = output_weight.shape[1] // 2

    def by_core(x):
        left, right = x[..., :cols], x[..., cols:]
        return jnp.where(first_core, left, right), jnp.where(first_core, right, left)

    weight_far = lax.ppermute(output_weight, "xh", SWAP)
    weight_rows = [output_weight, other_core(output_weight), weight_far, other_core(weight_far)]
    unit_rows = (HEADS, SPAN, 3 * HEAD)
    own, sent = move(
        cut_body,
        "cut",
        [unit_rows] * 2,
        [half_1],
        in_hbm(query_states[0]),
        in_hbm(key_states[0]),
        in_hbm(value_states[0]),
        space=pltpu.HBM,
    )
    (blocks,) = move(
        fill_body,
        "fill",
        [(UNITS, SPAN, 3 * HEAD + 512)],
        [core_1, xh_1],
        in_hbm(own),
        other_core(sent),
        *weight_rows,
        space=pltpu.HBM,
    )
    blocks = exchange(blocks, ZY)
    q, own_kv, *weight_own = move(
        split_body,
        "split",
        [(ROWS, HEAD), (ROWS, 2 * HEAD), (MANY, SPAN, 512), (UNITS - MANY, SPAN, 512)],
        [],
        blocks,
        space=pltpu.HBM,
    )
    far_kv = other_chip(own_kv)
    weight_other = [across(weight_own[0]), other_chip(weight_own[1])]
    near_kv = other_core(own_kv)
    bias = span_bias(span_order, block_mask, xl, core)

    up_mine, up_theirs = by_core(upstream[0])
    up = in_order(first_core, up_mine, other_core(up_theirs)).reshape(2, 2, SPAN, cols)
    up = in_order(half == 0, up[:, 0], up[:, 1]).reshape(4 * SPAN, cols)

    out, top, total = forward(True, in_hbm(q), (in_hbm(own_kv), near_kv), bias)
    far_kv, total = lax.optimization_barrier((far_kv, total))
    kvs = (own_kv, near_kv, far_kv, other_core(far_kv))
    pair, lse = forward(False, in_hbm(q), kvs[2:], bias, in_hbm(out), top, total)
    lses = jnp.concatenate([lse, other_core(lse)], axis=0)
    lses = jnp.concatenate([lses, other_chip(lses)], axis=0)

    place, lse = lax.optimization_barrier((xl_1, lse))
    weight, grad_own, grad_sent = weight_whole(
        place, [in_hbm(x) for x in weight_own], weight_other, up
    )
    (crossing,) = move(
        cross_body,
        "cross",
        [(UNITS, SPAN, 2 * HEAD)],
        [],
        in_hbm(pair),
        grad_own,
        other_core(grad_sent),
    )
    crossed = exchange(crossing, ZY)
    pairs = everyone(pair)

    att_own, g = move(
        land_body,
        "land",
        [(2 * SPAN, HEADS * HEAD), (ROWS, HEAD)],
        [],
        crossed,
        lses,
        space=[jax.ShapeDtypeStruct, pltpu.HBM],
    )
    gs = everyone(g)
    att_peer = other_core(att_own)
    term = weight_terms(att_own, att_peer, up).reshape(UNITS, SPAN, cols)
    term = exchange(term, ZY)

    query_out = query_grad(in_hbm(pair), in_hbm(g), lse, pairs[2], [in_hbm(x) for x in kvs], bias)
    key_out, value_out = key_grad(in_hbm(own_kv), bias, pairs, gs, lses)
    grads = [x.reshape(UNITS, SPAN, HEAD) for x in (query_out, key_out, value_out)]
    grads = exchange(jnp.concatenate(grads, axis=2), ZY)

    def project(att):
        return dot(att, weight, NN).astype(BF16).reshape(2, SPAN, cols)

    own, peer = project(att_own), project(att_peer)
    kept = [lax.dynamic_index_in_dim(x, core, 0, False) for x in (own, peer)]
    gone = jnp.stack([lax.dynamic_index_in_dim(x, 1 - core, 0, False) for x in (own, peer)])
    gone = other_core(gone)
    own = in_order(half == 0, kept[0], kept[1]).reshape(2 * SPAN, cols)
    peer = in_order(half == 0, gone[1], gone[0]).reshape(2 * SPAN, cols)
    projected = side_by_side(first_core, own, peer)

    summed = jnp.sum(term.astype(F32), axis=0).reshape(4, 16, cols)
    chip = 2 * xl + xh
    total = lax.dynamic_index_in_dim(summed, chip, 0, False)
    for step in (1, 2, 3):
        part = lax.dynamic_index_in_dim(summed, chip ^ step, 0, False)
        total = total + lax.ppermute(part, ("xl", "xh"), [(k, k ^ step) for k in range(4)])
    total = total.reshape(2, -1, cols)
    own = lax.dynamic_index_in_dim(total, core, 0, False)
    peer = other_core(lax.dynamic_index_in_dim(total, 1 - core, 0, False))
    weight_gradient = side_by_side(first_core, own, peer)

    peer = other_core(lax.dynamic_slice_in_dim(grads, (1 - core) * HEADS, HEADS, 0))
    own_rows = (2 * SPAN, HEADS * HEAD)
    query_gradient, key_gradient, value_gradient = move(
        final_body, "final", [own_rows] * 3, [core_1, half_1], grads, peer
    )
    return (
        projected[None],
        query_gradient[None],
        key_gradient[None],
        value_gradient[None],
        weight_gradient,
    )


def solution(mesh):
    axes = ("z", "y", "xl", "xh", "core")
    fine = Mesh(mesh.devices.reshape(4, 4, 2, 2, 2), axes)
    rows = P(("xh", "core"), ("z", "y", "xl"), None)
    return jax.shard_map(
        local,
        mesh=fine,
        in_specs=(rows, rows, rows, P(), P(), P(axes, None), rows),
        out_specs=(rows, rows, rows, rows, P(axes, None)),
        check_vma=False,
    )
```

```python
import functools

import jax
import jax.numpy as jnp
from jax import lax
from jax.experimental import pallas as pl
from jax.experimental.pallas import tpu as pltpu
from jax.sharding import Mesh, PartitionSpec as P

HEADS = 8
HEAD = 128
SPAN = 64
UNITS = 16
MANY = 12
ROWS = UNITS * SPAN
TILE = 256
LOW = -1e30
GRANT = 16 << 20
WIDE_GRANT = 32 << 20
SCALE = 1.0 / HEAD
F32 = jnp.float32
BF16 = jnp.bfloat16
NT = (((1,), (1,)), ((), ()))
NN = (((1,), (0,)), ((), ()))
TN = (((0,), (0,)), ((), ()))


def in_hbm(x):
    return pltpu.with_memory_space_constraint(x, pltpu.HBM)


def dot(a, b, dims):
    return lax.dot_general(a, b, dims, preferred_element_type=F32)


def span_hot(first_span):
    span = lax.broadcasted_iota(jnp.int32, (TILE, HEAD), 0) // SPAN + first_span
    lane = lax.broadcasted_iota(jnp.int32, (TILE, HEAD), 1)
    return (span == lane).astype(F32).astype(BF16)


def query_wide(query, first_span):
    return jnp.concatenate([query * BF16(SCALE), span_hot(first_span)], axis=1)


def spread_bias(bias):
    return jnp.broadcast_to(bias[:, None, :], (UNITS, SPAN, HEAD)).reshape(ROWS, HEAD).astype(BF16)


def fill_keys(chunks, bias_ref, ka_ref, first_chunk=0):
    for c, kv_ref in enumerate(chunks):
        rows = pl.ds(c * ROWS, ROWS)
        spans = slice((first_chunk + c) * UNITS, (first_chunk + c + 1) * UNITS)
        ka_ref[rows, :HEAD] = kv_ref[:, :HEAD]
        ka_ref[rows, HEAD:] = spread_bias(bias_ref[spans, :])


def later_in_span():
    key = lax.broadcasted_iota(jnp.int32, (TILE, TILE), 0)
    query = lax.broadcasted_iota(jnp.int32, (TILE, TILE), 1)
    return (key // SPAN == query // SPAN) & (key > query)


def forward_body(first, *refs):
    if first:
        q_ref, kv0, kv1, bias_ref, o_ref, m_ref, l_ref, ka_ref, s_ref = refs
    else:
        q_ref, kv0, kv1, bias_ref, o0_ref, m0_ref, l0_ref, pair_ref, lse_ref, ka_ref, s_ref = refs
    step = pl.program_id(0)
    chunks = (kv0, kv1)

    @pl.when(step == 0)
    def _():
        fill_keys(chunks, bias_ref, ka_ref, 0 if first else 2)

    q = q_ref[...]
    qa = query_wide(q, step * (TILE // SPAN))
    top = None if first else m0_ref[...]
    for c in range(2):
        rows = pl.ds(c * ROWS, ROWS)
        s_ref[rows, :] = dot(ka_ref[rows, :], qa, NT)
        if first and c == 0:
            own = pl.ds(pl.multiple_of(step * TILE, TILE), TILE)
            s_ref[own, :] = jnp.where(later_in_span(), LOW, s_ref[own, :])
        chunk_top = jnp.max(s_ref[rows, :], axis=0, keepdims=True)
        top = chunk_top if top is None else jnp.maximum(top, chunk_top)
    total = jnp.zeros((1, TILE), F32)
    out = jnp.zeros((HEAD, TILE), F32)
    for c, kv_ref in enumerate(chunks):
        weights = jnp.exp(s_ref[pl.ds(c * ROWS, ROWS), :] - top)
        total += jnp.sum(weights, axis=0, keepdims=True)
        out += dot(kv_ref[:, HEAD:], weights.astype(BF16), TN)
    if first:
        o_ref[...] = out
        m_ref[...] = top
        l_ref[...] = total
    else:
        fade = jnp.exp(m0_ref[...] - top)
        total += l0_ref[...] * fade
        out = (out + o0_ref[...] * fade) / total
        pair_ref[:, :HEAD] = q
        pair_ref[:, HEAD:] = out.T.astype(BF16)
        lse_ref[...] = top + jnp.log(total)


def tile_spec(cols):
    return pl.BlockSpec((TILE, cols), lambda i: (i, 0))


def row_spec(rows):
    return pl.BlockSpec((rows, TILE), lambda i: (0, i))


def cost(matmuls, pairs):
    return pl.CostEstimate(
        flops=matmuls * 2 * pairs * 2 * HEAD, bytes_accessed=4 << 20, transcendentals=pairs
    )


def once(*shape):
    return pl.BlockSpec(shape, lambda i: (0,) * len(shape), pipeline_mode=pl.Buffered(1))


def forward(first, q, kvs, bias, *carry):
    stat = jax.ShapeDtypeStruct((1, ROWS), F32)
    if first:
        outs = [pltpu.HBM((HEAD, ROWS), F32), stat, stat]
        out_specs = [row_spec(HEAD), row_spec(1), row_spec(1)]
    else:
        outs = [pltpu.HBM((ROWS, 2 * HEAD), BF16), stat]
        out_specs = [tile_spec(2 * HEAD), row_spec(1)]
    return pl.pallas_call(
        functools.partial(forward_body, first),
        out_shape=outs,
        grid=(ROWS // TILE,),
        in_specs=[
            tile_spec(HEAD),
            *[once(ROWS, 2 * HEAD)] * 2,
            once(4 * UNITS, HEAD),
            *[row_spec(x.shape[0]) for x in carry],
        ],
        out_specs=out_specs,
        scratch_shapes=[
            pltpu.VMEM((2 * ROWS, 2 * HEAD), BF16),
            pltpu.VMEM((2 * ROWS, TILE), F32),
        ],
        cost_estimate=cost(2, 2 * ROWS * ROWS),
        compiler_params=pltpu.CompilerParams(vmem_limit_bytes=GRANT),
        name="forward_near" if first else "forward_far",
    )(q, *kvs, bias, *carry)


def row_delta(g, att):
    return jnp.sum((g.astype(F32) * att.astype(F32)).T, axis=0, keepdims=True)


def query_body(pair_ref, g_ref, lse_ref, far_ref, kv0, kv1, kv2, kv3, bias_ref, dq_ref, ka_ref, s_ref):
    step = pl.program_id(0)
    chunks = (kv0, kv1, kv2, kv3)

    @pl.when(step == 0)
    def _():
        fill_keys(chunks, bias_ref, ka_ref)

    qa = query_wide(pair_ref[:, :HEAD], step * (TILE // SPAN))
    g = g_ref[...]
    lse = lse_ref[...]
    delta = row_delta(g, pair_ref[:, HEAD:])
    own = pl.ds(pl.multiple_of(step * TILE, TILE), TILE)
    s_ref[...] = dot(ka_ref[pl.ds(0, ROWS), :], qa, NT)
    s_ref[own, :] = jnp.where(later_in_span(), LOW, s_ref[own, :])
    total = jnp.zeros((HEAD, TILE), F32)
    for c, kv_ref in enumerate(chunks):
        scores = dot(ka_ref[pl.ds(c * ROWS, ROWS), :], qa, NT) if c else s_ref[...]
        prob = jnp.exp(scores - lse)
        dprob = dot(kv_ref[:, HEAD:], g, NT)
        ds = (prob * (dprob - delta)).astype(BF16)
        total += dot(kv_ref[:, :HEAD], ds, TN)
    dq_ref[...] = (total * SCALE).T.astype(BF16)


def query_grad(pair, g, lse, far, kvs, bias):
    return pl.pallas_call(
        query_body,
        out_shape=jax.ShapeDtypeStruct((ROWS, HEAD), BF16),
        grid=(ROWS // TILE,),
        in_specs=[
            tile_spec(2 * HEAD),
            tile_spec(HEAD),
            row_spec(1),
            pl.BlockSpec(memory_space=pl.ANY),
            *[once(ROWS, 2 * HEAD)] * 4,
            once(4 * UNITS, HEAD),
        ],
        out_specs=tile_spec(HEAD),
        scratch_shapes=[
            pltpu.VMEM((4 * ROWS, 2 * HEAD), BF16),
            pltpu.VMEM((ROWS, TILE), F32),
        ],
        cost_estimate=cost(3, 4 * ROWS * ROWS),
        compiler_params=pltpu.CompilerParams(vmem_limit_bytes=WIDE_GRANT),
        name="query_grad",
    )(pair, g, lse, far, *kvs, bias)


def key_body(*refs):
    kv_ref, bias_ref = refs[:2]
    pairs, gs, lses = refs[2:6], refs[6:10], refs[10]
    dk_ref, dv_ref, ka_ref, s_ref, dk_acc, dv_acc = refs[11:]
    ka_ref[:, :HEAD] = kv_ref[:, :HEAD]
    ka_ref[:, HEAD:] = spread_bias(bias_ref[:UNITS, :])
    dk_acc[...] = jnp.zeros_like(dk_acc)
    dv_acc[...] = jnp.zeros_like(dv_acc)

    def tile(i, _):
        rows = pl.ds(pl.multiple_of(i * TILE, TILE), TILE)
        dk = jnp.zeros((ROWS, HEAD), F32)
        dv = jnp.zeros((ROWS, HEAD), F32)
        for c in range(4):
            q = pairs[c][rows, :HEAD]
            g = gs[c][rows, :]
            lse = lses[c : c + 1, rows]
            delta = row_delta(g, pairs[c][rows, HEAD:])
            qa = query_wide(q, i * (TILE // SPAN) + c * UNITS)
            scores = dot(ka_ref[...], qa, NT)
            if c == 0:
                s_ref[...] = scores
                s_ref[rows, :] = jnp.where(later_in_span(), LOW, s_ref[rows, :])
                scores = s_ref[...]
            prob = jnp.exp(scores - lse)
            dprob = dot(kv_ref[:, HEAD:], g, NT)
            ds = (prob * (dprob - delta)).astype(BF16)
            dv += dot(prob.astype(BF16), g, NN)
            dk += dot(ds, q, NN)
        dk_acc[...] += dk
        dv_acc[...] += dv
        return 0

    lax.fori_loop(0, ROWS // TILE, tile, 0)
    dk_ref[...] = (dk_acc[...] * SCALE).astype(BF16)
    dv_ref[...] = dv_acc[...].astype(BF16)


def key_grad(kv, bias, pairs, gs, lses):
    return pl.pallas_call(
        key_body,
        out_shape=[jax.ShapeDtypeStruct((ROWS, HEAD), BF16)] * 2,
        grid=(1,),
        in_specs=[
            once(ROWS, 2 * HEAD),
            once(4 * UNITS, HEAD),
            *[once(ROWS, 2 * HEAD)] * 4,
            *[once(ROWS, HEAD)] * 4,
            once(4, ROWS),
        ],
        out_specs=[once(ROWS, HEAD)] * 2,
        scratch_shapes=[
            pltpu.VMEM((ROWS, 2 * HEAD), BF16),
            pltpu.VMEM((ROWS, TILE), F32),
            pltpu.VMEM((ROWS, HEAD), F32),
            pltpu.VMEM((ROWS, HEAD), F32),
        ],
        cost_estimate=cost(4, 4 * ROWS * ROWS),
        compiler_params=pltpu.CompilerParams(vmem_limit_bytes=WIDE_GRANT),
        name="key_grad",
    )(kv, bias, *pairs, *gs, lses)


ZY = ("z", "y")
CHIPS = ("z", "y", "xl", "xh")
SWAP = [(0, 1), (1, 0)]


def other_core(x):
    return lax.ppermute(x, "core", SWAP)


def other_chip(x):
    return lax.ppermute(x, "xl", SWAP)


def everyone(x):
    far = other_chip(x)
    return x, other_core(x), far, other_core(far)


def exchange(x, axes):
    return lax.all_to_all(x, axes, 0, 0, tiled=True)


def in_order(first, own, peer):
    return jnp.stack([jnp.where(first, own, peer), jnp.where(first, peer, own)])


def span_bias(span_order, block_mask, xl, core):
    count = span_order.shape[0]
    row = jnp.arange(count, dtype=jnp.int32)
    owner, unit = row // UNITS, row % UNITS
    row_xl = xl ^ (owner // 2)
    half = core ^ (owner % 2) ^ ((unit // 4 + unit % 4) % 2)
    storage = 2 * (2 * unit + row_xl) + half
    held = (storage[:, None] == jnp.arange(count, dtype=jnp.int32)[None, :]).astype(jnp.int32)
    position = jnp.sum(held * span_order[None, :], axis=1)
    hot = (position[:, None] == jnp.arange(count, dtype=jnp.int32)[None, :]).astype(F32)
    pairs = jnp.dot(hot, jnp.dot(block_mask.astype(F32).T, hot.T))
    allowed = (pairs > 0.5) & (position[:, None] <= position[None, :])
    bias = jnp.where(allowed, 0.0, LOW).astype(F32)
    return jnp.pad(bias, ((0, 0), (0, HEAD - count)))


def side_by_side(first, own, peer):
    return jnp.concatenate([jnp.where(first, own, peer), jnp.where(first, peer, own)], axis=-1)


def across(x):
    return lax.ppermute(x, ("xl", "xh"), [(k, k ^ 3) for k in range(4)])


def weight_body(xl_ref, own0, own1, other0, other1, up_ref, out_ref, keep_ref, send_ref, w_ref):
    for flip, pieces in enumerate(((own0, own1), (other0, other1))):
        for units, part in zip((slice(0, MANY), slice(MANY, UNITS)), pieces):
            for c in range(2):
                rows = part[:, c * 32 : (c + 1) * 32, :]
                w_ref[units, xl_ref[0] ^ flip, :, c * 512 : (c + 1) * 512] = rows
    weight = w_ref[...].reshape(1024, 1024)
    out_ref[...] = weight
    for rows, out in ((slice(0, 128), keep_ref), (slice(128, 256), send_ref)):
        out[...] = dot(up_ref[rows, :], weight, NT)


def weight_whole(xl, own, other, up):
    return pl.pallas_call(
        weight_body,
        out_shape=[
            pltpu.HBM((1024, 1024), BF16),
            jax.ShapeDtypeStruct((128, 1024), F32),
            jax.ShapeDtypeStruct((128, 1024), F32),
        ],
        grid=(1,),
        in_specs=[pl.BlockSpec(memory_space=pltpu.SMEM)]
        + [once(*x.shape) for x in (*own, *other, up)],
        out_specs=[once(1024, 1024), once(128, 1024), once(128, 1024)],
        scratch_shapes=[pltpu.VMEM((UNITS, 2, 32, 1024), BF16)],
        cost_estimate=pl.CostEstimate(
            flops=2 * 256 * 1024 * 1024, bytes_accessed=4 << 20, transcendentals=0
        ),
        compiler_params=pltpu.CompilerParams(vmem_limit_bytes=GRANT),
        name="weight_whole",
    )(xl, *own, *other, up)


def term_body(own_ref, peer_ref, up_ref, out_ref):
    att = jnp.concatenate([own_ref[...], peer_ref[...]], axis=0)
    for c in range(2):
        cols = slice(c * 512, (c + 1) * 512)
        out_ref[:, cols] = dot(att, up_ref[:, cols], TN).astype(BF16)


def weight_terms(own, peer, up):
    return pl.pallas_call(
        term_body,
        out_shape=pltpu.HBM((1024, 1024), BF16),
        grid=(1,),
        in_specs=[once(128, 1024), once(128, 1024), once(256, 1024)],
        out_specs=once(1024, 1024),
        cost_estimate=pl.CostEstimate(
            flops=2 * 256 * 1024 * 1024, bytes_accessed=4 << 20, transcendentals=0
        ),
        compiler_params=pltpu.CompilerParams(vmem_limit_bytes=GRANT),
        name="weight_terms",
    )(own, peer, up)


IN_SMEM = pl.BlockSpec(memory_space=pltpu.SMEM)


def move(body, name, outs, scalars, *arrays, space=jax.ShapeDtypeStruct, after=()):
    spaces = space if isinstance(space, list) else [space] * len(outs)
    read = len(scalars) + len(arrays)

    def run(*refs):
        body(*refs[:read], *refs[read + len(after) :])

    return pl.pallas_call(
        run,
        out_shape=[make(shape, BF16) for make, shape in zip(spaces, outs)],
        grid=(1,),
        in_specs=[IN_SMEM] * len(scalars)
        + [once(*x.shape) for x in arrays]
        + [pl.BlockSpec(memory_space=pl.ANY)] * len(after),
        out_specs=[once(*shape) for shape in outs],
        cost_estimate=pl.CostEstimate(flops=0, bytes_accessed=4 << 20, transcendentals=0),
        compiler_params=pltpu.CompilerParams(vmem_limit_bytes=GRANT),
        name=name,
    )(*scalars, *arrays, *after)


def head_cols(h):
    return slice(h * HEAD, (h + 1) * HEAD)


def span_rows(half):
    return pl.ds(pl.multiple_of(half * SPAN, SPAN), SPAN)


def cut_body(half_ref, q_ref, k_ref, v_ref, own_ref, sent_ref):
    for side, out in enumerate((own_ref, sent_ref)):
        rows = span_rows(half_ref[0] ^ side)
        for t, x in enumerate((q_ref, k_ref, v_ref)):
            for h in range(HEADS):
                out[h, :, head_cols(t)] = x[rows, head_cols(h)]


def fill_body(core_ref, xh_ref, own_ref, peer_ref, w0, w1, w2, w3, out_ref):
    core, xh = core_ref[0], xh_ref[0]
    out_ref[pl.ds(core * HEADS, HEADS), :, : 3 * HEAD] = own_ref[...]
    out_ref[pl.ds((1 - core) * HEADS, HEADS), :, : 3 * HEAD] = peer_ref[...]
    first, mine_first = core == 0, xh == 0
    w = [jnp.where(first, x[:, :1024], x[:, 1024:]).astype(F32) for x in (w0, w1, w2, w3)]
    near = [jnp.where(first, w[0], w[1]), jnp.where(first, w[1], w[0])]
    far = [jnp.where(first, w[2], w[3]), jnp.where(first, w[3], w[2])]
    front = [jnp.where(mine_first, a, b) for a, b in zip(near, far)]
    back = [jnp.where(mine_first, b, a) for a, b in zip(near, far)]
    rows = jnp.concatenate(front + back, axis=0).astype(BF16)
    for c in range(2):
        part = rows[:, c * 512 : (c + 1) * 512]
        for unit in range(UNITS):
            out_ref[unit, c * 32 : (c + 1) * 32, 3 * HEAD :] = part


def up_body(core_ref, half_ref, own_ref, peer_ref, out_ref):
    core, half = core_ref[0], half_ref[0]
    for side in range(2):
        rows = span_rows(half ^ side)
        wide = own_ref[rows, :]
        mine = jnp.where(core == 0, wide[:, :1024], wide[:, 1024:])
        out_ref[span_rows(2 * side + core), :] = mine
        out_ref[span_rows(2 * side + 1 - core), :] = peer_ref[rows, :]


def split_body(x_ref, q_ref, kv_ref, w0_ref, w1_ref):
    x = x_ref[...]
    q_ref[...] = x[:, :, :HEAD].reshape(ROWS, HEAD)
    kv_ref[...] = x[:, :, HEAD : 3 * HEAD].reshape(ROWS, 2 * HEAD)
    w0_ref[...] = x[:MANY, :, 3 * HEAD :]
    w1_ref[...] = x[MANY:, :, 3 * HEAD :]


def cross_body(pair_ref, own_ref, peer_ref, out_ref):
    for s in range(2):
        for h in range(HEADS):
            unit, rows = s * HEADS + h, slice(s * SPAN, (s + 1) * SPAN)
            out_ref[unit, :, :HEAD] = pair_ref[unit * SPAN : (unit + 1) * SPAN, HEAD:]
            total = own_ref[rows, head_cols(h)] + peer_ref[rows, head_cols(h)]
            out_ref[unit, :, HEAD:] = total.astype(BF16)


def land_body(x_ref, att_ref, g_ref):
    g_ref[...] = x_ref[:, :, HEAD:].reshape(ROWS, HEAD)
    for s in range(2):
        for h in range(HEADS):
            att_ref[s * SPAN : (s + 1) * SPAN, head_cols(h)] = x_ref[s * HEADS + h, :, :HEAD]


def final_body(core_ref, half_ref, own_ref, peer_ref, dq_ref, dk_ref, dv_ref):
    core, half = core_ref[0], half_ref[0]
    for t, out in enumerate((dq_ref, dk_ref, dv_ref)):
        for h in range(HEADS):
            out[span_rows(half), head_cols(h)] = own_ref[core * HEADS + h, :, head_cols(t)]
            out[span_rows(1 - half), head_cols(h)] = peer_ref[h, :, head_cols(t)]


def local(query_states, key_states, value_states, span_order, block_mask, output_weight, upstream):
    z, y, xl, xh, core = (lax.axis_index(a) for a in ("z", "y", "xl", "xh", "core"))
    first_core = core == 0
    half = core ^ ((z + y) % 2)
    core_1, xl_1, xh_1, half_1 = (x.reshape(1) for x in (core, xl, xh, half))
    cols = output_weight.shape[1] // 2

    bias = span_bias(span_order, block_mask, xl, core)
    wide = upstream[0]
    up_sent = jnp.where(first_core, wide[:, cols:], wide[:, :cols])
    (up,) = move(
        up_body,
        "up",
        [(4 * SPAN, cols)],
        [core_1, half_1],
        in_hbm(wide),
        other_core(up_sent),
        space=pltpu.HBM,
    )

    weight_far = lax.ppermute(output_weight, "xh", SWAP)
    weight_rows = [output_weight, other_core(output_weight), weight_far, other_core(weight_far)]
    unit_rows = (HEADS, SPAN, 3 * HEAD)
    own, sent = move(
        cut_body,
        "cut",
        [unit_rows] * 2,
        [half_1],
        in_hbm(query_states[0]),
        in_hbm(key_states[0]),
        in_hbm(value_states[0]),
        space=pltpu.HBM,
    )
    (blocks,) = move(
        fill_body,
        "fill",
        [(UNITS, SPAN, 3 * HEAD + 512)],
        [core_1, xh_1],
        in_hbm(own),
        other_core(sent),
        *weight_rows,
        after=(in_hbm(up), bias),
    )
    blocks = exchange(blocks, ZY)
    q, own_kv, *weight_own = move(
        split_body,
        "split",
        [(ROWS, HEAD), (ROWS, 2 * HEAD), (MANY, SPAN, 512), (UNITS - MANY, SPAN, 512)],
        [],
        blocks,
        space=pltpu.HBM,
    )
    far_kv = other_chip(own_kv)
    weight_other = [across(weight_own[0]), other_chip(weight_own[1])]
    near_kv = other_core(own_kv)
    out, top, total = forward(True, in_hbm(q), (in_hbm(own_kv), near_kv), bias)
    far_kv, total = lax.optimization_barrier((far_kv, total))
    kvs = (own_kv, near_kv, far_kv, other_core(far_kv))
    pair, lse = forward(False, in_hbm(q), kvs[2:], bias, in_hbm(out), top, total)
    lses = jnp.concatenate([lse, other_core(lse)], axis=0)
    lses = jnp.concatenate([lses, other_chip(lses)], axis=0)

    place, lse = lax.optimization_barrier((xl_1, lse))
    weight, grad_own, grad_sent = weight_whole(
        place, [in_hbm(x) for x in weight_own], weight_other, in_hbm(up)
    )
    (crossing,) = move(
        cross_body,
        "cross",
        [(UNITS, SPAN, 2 * HEAD)],
        [],
        in_hbm(pair),
        grad_own,
        other_core(grad_sent),
    )
    crossed = exchange(crossing, ZY)
    pair_sent, lses = lax.optimization_barrier((pair, lses))
    pairs = everyone(pair_sent)

    att_own, g = move(
        land_body,
        "land",
        [(2 * SPAN, HEADS * HEAD), (ROWS, HEAD)],
        [],
        crossed,
        after=(lses,),
        space=[jax.ShapeDtypeStruct, pltpu.HBM],
    )
    gs = everyone(g)
    att_peer = other_core(att_own)
    term = weight_terms(att_own, att_peer, in_hbm(up)).reshape(UNITS, SPAN, cols)
    term = exchange(term, ZY)

    query_out = query_grad(in_hbm(pair), in_hbm(g), lse, pairs[2], [in_hbm(x) for x in kvs], bias)
    key_out, value_out = key_grad(in_hbm(own_kv), bias, pairs, gs, lses)
    grads = [x.reshape(UNITS, SPAN, HEAD) for x in (query_out, key_out, value_out)]
    grads = exchange(jnp.concatenate(grads, axis=2), ZY)

    def project(att):
        return dot(att, weight, NN).astype(BF16).reshape(2, SPAN, cols)

    own, peer = project(att_own), project(att_peer)
    kept = [lax.dynamic_index_in_dim(x, core, 0, False) for x in (own, peer)]
    gone = jnp.stack([lax.dynamic_index_in_dim(x, 1 - core, 0, False) for x in (own, peer)])
    gone = other_core(gone)
    own = in_order(half == 0, kept[0], kept[1]).reshape(2 * SPAN, cols)
    peer = in_order(half == 0, gone[1], gone[0]).reshape(2 * SPAN, cols)
    projected = side_by_side(first_core, own, peer)

    summed = jnp.sum(term.astype(F32), axis=0).reshape(4, 16, cols)
    chip = 2 * xl + xh
    total = lax.dynamic_index_in_dim(summed, chip, 0, False)
    for step in (1, 2, 3):
        part = lax.dynamic_index_in_dim(summed, chip ^ step, 0, False)
        total = total + lax.ppermute(part, ("xl", "xh"), [(k, k ^ step) for k in range(4)])
    total = total.reshape(2, -1, cols)
    own = lax.dynamic_index_in_dim(total, core, 0, False)
    peer = other_core(lax.dynamic_index_in_dim(total, 1 - core, 0, False))
    weight_gradient = side_by_side(first_core, own, peer)

    peer = other_core(lax.dynamic_slice_in_dim(grads, (1 - core) * HEADS, HEADS, 0))
    own_rows = (2 * SPAN, HEADS * HEAD)
    query_gradient, key_gradient, value_gradient = move(
        final_body, "final", [own_rows] * 3, [core_1, half_1], grads, peer
    )
    return (
        projected[None],
        query_gradient[None],
        key_gradient[None],
        value_gradient[None],
        weight_gradient,
    )


def solution(mesh):
    axes = ("z", "y", "xl", "xh", "core")
    fine = Mesh(mesh.devices.reshape(4, 4, 2, 2, 2), axes)
    rows = P(("xh", "core"), ("z", "y", "xl"), None)
    return jax.shard_map(
        local,
        mesh=fine,
        in_specs=(rows, rows, rows, P(), P(), P(axes, None), rows),
        out_specs=(rows, rows, rows, rows, P(axes, None)),
        check_vma=False,
    )
```

```python
import functools

import jax
import jax.numpy as jnp
from jax import lax
from jax.experimental import pallas as pl
from jax.experimental.pallas import tpu as pltpu
from jax.sharding import Mesh, PartitionSpec as P

HEADS = 8
HEAD = 128
SPAN = 64
UNITS = 16
MANY = 12
ROWS = UNITS * SPAN
TILE = 256
LOW = -1e30
GRANT = 16 << 20
WIDE_GRANT = 32 << 20
SCALE = 1.0 / HEAD
F32 = jnp.float32
BF16 = jnp.bfloat16
NT = (((1,), (1,)), ((), ()))
NN = (((1,), (0,)), ((), ()))
TN = (((0,), (0,)), ((), ()))


def in_hbm(x):
    return pltpu.with_memory_space_constraint(x, pltpu.HBM)


def dot(a, b, dims):
    return lax.dot_general(a, b, dims, preferred_element_type=F32)


def span_hot(first_span):
    span = lax.broadcasted_iota(jnp.int32, (TILE, HEAD), 0) // SPAN + first_span
    lane = lax.broadcasted_iota(jnp.int32, (TILE, HEAD), 1)
    return (span == lane).astype(F32).astype(BF16)


def query_wide(query, first_span):
    return jnp.concatenate([query * BF16(SCALE), span_hot(first_span)], axis=1)


def spread_bias(bias):
    return jnp.broadcast_to(bias[:, None, :], (UNITS, SPAN, HEAD)).reshape(ROWS, HEAD).astype(BF16)


def fill_keys(chunks, bias_ref, ka_ref, first_chunk=0):
    for c, kv_ref in enumerate(chunks):
        rows = pl.ds(c * ROWS, ROWS)
        spans = slice((first_chunk + c) * UNITS, (first_chunk + c + 1) * UNITS)
        ka_ref[rows, :HEAD] = kv_ref[:, :HEAD]
        ka_ref[rows, HEAD:] = spread_bias(bias_ref[spans, :])


def later_in_span():
    key = lax.broadcasted_iota(jnp.int32, (TILE, TILE), 0)
    query = lax.broadcasted_iota(jnp.int32, (TILE, TILE), 1)
    return (key // SPAN == query // SPAN) & (key > query)


def forward_body(first, *refs):
    if first:
        q_ref, kv0, kv1, bias_ref, o_ref, m_ref, l_ref, ka_ref, s_ref = refs
    else:
        q_ref, kv0, kv1, bias_ref, o0_ref, m0_ref, l0_ref, pair_ref, lse_ref, ka_ref, s_ref = refs
    step = pl.program_id(0)
    chunks = (kv0, kv1)

    @pl.when(step == 0)
    def _():
        fill_keys(chunks, bias_ref, ka_ref, 0 if first else 2)

    q = q_ref[...]
    qa = query_wide(q, step * (TILE // SPAN))
    top = None if first else m0_ref[...]
    for c in range(2):
        rows = pl.ds(c * ROWS, ROWS)
        s_ref[rows, :] = dot(ka_ref[rows, :], qa, NT)
        if first and c == 0:
            own = pl.ds(pl.multiple_of(step * TILE, TILE), TILE)
            s_ref[own, :] = jnp.where(later_in_span(), LOW, s_ref[own, :])
        chunk_top = jnp.max(s_ref[rows, :], axis=0, keepdims=True)
        top = chunk_top if top is None else jnp.maximum(top, chunk_top)
    total = jnp.zeros((1, TILE), F32)
    out = jnp.zeros((HEAD, TILE), F32)
    for c, kv_ref in enumerate(chunks):
        weights = jnp.exp(s_ref[pl.ds(c * ROWS, ROWS), :] - top)
        total += jnp.sum(weights, axis=0, keepdims=True)
        out += dot(kv_ref[:, HEAD:], weights.astype(BF16), TN)
    if first:
        o_ref[...] = out
        m_ref[...] = top
        l_ref[...] = total
    else:
        fade = jnp.exp(m0_ref[...] - top)
        total += l0_ref[...] * fade
        out = (out + o0_ref[...] * fade) / total
        pair_ref[:, :HEAD] = q
        pair_ref[:, HEAD:] = out.T.astype(BF16)
        lse_ref[...] = top + jnp.log(total)


def tile_spec(cols):
    return pl.BlockSpec((TILE, cols), lambda i: (i, 0))


def row_spec(rows):
    return pl.BlockSpec((rows, TILE), lambda i: (0, i))


def cost(matmuls, pairs):
    return pl.CostEstimate(
        flops=matmuls * 2 * pairs * 2 * HEAD, bytes_accessed=4 << 20, transcendentals=pairs
    )


def once(*shape):
    return pl.BlockSpec(shape, lambda i: (0,) * len(shape), pipeline_mode=pl.Buffered(1))


def forward(first, q, kvs, bias, *carry):
    stat = jax.ShapeDtypeStruct((1, ROWS), F32)
    if first:
        outs = [pltpu.HBM((HEAD, ROWS), F32), stat, stat]
        out_specs = [row_spec(HEAD), row_spec(1), row_spec(1)]
    else:
        outs = [pltpu.HBM((ROWS, 2 * HEAD), BF16), stat]
        out_specs = [tile_spec(2 * HEAD), row_spec(1)]
    return pl.pallas_call(
        functools.partial(forward_body, first),
        out_shape=outs,
        grid=(ROWS // TILE,),
        in_specs=[
            tile_spec(HEAD),
            *[once(ROWS, 2 * HEAD)] * 2,
            once(4 * UNITS, HEAD),
            *[row_spec(x.shape[0]) for x in carry],
        ],
        out_specs=out_specs,
        scratch_shapes=[
            pltpu.VMEM((2 * ROWS, 2 * HEAD), BF16),
            pltpu.VMEM((2 * ROWS, TILE), F32),
        ],
        cost_estimate=cost(2, 2 * ROWS * ROWS),
        compiler_params=pltpu.CompilerParams(vmem_limit_bytes=GRANT),
        name="forward_near" if first else "forward_far",
    )(q, *kvs, bias, *carry)


def row_delta(g, att):
    return jnp.sum((g.astype(F32) * att.astype(F32)).T, axis=0, keepdims=True)


def query_body(pair_ref, g_ref, lse_ref, far_ref, kv0, kv1, kv2, kv3, bias_ref, dq_ref, ka_ref, s_ref):
    step = pl.program_id(0)
    chunks = (kv0, kv1, kv2, kv3)

    @pl.when(step == 0)
    def _():
        fill_keys(chunks, bias_ref, ka_ref)

    qa = query_wide(pair_ref[:, :HEAD], step * (TILE // SPAN))
    g = g_ref[...]
    lse = lse_ref[...]
    delta = row_delta(g, pair_ref[:, HEAD:])
    own = pl.ds(pl.multiple_of(step * TILE, TILE), TILE)
    s_ref[...] = dot(ka_ref[pl.ds(0, ROWS), :], qa, NT)
    s_ref[own, :] = jnp.where(later_in_span(), LOW, s_ref[own, :])
    total = jnp.zeros((HEAD, TILE), F32)
    for c, kv_ref in enumerate(chunks):
        scores = dot(ka_ref[pl.ds(c * ROWS, ROWS), :], qa, NT) if c else s_ref[...]
        prob = jnp.exp(scores - lse)
        dprob = dot(kv_ref[:, HEAD:], g, NT)
        ds = (prob * (dprob - delta)).astype(BF16)
        total += dot(kv_ref[:, :HEAD], ds, TN)
    dq_ref[...] = (total * SCALE).T.astype(BF16)


def query_grad(pair, g, lse, far, kvs, bias):
    return pl.pallas_call(
        query_body,
        out_shape=jax.ShapeDtypeStruct((ROWS, HEAD), BF16),
        grid=(ROWS // TILE,),
        in_specs=[
            tile_spec(2 * HEAD),
            tile_spec(HEAD),
            row_spec(1),
            pl.BlockSpec(memory_space=pl.ANY),
            *[once(ROWS, 2 * HEAD)] * 4,
            once(4 * UNITS, HEAD),
        ],
        out_specs=tile_spec(HEAD),
        scratch_shapes=[
            pltpu.VMEM((4 * ROWS, 2 * HEAD), BF16),
            pltpu.VMEM((ROWS, TILE), F32),
        ],
        cost_estimate=cost(3, 4 * ROWS * ROWS),
        compiler_params=pltpu.CompilerParams(vmem_limit_bytes=WIDE_GRANT),
        name="query_grad",
    )(pair, g, lse, far, *kvs, bias)


def key_body(*refs):
    kv_ref, bias_ref = refs[:2]
    pairs, gs, lses = refs[2:6], refs[6:10], refs[10]
    dk_ref, dv_ref, ka_ref, s_ref, dk_acc, dv_acc = refs[11:]
    ka_ref[:, :HEAD] = kv_ref[:, :HEAD]
    ka_ref[:, HEAD:] = spread_bias(bias_ref[:UNITS, :])
    dk_acc[...] = jnp.zeros_like(dk_acc)
    dv_acc[...] = jnp.zeros_like(dv_acc)

    def tile(i, _):
        rows = pl.ds(pl.multiple_of(i * TILE, TILE), TILE)
        dk = jnp.zeros((ROWS, HEAD), F32)
        dv = jnp.zeros((ROWS, HEAD), F32)
        for c in range(4):
            q = pairs[c][rows, :HEAD]
            g = gs[c][rows, :]
            lse = lses[c : c + 1, rows]
            delta = row_delta(g, pairs[c][rows, HEAD:])
            qa = query_wide(q, i * (TILE // SPAN) + c * UNITS)
            scores = dot(ka_ref[...], qa, NT)
            if c == 0:
                s_ref[...] = scores
                s_ref[rows, :] = jnp.where(later_in_span(), LOW, s_ref[rows, :])
                scores = s_ref[...]
            prob = jnp.exp(scores - lse)
            dprob = dot(kv_ref[:, HEAD:], g, NT)
            ds = (prob * (dprob - delta)).astype(BF16)
            dv += dot(prob.astype(BF16), g, NN)
            dk += dot(ds, q, NN)
        dk_acc[...] += dk
        dv_acc[...] += dv
        return 0

    lax.fori_loop(0, ROWS // TILE, tile, 0)
    dk_ref[...] = (dk_acc[...] * SCALE).astype(BF16)
    dv_ref[...] = dv_acc[...].astype(BF16)


def key_grad(kv, bias, pairs, gs, lses):
    return pl.pallas_call(
        key_body,
        out_shape=[jax.ShapeDtypeStruct((ROWS, HEAD), BF16)] * 2,
        grid=(1,),
        in_specs=[
            once(ROWS, 2 * HEAD),
            once(4 * UNITS, HEAD),
            *[once(ROWS, 2 * HEAD)] * 4,
            *[once(ROWS, HEAD)] * 4,
            once(4, ROWS),
        ],
        out_specs=[once(ROWS, HEAD)] * 2,
        scratch_shapes=[
            pltpu.VMEM((ROWS, 2 * HEAD), BF16),
            pltpu.VMEM((ROWS, TILE), F32),
            pltpu.VMEM((ROWS, HEAD), F32),
            pltpu.VMEM((ROWS, HEAD), F32),
        ],
        cost_estimate=cost(4, 4 * ROWS * ROWS),
        compiler_params=pltpu.CompilerParams(vmem_limit_bytes=WIDE_GRANT),
        name="key_grad",
    )(kv, bias, *pairs, *gs, lses)


ZY = ("z", "y")
CHIPS = ("z", "y", "xl", "xh")
SWAP = [(0, 1), (1, 0)]


def other_core(x):
    return lax.ppermute(x, "core", SWAP)


def other_chip(x):
    return lax.ppermute(x, "xl", SWAP)


def everyone(x):
    far = other_chip(x)
    return x, other_core(x), far, other_core(far)


def exchange(x, axes):
    return lax.all_to_all(x, axes, 0, 0, tiled=True)


def in_order(first, own, peer):
    return jnp.stack([jnp.where(first, own, peer), jnp.where(first, peer, own)])


def span_bias(span_order, block_mask, xl, core):
    count = span_order.shape[0]
    row = jnp.arange(count, dtype=jnp.int32)
    owner, unit = row // UNITS, row % UNITS
    row_xl = xl ^ (owner // 2)
    half = core ^ (owner % 2) ^ ((unit // 4 + unit % 4) % 2)
    storage = 2 * (2 * unit + row_xl) + half
    held = (storage[:, None] == jnp.arange(count, dtype=jnp.int32)[None, :]).astype(jnp.int32)
    position = jnp.sum(held * span_order[None, :], axis=1)
    hot = (position[:, None] == jnp.arange(count, dtype=jnp.int32)[None, :]).astype(F32)
    pairs = jnp.dot(hot, jnp.dot(block_mask.astype(F32).T, hot.T))
    allowed = (pairs > 0.5) & (position[:, None] <= position[None, :])
    bias = jnp.where(allowed, 0.0, LOW).astype(F32)
    return jnp.pad(bias, ((0, 0), (0, HEAD - count)))


def side_by_side(first, own, peer):
    return jnp.concatenate([jnp.where(first, own, peer), jnp.where(first, peer, own)], axis=-1)


def across(x):
    return lax.ppermute(x, ("xl", "xh"), [(k, k ^ 3) for k in range(4)])


def weight_body(xl_ref, own0, own1, other0, other1, up_ref, out_ref, keep_ref, send_ref, w_ref):
    for flip, pieces in enumerate(((own0, own1), (other0, other1))):
        for units, part in zip((slice(0, MANY), slice(MANY, UNITS)), pieces):
            for c in range(2):
                rows = part[:, c * 32 : (c + 1) * 32, :]
                w_ref[units, xl_ref[0] ^ flip, :, c * 512 : (c + 1) * 512] = rows
    weight = w_ref[...].reshape(1024, 1024)
    out_ref[...] = weight
    for rows, out in ((slice(0, 128), keep_ref), (slice(128, 256), send_ref)):
        out[...] = dot(up_ref[rows, :], weight, NT)


def weight_whole(xl, own, other, up):
    return pl.pallas_call(
        weight_body,
        out_shape=[
            pltpu.HBM((1024, 1024), BF16),
            jax.ShapeDtypeStruct((128, 1024), F32),
            jax.ShapeDtypeStruct((128, 1024), F32),
        ],
        grid=(1,),
        in_specs=[pl.BlockSpec(memory_space=pltpu.SMEM)]
        + [once(*x.shape) for x in (*own, *other, up)],
        out_specs=[once(1024, 1024), once(128, 1024), once(128, 1024)],
        scratch_shapes=[pltpu.VMEM((UNITS, 2, 32, 1024), BF16)],
        cost_estimate=pl.CostEstimate(
            flops=2 * 256 * 1024 * 1024, bytes_accessed=4 << 20, transcendentals=0
        ),
        compiler_params=pltpu.CompilerParams(vmem_limit_bytes=GRANT),
        name="weight_whole",
    )(xl, *own, *other, up)


def term_body(own_ref, peer_ref, up_ref, out_ref):
    att = jnp.concatenate([own_ref[...], peer_ref[...]], axis=0)
    for c in range(2):
        cols = slice(c * 512, (c + 1) * 512)
        out_ref[:, cols] = dot(att, up_ref[:, cols], TN).astype(BF16)


def weight_terms(own, peer, up):
    return pl.pallas_call(
        term_body,
        out_shape=pltpu.HBM((1024, 1024), BF16),
        grid=(1,),
        in_specs=[once(128, 1024), once(128, 1024), once(256, 1024)],
        out_specs=once(1024, 1024),
        cost_estimate=pl.CostEstimate(
            flops=2 * 256 * 1024 * 1024, bytes_accessed=4 << 20, transcendentals=0
        ),
        compiler_params=pltpu.CompilerParams(vmem_limit_bytes=GRANT),
        name="weight_terms",
    )(own, peer, up)


IN_SMEM = pl.BlockSpec(memory_space=pltpu.SMEM)


def move(body, name, outs, scalars, *arrays, space=jax.ShapeDtypeStruct, after=()):
    spaces = space if isinstance(space, list) else [space] * len(outs)
    read = len(scalars) + len(arrays)

    def run(*refs):
        body(*refs[:read], *refs[read + len(after) :])

    return pl.pallas_call(
        run,
        out_shape=[make(shape, BF16) for make, shape in zip(spaces, outs)],
        grid=(1,),
        in_specs=[IN_SMEM] * len(scalars)
        + [once(*x.shape) for x in arrays]
        + [pl.BlockSpec(memory_space=pl.ANY)] * len(after),
        out_specs=[once(*shape) for shape in outs],
        cost_estimate=pl.CostEstimate(flops=0, bytes_accessed=4 << 20, transcendentals=0),
        compiler_params=pltpu.CompilerParams(vmem_limit_bytes=GRANT),
        name=name,
    )(*scalars, *arrays, *after)


def head_cols(h):
    return slice(h * HEAD, (h + 1) * HEAD)


def span_rows(half):
    return pl.ds(pl.multiple_of(half * SPAN, SPAN), SPAN)


def cut_body(half_ref, q_ref, k_ref, v_ref, own_ref, sent_ref):
    for side, out in enumerate((own_ref, sent_ref)):
        rows = span_rows(half_ref[0] ^ side)
        for t, x in enumerate((q_ref, k_ref, v_ref)):
            for h in range(HEADS):
                out[h, :, head_cols(t)] = x[rows, head_cols(h)]


def fill_body(core_ref, xh_ref, own_ref, peer_ref, w0, w1, w2, w3, out_ref):
    core, xh = core_ref[0], xh_ref[0]
    out_ref[pl.ds(core * HEADS, HEADS), :, : 3 * HEAD] = own_ref[...]
    out_ref[pl.ds((1 - core) * HEADS, HEADS), :, : 3 * HEAD] = peer_ref[...]
    first, mine_first = core == 0, xh == 0
    w = [jnp.where(first, x[:, :1024], x[:, 1024:]).astype(F32) for x in (w0, w1, w2, w3)]
    near = [jnp.where(first, w[0], w[1]), jnp.where(first, w[1], w[0])]
    far = [jnp.where(first, w[2], w[3]), jnp.where(first, w[3], w[2])]
    front = [jnp.where(mine_first, a, b) for a, b in zip(near, far)]
    back = [jnp.where(mine_first, b, a) for a, b in zip(near, far)]
    rows = jnp.concatenate(front + back, axis=0).astype(BF16)
    for c in range(2):
        part = rows[:, c * 512 : (c + 1) * 512]
        for unit in range(UNITS):
            out_ref[unit, c * 32 : (c + 1) * 32, 3 * HEAD :] = part


def up_body(core_ref, half_ref, own_ref, peer_ref, out_ref):
    core, half = core_ref[0], half_ref[0]
    for side in range(2):
        rows = span_rows(half ^ side)
        wide = own_ref[rows, :]
        mine = jnp.where(core == 0, wide[:, :1024], wide[:, 1024:])
        out_ref[span_rows(2 * side + core), :] = mine
        out_ref[span_rows(2 * side + 1 - core), :] = peer_ref[rows, :]


def split_body(x_ref, q_ref, kv_ref, w0_ref, w1_ref):
    x = x_ref[...]
    q_ref[...] = x[:, :, :HEAD].reshape(ROWS, HEAD)
    kv_ref[...] = x[:, :, HEAD : 3 * HEAD].reshape(ROWS, 2 * HEAD)
    w0_ref[...] = x[:MANY, :, 3 * HEAD :]
    w1_ref[...] = x[MANY:, :, 3 * HEAD :]


def cross_body(pair_ref, own_ref, peer_ref, out_ref):
    for s in range(2):
        for h in range(HEADS):
            unit, rows = s * HEADS + h, slice(s * SPAN, (s + 1) * SPAN)
            out_ref[unit, :, :HEAD] = pair_ref[unit * SPAN : (unit + 1) * SPAN, HEAD:]
            total = own_ref[rows, head_cols(h)] + peer_ref[rows, head_cols(h)]
            out_ref[unit, :, HEAD:] = total.astype(BF16)


def land_body(x_ref, att_ref, g_ref):
    g_ref[...] = x_ref[:, :, HEAD:].reshape(ROWS, HEAD)
    for s in range(2):
        for h in range(HEADS):
            att_ref[s * SPAN : (s + 1) * SPAN, head_cols(h)] = x_ref[s * HEADS + h, :, :HEAD]


def final_body(core_ref, half_ref, own_ref, peer_ref, dq_ref, dk_ref, dv_ref):
    core, half = core_ref[0], half_ref[0]
    for t, out in enumerate((dq_ref, dk_ref, dv_ref)):
        for h in range(HEADS):
            out[span_rows(half), head_cols(h)] = own_ref[core * HEADS + h, :, head_cols(t)]
            out[span_rows(1 - half), head_cols(h)] = peer_ref[h, :, head_cols(t)]


def local(query_states, key_states, value_states, span_order, block_mask, output_weight, upstream):
    z, y, xl, xh, core = (lax.axis_index(a) for a in ("z", "y", "xl", "xh", "core"))
    first_core = core == 0
    half = core ^ ((z + y) % 2)
    core_1, xl_1, xh_1, half_1 = (x.reshape(1) for x in (core, xl, xh, half))
    cols = output_weight.shape[1] // 2

    weight_far = lax.ppermute(output_weight, "xh", SWAP)
    weight_rows = [output_weight, other_core(output_weight), weight_far, other_core(weight_far)]
    unit_rows = (HEADS, SPAN, 3 * HEAD)
    own, sent = move(
        cut_body,
        "cut",
        [unit_rows] * 2,
        [half_1],
        in_hbm(query_states[0]),
        in_hbm(key_states[0]),
        in_hbm(value_states[0]),
        space=pltpu.HBM,
    )
    (blocks,) = move(
        fill_body,
        "fill",
        [(UNITS, SPAN, 3 * HEAD + 512)],
        [core_1, xh_1],
        in_hbm(own),
        other_core(sent),
        *weight_rows,
    )
    blocks = exchange(blocks, ZY)
    q, own_kv, *weight_own = move(
        split_body,
        "split",
        [(ROWS, HEAD), (ROWS, 2 * HEAD), (MANY, SPAN, 512), (UNITS - MANY, SPAN, 512)],
        [],
        blocks,
        space=pltpu.HBM,
    )
    far_kv = other_chip(own_kv)
    weight_other = [across(weight_own[0]), other_chip(weight_own[1])]
    near_kv = other_core(own_kv)
    own_kv, span_order, wide = lax.optimization_barrier((own_kv, span_order, upstream[0]))
    bias = span_bias(span_order, block_mask, xl, core)

    up_sent = jnp.where(first_core, wide[:, cols:], wide[:, :cols])
    (up,) = move(
        up_body,
        "up",
        [(4 * SPAN, cols)],
        [core_1, half_1],
        in_hbm(wide),
        other_core(up_sent),
        space=pltpu.HBM,
    )

    out, top, total = forward(True, in_hbm(q), (in_hbm(own_kv), near_kv), bias)
    far_kv, total = lax.optimization_barrier((far_kv, total))
    kvs = (own_kv, near_kv, far_kv, other_core(far_kv))
    pair, lse = forward(False, in_hbm(q), kvs[2:], bias, in_hbm(out), top, total)
    lses = jnp.concatenate([lse, other_core(lse)], axis=0)
    lses = jnp.concatenate([lses, other_chip(lses)], axis=0)

    place, lse = lax.optimization_barrier((xl_1, lse))
    weight, grad_own, grad_sent = weight_whole(
        place, [in_hbm(x) for x in weight_own], weight_other, in_hbm(up)
    )
    (crossing,) = move(
        cross_body,
        "cross",
        [(UNITS, SPAN, 2 * HEAD)],
        [],
        in_hbm(pair),
        grad_own,
        other_core(grad_sent),
    )
    crossed = exchange(crossing, ZY)
    pair_sent, lses = lax.optimization_barrier((pair, lses))
    pair_far = other_chip(pair_sent)

    att_own, g = move(
        land_body,
        "land",
        [(2 * SPAN, HEADS * HEAD), (ROWS, HEAD)],
        [],
        crossed,
        after=(lses,),
        space=[jax.ShapeDtypeStruct, pltpu.HBM],
    )
    gs = everyone(g)
    att_peer = other_core(att_own)
    term = weight_terms(att_own, att_peer, in_hbm(up)).reshape(UNITS, SPAN, cols)
    term = exchange(term, ZY)
    att_peer, pair_far = lax.optimization_barrier((att_peer, pair_far))
    pairs = (pair_sent, other_core(pair_sent), pair_far, other_core(pair_far))

    query_out = query_grad(in_hbm(pair), in_hbm(g), lse, pairs[2], [in_hbm(x) for x in kvs], bias)
    key_out, value_out = key_grad(in_hbm(own_kv), bias, pairs, gs, lses)
    grads = [x.reshape(UNITS, SPAN, HEAD) for x in (query_out, key_out, value_out)]
    grads = exchange(jnp.concatenate(grads, axis=2), ZY)

    def project(att):
        return dot(att, weight, NN).astype(BF16).reshape(2, SPAN, cols)

    own, peer = project(att_own), project(att_peer)
    kept = [lax.dynamic_index_in_dim(x, core, 0, False) for x in (own, peer)]
    gone = jnp.stack([lax.dynamic_index_in_dim(x, 1 - core, 0, False) for x in (own, peer)])
    gone = other_core(gone)
    own = in_order(half == 0, kept[0], kept[1]).reshape(2 * SPAN, cols)
    peer = in_order(half == 0, gone[1], gone[0]).reshape(2 * SPAN, cols)
    projected = side_by_side(first_core, own, peer)

    summed = jnp.sum(term.astype(F32), axis=0).reshape(4, 16, cols)
    chip = 2 * xl + xh
    total = lax.dynamic_index_in_dim(summed, chip, 0, False)
    for step in (1, 2, 3):
        part = lax.dynamic_index_in_dim(summed, chip ^ step, 0, False)
        total = total + lax.ppermute(part, ("xl", "xh"), [(k, k ^ step) for k in range(4)])
    total = total.reshape(2, -1, cols)
    own = lax.dynamic_index_in_dim(total, core, 0, False)
    peer = other_core(lax.dynamic_index_in_dim(total, 1 - core, 0, False))
    weight_gradient = side_by_side(first_core, own, peer)

    peer = other_core(lax.dynamic_slice_in_dim(grads, (1 - core) * HEADS, HEADS, 0))
    own_rows = (2 * SPAN, HEADS * HEAD)
    query_gradient, key_gradient, value_gradient = move(
        final_body, "final", [own_rows] * 3, [core_1, half_1], grads, peer
    )
    return (
        projected[None],
        query_gradient[None],
        key_gradient[None],
        value_gradient[None],
        weight_gradient,
    )


def solution(mesh):
    axes = ("z", "y", "xl", "xh", "core")
    fine = Mesh(mesh.devices.reshape(4, 4, 2, 2, 2), axes)
    rows = P(("xh", "core"), ("z", "y", "xl"), None)
    return jax.shard_map(
        local,
        mesh=fine,
        in_specs=(rows, rows, rows, P(), P(), P(axes, None), rows),
        out_specs=(rows, rows, rows, rows, P(axes, None)),
        check_vma=False,
    )
```

```python
import functools

import jax
import jax.numpy as jnp
from jax import lax
from jax.experimental import pallas as pl
from jax.experimental.pallas import tpu as pltpu
from jax.sharding import Mesh, PartitionSpec as P

HEADS = 8
HEAD = 128
SPAN = 64
UNITS = 16
MANY = 12
ROWS = UNITS * SPAN
TILE = 256
LOW = -1e30
GRANT = 16 << 20
WIDE_GRANT = 32 << 20
SCALE = 1.0 / HEAD
F32 = jnp.float32
BF16 = jnp.bfloat16
NT = (((1,), (1,)), ((), ()))
NN = (((1,), (0,)), ((), ()))
TN = (((0,), (0,)), ((), ()))


def in_hbm(x):
    return pltpu.with_memory_space_constraint(x, pltpu.HBM)


def dot(a, b, dims):
    return lax.dot_general(a, b, dims, preferred_element_type=F32)


def span_hot(first_span):
    span = lax.broadcasted_iota(jnp.int32, (TILE, HEAD), 0) // SPAN + first_span
    lane = lax.broadcasted_iota(jnp.int32, (TILE, HEAD), 1)
    return (span == lane).astype(F32).astype(BF16)


def query_wide(query, first_span):
    return jnp.concatenate([query * BF16(SCALE), span_hot(first_span)], axis=1)


def spread_bias(bias):
    return jnp.broadcast_to(bias[:, None, :], (UNITS, SPAN, HEAD)).reshape(ROWS, HEAD).astype(BF16)


def fill_keys(chunks, bias_ref, ka_ref, first_chunk=0):
    for c, kv_ref in enumerate(chunks):
        rows = pl.ds(c * ROWS, ROWS)
        spans = slice((first_chunk + c) * UNITS, (first_chunk + c + 1) * UNITS)
        ka_ref[rows, :HEAD] = kv_ref[:, :HEAD]
        ka_ref[rows, HEAD:] = spread_bias(bias_ref[spans, :])


def later_in_span():
    key = lax.broadcasted_iota(jnp.int32, (TILE, TILE), 0)
    query = lax.broadcasted_iota(jnp.int32, (TILE, TILE), 1)
    return (key // SPAN == query // SPAN) & (key > query)


def forward_body(first, *refs):
    if first:
        q_ref, kv0, kv1, bias_ref, o_ref, m_ref, l_ref, ka_ref, s_ref = refs
    else:
        q_ref, kv0, kv1, bias_ref, o0_ref, m0_ref, l0_ref, pair_ref, lse_ref, ka_ref, s_ref = refs
    step = pl.program_id(0)
    chunks = (kv0, kv1)

    @pl.when(step == 0)
    def _():
        fill_keys(chunks, bias_ref, ka_ref, 0 if first else 2)

    q = q_ref[...]
    qa = query_wide(q, step * (TILE // SPAN))
    top = None if first else m0_ref[...]
    for c in range(2):
        rows = pl.ds(c * ROWS, ROWS)
        s_ref[rows, :] = dot(ka_ref[rows, :], qa, NT)
        if first and c == 0:
            own = pl.ds(pl.multiple_of(step * TILE, TILE), TILE)
            s_ref[own, :] = jnp.where(later_in_span(), LOW, s_ref[own, :])
        chunk_top = jnp.max(s_ref[rows, :], axis=0, keepdims=True)
        top = chunk_top if top is None else jnp.maximum(top, chunk_top)
    total = jnp.zeros((1, TILE), F32)
    out = jnp.zeros((HEAD, TILE), F32)
    for c, kv_ref in enumerate(chunks):
        weights = jnp.exp(s_ref[pl.ds(c * ROWS, ROWS), :] - top)
        total += jnp.sum(weights, axis=0, keepdims=True)
        out += dot(kv_ref[:, HEAD:], weights.astype(BF16), TN)
    if first:
        o_ref[...] = out
        m_ref[...] = top
        l_ref[...] = total
    else:
        fade = jnp.exp(m0_ref[...] - top)
        total += l0_ref[...] * fade
        out = (out + o0_ref[...] * fade) / total
        pair_ref[:, :HEAD] = q
        pair_ref[:, HEAD:] = out.T.astype(BF16)
        lse_ref[...] = top + jnp.log(total)


def tile_spec(cols):
    return pl.BlockSpec((TILE, cols), lambda i: (i, 0))


def row_spec(rows):
    return pl.BlockSpec((rows, TILE), lambda i: (0, i))


def cost(matmuls, pairs):
    return pl.CostEstimate(
        flops=matmuls * 2 * pairs * 2 * HEAD, bytes_accessed=4 << 20, transcendentals=pairs
    )


def once(*shape):
    return pl.BlockSpec(shape, lambda i: (0,) * len(shape), pipeline_mode=pl.Buffered(1))


def forward(first, q, kvs, bias, *carry):
    stat = jax.ShapeDtypeStruct((1, ROWS), F32)
    if first:
        outs = [pltpu.HBM((HEAD, ROWS), F32), stat, stat]
        out_specs = [row_spec(HEAD), row_spec(1), row_spec(1)]
    else:
        outs = [pltpu.HBM((ROWS, 2 * HEAD), BF16), stat]
        out_specs = [tile_spec(2 * HEAD), row_spec(1)]
    return pl.pallas_call(
        functools.partial(forward_body, first),
        out_shape=outs,
        grid=(ROWS // TILE,),
        in_specs=[
            tile_spec(HEAD),
            *[once(ROWS, 2 * HEAD)] * 2,
            once(4 * UNITS, HEAD),
            *[row_spec(x.shape[0]) for x in carry],
        ],
        out_specs=out_specs,
        scratch_shapes=[
            pltpu.VMEM((2 * ROWS, 2 * HEAD), BF16),
            pltpu.VMEM((2 * ROWS, TILE), F32),
        ],
        cost_estimate=cost(2, 2 * ROWS * ROWS),
        compiler_params=pltpu.CompilerParams(vmem_limit_bytes=GRANT),
        name="forward_near" if first else "forward_far",
    )(q, *kvs, bias, *carry)


def row_delta(g, att):
    return jnp.sum((g.astype(F32) * att.astype(F32)).T, axis=0, keepdims=True)


def query_body(pair_ref, g_ref, lse_ref, kv0, kv1, kv2, kv3, bias_ref, dq_ref, ka_ref, s_ref):
    step = pl.program_id(0)
    chunks = (kv0, kv1, kv2, kv3)

    @pl.when(step == 0)
    def _():
        fill_keys(chunks, bias_ref, ka_ref)

    qa = query_wide(pair_ref[:, :HEAD], step * (TILE // SPAN))
    g = g_ref[...]
    lse = lse_ref[...]
    delta = row_delta(g, pair_ref[:, HEAD:])
    own = pl.ds(pl.multiple_of(step * TILE, TILE), TILE)
    s_ref[...] = dot(ka_ref[pl.ds(0, ROWS), :], qa, NT)
    s_ref[own, :] = jnp.where(later_in_span(), LOW, s_ref[own, :])
    total = jnp.zeros((HEAD, TILE), F32)
    for c, kv_ref in enumerate(chunks):
        scores = dot(ka_ref[pl.ds(c * ROWS, ROWS), :], qa, NT) if c else s_ref[...]
        prob = jnp.exp(scores - lse)
        dprob = dot(kv_ref[:, HEAD:], g, NT)
        ds = (prob * (dprob - delta)).astype(BF16)
        total += dot(kv_ref[:, :HEAD], ds, TN)
    dq_ref[...] = (total * SCALE).T.astype(BF16)


def query_grad(pair, g, lse, kvs, bias):
    return pl.pallas_call(
        query_body,
        out_shape=jax.ShapeDtypeStruct((ROWS, HEAD), BF16),
        grid=(ROWS // TILE,),
        in_specs=[
            tile_spec(2 * HEAD),
            tile_spec(HEAD),
            row_spec(1),
            *[once(ROWS, 2 * HEAD)] * 4,
            once(4 * UNITS, HEAD),
        ],
        out_specs=tile_spec(HEAD),
        scratch_shapes=[
            pltpu.VMEM((4 * ROWS, 2 * HEAD), BF16),
            pltpu.VMEM((ROWS, TILE), F32),
        ],
        cost_estimate=cost(3, 4 * ROWS * ROWS),
        compiler_params=pltpu.CompilerParams(vmem_limit_bytes=WIDE_GRANT),
        name="query_grad",
    )(pair, g, lse, *kvs, bias)


def key_body(*refs):
    kv_ref, bias_ref = refs[:2]
    pairs, gs, lses = refs[2:6], refs[6:10], refs[10]
    dk_ref, dv_ref, ka_ref, s_ref, dk_acc, dv_acc = refs[11:]
    ka_ref[:, :HEAD] = kv_ref[:, :HEAD]
    ka_ref[:, HEAD:] = spread_bias(bias_ref[:UNITS, :])
    dk_acc[...] = jnp.zeros_like(dk_acc)
    dv_acc[...] = jnp.zeros_like(dv_acc)

    def tile(i, _):
        rows = pl.ds(pl.multiple_of(i * TILE, TILE), TILE)
        dk = jnp.zeros((ROWS, HEAD), F32)
        dv = jnp.zeros((ROWS, HEAD), F32)
        for c in range(4):
            q = pairs[c][rows, :HEAD]
            g = gs[c][rows, :]
            lse = lses[c : c + 1, rows]
            delta = row_delta(g, pairs[c][rows, HEAD:])
            qa = query_wide(q, i * (TILE // SPAN) + c * UNITS)
            scores = dot(ka_ref[...], qa, NT)
            if c == 0:
                s_ref[...] = scores
                s_ref[rows, :] = jnp.where(later_in_span(), LOW, s_ref[rows, :])
                scores = s_ref[...]
            prob = jnp.exp(scores - lse)
            dprob = dot(kv_ref[:, HEAD:], g, NT)
            ds = (prob * (dprob - delta)).astype(BF16)
            dv += dot(prob.astype(BF16), g, NN)
            dk += dot(ds, q, NN)
        dk_acc[...] += dk
        dv_acc[...] += dv
        return 0

    lax.fori_loop(0, ROWS // TILE, tile, 0)
    dk_ref[...] = (dk_acc[...] * SCALE).astype(BF16)
    dv_ref[...] = dv_acc[...].astype(BF16)


def key_grad(kv, bias, pairs, gs, lses):
    return pl.pallas_call(
        key_body,
        out_shape=[jax.ShapeDtypeStruct((ROWS, HEAD), BF16)] * 2,
        grid=(1,),
        in_specs=[
            once(ROWS, 2 * HEAD),
            once(4 * UNITS, HEAD),
            *[once(ROWS, 2 * HEAD)] * 4,
            *[once(ROWS, HEAD)] * 4,
            once(4, ROWS),
        ],
        out_specs=[once(ROWS, HEAD)] * 2,
        scratch_shapes=[
            pltpu.VMEM((ROWS, 2 * HEAD), BF16),
            pltpu.VMEM((ROWS, TILE), F32),
            pltpu.VMEM((ROWS, HEAD), F32),
            pltpu.VMEM((ROWS, HEAD), F32),
        ],
        cost_estimate=cost(4, 4 * ROWS * ROWS),
        compiler_params=pltpu.CompilerParams(vmem_limit_bytes=WIDE_GRANT),
        name="key_grad",
    )(kv, bias, *pairs, *gs, lses)


ZY = ("z", "y")
CHIPS = ("z", "y", "xl", "xh")
SWAP = [(0, 1), (1, 0)]


def other_core(x):
    return lax.ppermute(x, "core", SWAP)


def other_chip(x):
    return lax.ppermute(x, "xl", SWAP)


def everyone(x):
    far = other_chip(x)
    return x, other_core(x), far, other_core(far)


def exchange(x, axes):
    return lax.all_to_all(x, axes, 0, 0, tiled=True)


def in_order(first, own, peer):
    return jnp.stack([jnp.where(first, own, peer), jnp.where(first, peer, own)])


def span_bias(span_order, block_mask, xl, core):
    count = span_order.shape[0]
    row = jnp.arange(count, dtype=jnp.int32)
    owner, unit = row // UNITS, row % UNITS
    row_xl = xl ^ (owner // 2)
    half = core ^ (owner % 2) ^ ((unit // 4 + unit % 4) % 2)
    storage = 2 * (2 * unit + row_xl) + half
    held = (storage[:, None] == jnp.arange(count, dtype=jnp.int32)[None, :]).astype(jnp.int32)
    position = jnp.sum(held * span_order[None, :], axis=1)
    hot = (position[:, None] == jnp.arange(count, dtype=jnp.int32)[None, :]).astype(F32)
    pairs = jnp.dot(hot, jnp.dot(block_mask.astype(F32).T, hot.T))
    allowed = (pairs > 0.5) & (position[:, None] <= position[None, :])
    bias = jnp.where(allowed, 0.0, LOW).astype(F32)
    return jnp.pad(bias, ((0, 0), (0, HEAD - count)))


def side_by_side(first, own, peer):
    return jnp.concatenate([jnp.where(first, own, peer), jnp.where(first, peer, own)], axis=-1)


def across(x):
    return lax.ppermute(x, ("xl", "xh"), [(k, k ^ 3) for k in range(4)])


def weight_body(xl_ref, own0, own1, other0, other1, up_ref, out_ref, keep_ref, send_ref, w_ref):
    for flip, pieces in enumerate(((own0, own1), (other0, other1))):
        for units, part in zip((slice(0, MANY), slice(MANY, UNITS)), pieces):
            for c in range(2):
                rows = part[:, c * 32 : (c + 1) * 32, :]
                w_ref[units, xl_ref[0] ^ flip, :, c * 512 : (c + 1) * 512] = rows
    weight = w_ref[...].reshape(1024, 1024)
    out_ref[...] = weight
    for rows, out in ((slice(0, 128), keep_ref), (slice(128, 256), send_ref)):
        out[...] = dot(up_ref[rows, :], weight, NT)


def weight_whole(xl, own, other, up):
    return pl.pallas_call(
        weight_body,
        out_shape=[
            pltpu.HBM((1024, 1024), BF16),
            jax.ShapeDtypeStruct((128, 1024), F32),
            jax.ShapeDtypeStruct((128, 1024), F32),
        ],
        grid=(1,),
        in_specs=[pl.BlockSpec(memory_space=pltpu.SMEM)]
        + [once(*x.shape) for x in (*own, *other, up)],
        out_specs=[once(1024, 1024), once(128, 1024), once(128, 1024)],
        scratch_shapes=[pltpu.VMEM((UNITS, 2, 32, 1024), BF16)],
        cost_estimate=pl.CostEstimate(
            flops=2 * 256 * 1024 * 1024, bytes_accessed=4 << 20, transcendentals=0
        ),
        compiler_params=pltpu.CompilerParams(vmem_limit_bytes=GRANT),
        name="weight_whole",
    )(xl, *own, *other, up)


def term_body(own_ref, peer_ref, up_ref, out_ref, token_ref):
    token_ref[...] = jnp.zeros_like(token_ref)
    att = jnp.concatenate([own_ref[...], peer_ref[...]], axis=0)
    for c in range(2):
        cols = slice(c * 512, (c + 1) * 512)
        out_ref[:, cols] = dot(att, up_ref[:, cols], TN).astype(BF16)


def weight_terms(own, peer, up):
    return pl.pallas_call(
        term_body,
        out_shape=[pltpu.HBM((1024, 1024), BF16), jax.ShapeDtypeStruct((8, HEAD), F32)],
        grid=(1,),
        in_specs=[once(128, 1024), once(128, 1024), once(256, 1024)],
        out_specs=[once(1024, 1024), once(8, HEAD)],
        cost_estimate=pl.CostEstimate(
            flops=2 * 256 * 1024 * 1024, bytes_accessed=4 << 20, transcendentals=0
        ),
        compiler_params=pltpu.CompilerParams(vmem_limit_bytes=GRANT),
        name="weight_terms",
    )(own, peer, up)


IN_SMEM = pl.BlockSpec(memory_space=pltpu.SMEM)


def move(body, name, outs, scalars, *arrays, space=jax.ShapeDtypeStruct, after=()):
    spaces = space if isinstance(space, list) else [space] * len(outs)
    read = len(scalars) + len(arrays)

    def run(*refs):
        body(*refs[:read], *refs[read + len(after) :])

    return pl.pallas_call(
        run,
        out_shape=[make(shape, BF16) for make, shape in zip(spaces, outs)],
        grid=(1,),
        in_specs=[IN_SMEM] * len(scalars)
        + [once(*x.shape) for x in arrays]
        + [pl.BlockSpec(memory_space=pl.ANY)] * len(after),
        out_specs=[once(*shape) for shape in outs],
        cost_estimate=pl.CostEstimate(flops=0, bytes_accessed=4 << 20, transcendentals=0),
        compiler_params=pltpu.CompilerParams(vmem_limit_bytes=GRANT),
        name=name,
    )(*scalars, *arrays, *after)


def head_cols(h):
    return slice(h * HEAD, (h + 1) * HEAD)


def span_rows(half):
    return pl.ds(pl.multiple_of(half * SPAN, SPAN), SPAN)


def cut_body(half_ref, q_ref, k_ref, v_ref, own_ref, sent_ref):
    for side, out in enumerate((own_ref, sent_ref)):
        rows = span_rows(half_ref[0] ^ side)
        for t, x in enumerate((q_ref, k_ref, v_ref)):
            for h in range(HEADS):
                out[h, :, head_cols(t)] = x[rows, head_cols(h)]


def fill_body(core_ref, xh_ref, own_ref, peer_ref, w0, w1, w2, w3, out_ref):
    core, xh = core_ref[0], xh_ref[0]
    out_ref[pl.ds(core * HEADS, HEADS), :, : 3 * HEAD] = own_ref[...]
    out_ref[pl.ds((1 - core) * HEADS, HEADS), :, : 3 * HEAD] = peer_ref[...]
    first, mine_first = core == 0, xh == 0
    w = [jnp.where(first, x[:, :1024], x[:, 1024:]).astype(F32) for x in (w0, w1, w2, w3)]
    near = [jnp.where(first, w[0], w[1]), jnp.where(first, w[1], w[0])]
    far = [jnp.where(first, w[2], w[3]), jnp.where(first, w[3], w[2])]
    front = [jnp.where(mine_first, a, b) for a, b in zip(near, far)]
    back = [jnp.where(mine_first, b, a) for a, b in zip(near, far)]
    rows = jnp.concatenate(front + back, axis=0).astype(BF16)
    for c in range(2):
        part = rows[:, c * 512 : (c + 1) * 512]
        for unit in range(UNITS):
            out_ref[unit, c * 32 : (c + 1) * 32, 3 * HEAD :] = part


def up_body(core_ref, half_ref, own_ref, peer_ref, out_ref):
    core, half = core_ref[0], half_ref[0]
    for side in range(2):
        rows = span_rows(half ^ side)
        wide = own_ref[rows, :]
        mine = jnp.where(core == 0, wide[:, :1024], wide[:, 1024:])
        out_ref[span_rows(2 * side + core), :] = mine
        out_ref[span_rows(2 * side + 1 - core), :] = peer_ref[rows, :]


def split_body(x_ref, q_ref, kv_ref, w0_ref, w1_ref):
    x = x_ref[...]
    q_ref[...] = x[:, :, :HEAD].reshape(ROWS, HEAD)
    kv_ref[...] = x[:, :, HEAD : 3 * HEAD].reshape(ROWS, 2 * HEAD)
    w0_ref[...] = x[:MANY, :, 3 * HEAD :]
    w1_ref[...] = x[MANY:, :, 3 * HEAD :]


def cross_body(pair_ref, own_ref, peer_ref, out_ref):
    for s in range(2):
        for h in range(HEADS):
            unit, rows = s * HEADS + h, slice(s * SPAN, (s + 1) * SPAN)
            out_ref[unit, :, :HEAD] = pair_ref[unit * SPAN : (unit + 1) * SPAN, HEAD:]
            total = own_ref[rows, head_cols(h)] + peer_ref[rows, head_cols(h)]
            out_ref[unit, :, HEAD:] = total.astype(BF16)


def land_body(x_ref, att_ref, g_ref):
    g_ref[...] = x_ref[:, :, HEAD:].reshape(ROWS, HEAD)
    for s in range(2):
        for h in range(HEADS):
            att_ref[s * SPAN : (s + 1) * SPAN, head_cols(h)] = x_ref[s * HEADS + h, :, :HEAD]


def final_body(core_ref, half_ref, own_ref, peer_ref, dq_ref, dk_ref, dv_ref):
    core, half = core_ref[0], half_ref[0]
    for t, out in enumerate((dq_ref, dk_ref, dv_ref)):
        for h in range(HEADS):
            out[span_rows(half), head_cols(h)] = own_ref[core * HEADS + h, :, head_cols(t)]
            out[span_rows(1 - half), head_cols(h)] = peer_ref[h, :, head_cols(t)]


def local(query_states, key_states, value_states, span_order, block_mask, output_weight, upstream):
    z, y, xl, xh, core = (lax.axis_index(a) for a in ("z", "y", "xl", "xh", "core"))
    first_core = core == 0
    half = core ^ ((z + y) % 2)
    core_1, xl_1, xh_1, half_1 = (x.reshape(1) for x in (core, xl, xh, half))
    cols = output_weight.shape[1] // 2

    weight_far = lax.ppermute(output_weight, "xh", SWAP)
    weight_rows = [output_weight, other_core(output_weight), weight_far, other_core(weight_far)]
    unit_rows = (HEADS, SPAN, 3 * HEAD)
    own, sent = move(
        cut_body,
        "cut",
        [unit_rows] * 2,
        [half_1],
        in_hbm(query_states[0]),
        in_hbm(key_states[0]),
        in_hbm(value_states[0]),
        space=pltpu.HBM,
    )
    (blocks,) = move(
        fill_body,
        "fill",
        [(UNITS, SPAN, 3 * HEAD + 512)],
        [core_1, xh_1],
        in_hbm(own),
        other_core(sent),
        *weight_rows,
    )
    blocks = exchange(blocks, ZY)
    q, own_kv, *weight_own = move(
        split_body,
        "split",
        [(ROWS, HEAD), (ROWS, 2 * HEAD), (MANY, SPAN, 512), (UNITS - MANY, SPAN, 512)],
        [],
        blocks,
        space=pltpu.HBM,
    )
    far_kv = other_chip(own_kv)
    weight_other = [across(weight_own[0]), other_chip(weight_own[1])]
    near_kv = other_core(own_kv)
    own_kv, span_order, wide, side, which = lax.optimization_barrier(
        (own_kv, span_order, upstream[0], xl, core)
    )
    bias = span_bias(span_order, block_mask, side, which)

    up_sent = jnp.where(first_core, wide[:, cols:], wide[:, :cols])
    (up,) = move(
        up_body,
        "up",
        [(4 * SPAN, cols)],
        [core_1, half_1],
        in_hbm(wide),
        other_core(up_sent),
        space=pltpu.HBM,
    )

    out, top, total = forward(True, in_hbm(q), (in_hbm(own_kv), near_kv), bias)
    far_kv, total, up = lax.optimization_barrier((far_kv, total, up))
    kvs = (own_kv, near_kv, far_kv, other_core(far_kv))
    pair, lse = forward(False, in_hbm(q), kvs[2:], bias, in_hbm(out), top, total)
    lses = jnp.concatenate([lse, other_core(lse)], axis=0)
    lses = jnp.concatenate([lses, other_chip(lses)], axis=0)

    place, lse = lax.optimization_barrier((xl_1, lse))
    weight, grad_own, grad_sent = weight_whole(
        place, [in_hbm(x) for x in weight_own], weight_other, in_hbm(up)
    )
    (crossing,) = move(
        cross_body,
        "cross",
        [(UNITS, SPAN, 2 * HEAD)],
        [],
        in_hbm(pair),
        grad_own,
        other_core(grad_sent),
    )
    crossed = exchange(crossing, ZY)
    pair_sent, lses = lax.optimization_barrier((pair, lses))
    pair_far = other_chip(pair_sent)

    att_own, g = move(
        land_body,
        "land",
        [(2 * SPAN, HEADS * HEAD), (ROWS, HEAD)],
        [],
        crossed,
        after=(lses,),
        space=[jax.ShapeDtypeStruct, pltpu.HBM],
    )
    gs = everyone(g)
    att_peer = other_core(att_own)
    term, token = weight_terms(att_own, att_peer, in_hbm(up))
    term = exchange(term.reshape(UNITS, SPAN, cols), ZY)
    weight, pair_far, token = lax.optimization_barrier((weight, pair_far, token))
    pairs = (pair_sent, other_core(pair_sent), pair_far, other_core(pair_far))

    query_out = query_grad(in_hbm(pair), in_hbm(g), lse, [in_hbm(x) for x in kvs], bias)
    key_out, value_out = key_grad(in_hbm(own_kv), bias, pairs, gs, lses)
    grads = [x.reshape(UNITS, SPAN, HEAD) for x in (query_out, key_out, value_out)]
    grads = exchange(jnp.concatenate(grads, axis=2), ZY)

    def project(att):
        return dot(att, weight, NN).astype(BF16).reshape(2, SPAN, cols)

    own, peer = project(att_own), project(att_peer)
    kept = [lax.dynamic_index_in_dim(x, core, 0, False) for x in (own, peer)]
    gone = jnp.stack([lax.dynamic_index_in_dim(x, 1 - core, 0, False) for x in (own, peer)])
    gone = other_core(gone)
    own = in_order(half == 0, kept[0], kept[1]).reshape(2 * SPAN, cols)
    peer = in_order(half == 0, gone[1], gone[0]).reshape(2 * SPAN, cols)
    projected = side_by_side(first_core, own, peer)

    summed = jnp.sum(term.astype(F32), axis=0).reshape(4, 16, cols)
    chip = 2 * xl + xh
    total = lax.dynamic_index_in_dim(summed, chip, 0, False)
    for step in (1, 2, 3):
        part = lax.dynamic_index_in_dim(summed, chip ^ step, 0, False)
        total = total + lax.ppermute(part, ("xl", "xh"), [(k, k ^ step) for k in range(4)])
    total = total.reshape(2, -1, cols)
    own = lax.dynamic_index_in_dim(total, core, 0, False)
    peer = other_core(lax.dynamic_index_in_dim(total, 1 - core, 0, False))
    weight_gradient = side_by_side(first_core, own, peer)

    peer = other_core(lax.dynamic_slice_in_dim(grads, (1 - core) * HEADS, HEADS, 0))
    own_rows = (2 * SPAN, HEADS * HEAD)
    query_gradient, key_gradient, value_gradient = move(
        final_body, "final", [own_rows] * 3, [core_1, half_1], grads, peer, after=(token,)
    )
    return (
        projected[None],
        query_gradient[None],
        key_gradient[None],
        value_gradient[None],
        weight_gradient,
    )


def solution(mesh):
    axes = ("z", "y", "xl", "xh", "core")
    fine = Mesh(mesh.devices.reshape(4, 4, 2, 2, 2), axes)
    rows = P(("xh", "core"), ("z", "y", "xl"), None)
    return jax.shard_map(
        local,
        mesh=fine,
        in_specs=(rows, rows, rows, P(), P(), P(axes, None), rows),
        out_specs=(rows, rows, rows, rows, P(axes, None)),
        check_vma=False,
    )
```

```python
import functools

import jax
import jax.numpy as jnp
from jax import lax
from jax.experimental import pallas as pl
from jax.experimental.pallas import tpu as pltpu
from jax.sharding import Mesh, PartitionSpec as P

HEADS = 8
HEAD = 128
SPAN = 64
UNITS = 16
MANY = 12
ROWS = UNITS * SPAN
TILE = 256
LOW = -1e30
GRANT = 16 << 20
WIDE_GRANT = 32 << 20
SCALE = 1.0 / HEAD
F32 = jnp.float32
BF16 = jnp.bfloat16
NT = (((1,), (1,)), ((), ()))
NN = (((1,), (0,)), ((), ()))
TN = (((0,), (0,)), ((), ()))


def in_hbm(x):
    return pltpu.with_memory_space_constraint(x, pltpu.HBM)


def dot(a, b, dims):
    return lax.dot_general(a, b, dims, preferred_element_type=F32)


def span_hot(first_span):
    span = lax.broadcasted_iota(jnp.int32, (TILE, HEAD), 0) // SPAN + first_span
    lane = lax.broadcasted_iota(jnp.int32, (TILE, HEAD), 1)
    return (span == lane).astype(F32).astype(BF16)


def query_wide(query, first_span):
    return jnp.concatenate([query * BF16(SCALE), span_hot(first_span)], axis=1)


def spread_bias(bias):
    return jnp.broadcast_to(bias[:, None, :], (UNITS, SPAN, HEAD)).reshape(ROWS, HEAD).astype(BF16)


def fill_keys(chunks, bias_ref, ka_ref, first_chunk=0):
    for c, kv_ref in enumerate(chunks):
        rows = pl.ds(c * ROWS, ROWS)
        spans = slice((first_chunk + c) * UNITS, (first_chunk + c + 1) * UNITS)
        ka_ref[rows, :HEAD] = kv_ref[:, :HEAD]
        ka_ref[rows, HEAD:] = spread_bias(bias_ref[spans, :])


def later_in_span():
    key = lax.broadcasted_iota(jnp.int32, (TILE, TILE), 0)
    query = lax.broadcasted_iota(jnp.int32, (TILE, TILE), 1)
    return (key // SPAN == query // SPAN) & (key > query)


def forward_body(first, *refs):
    if first:
        q_ref, kv0, kv1, bias_ref, o_ref, m_ref, l_ref, ka_ref, s_ref = refs
    else:
        q_ref, kv0, kv1, bias_ref, o0_ref, m0_ref, l0_ref, pair_ref, lse_ref, ka_ref, s_ref = refs
    step = pl.program_id(0)
    chunks = (kv0, kv1)

    @pl.when(step == 0)
    def _():
        fill_keys(chunks, bias_ref, ka_ref, 0 if first else 2)

    q = q_ref[...]
    qa = query_wide(q, step * (TILE // SPAN))
    top = None if first else m0_ref[...]
    for c in range(2):
        rows = pl.ds(c * ROWS, ROWS)
        s_ref[rows, :] = dot(ka_ref[rows, :], qa, NT)
        if first and c == 0:
            own = pl.ds(pl.multiple_of(step * TILE, TILE), TILE)
            s_ref[own, :] = jnp.where(later_in_span(), LOW, s_ref[own, :])
        chunk_top = jnp.max(s_ref[rows, :], axis=0, keepdims=True)
        top = chunk_top if top is None else jnp.maximum(top, chunk_top)
    total = jnp.zeros((1, TILE), F32)
    out = jnp.zeros((HEAD, TILE), F32)
    for c, kv_ref in enumerate(chunks):
        weights = jnp.exp(s_ref[pl.ds(c * ROWS, ROWS), :] - top)
        total += jnp.sum(weights, axis=0, keepdims=True)
        out += dot(kv_ref[:, HEAD:], weights.astype(BF16), TN)
    if first:
        o_ref[...] = out
        m_ref[...] = top
        l_ref[...] = total
    else:
        fade = jnp.exp(m0_ref[...] - top)
        total += l0_ref[...] * fade
        out = (out + o0_ref[...] * fade) / total
        pair_ref[:, :HEAD] = q
        pair_ref[:, HEAD:] = out.T.astype(BF16)
        lse_ref[...] = top + jnp.log(total)


def tile_spec(cols):
    return pl.BlockSpec((TILE, cols), lambda i: (i, 0))


def row_spec(rows):
    return pl.BlockSpec((rows, TILE), lambda i: (0, i))


def cost(matmuls, pairs):
    return pl.CostEstimate(
        flops=matmuls * 2 * pairs * 2 * HEAD, bytes_accessed=4 << 20, transcendentals=pairs
    )


def once(*shape):
    return pl.BlockSpec(shape, lambda i: (0,) * len(shape), pipeline_mode=pl.Buffered(1))


def forward(first, q, kvs, bias, *carry):
    stat = jax.ShapeDtypeStruct((1, ROWS), F32)
    if first:
        outs = [pltpu.HBM((HEAD, ROWS), F32), stat, stat]
        out_specs = [row_spec(HEAD), row_spec(1), row_spec(1)]
    else:
        outs = [pltpu.HBM((ROWS, 2 * HEAD), BF16), stat]
        out_specs = [tile_spec(2 * HEAD), row_spec(1)]
    return pl.pallas_call(
        functools.partial(forward_body, first),
        out_shape=outs,
        grid=(ROWS // TILE,),
        in_specs=[
            tile_spec(HEAD),
            *[once(ROWS, 2 * HEAD)] * 2,
            once(4 * UNITS, HEAD),
            *[row_spec(x.shape[0]) for x in carry],
        ],
        out_specs=out_specs,
        scratch_shapes=[
            pltpu.VMEM((2 * ROWS, 2 * HEAD), BF16),
            pltpu.VMEM((2 * ROWS, TILE), F32),
        ],
        cost_estimate=cost(2, 2 * ROWS * ROWS),
        compiler_params=pltpu.CompilerParams(vmem_limit_bytes=GRANT),
        name="forward_near" if first else "forward_far",
    )(q, *kvs, bias, *carry)


def row_delta(g, att):
    return jnp.sum((g.astype(F32) * att.astype(F32)).T, axis=0, keepdims=True)


def query_body(pair_ref, g_ref, lse_ref, kv0, kv1, kv2, kv3, bias_ref, dq_ref, ka_ref, s_ref):
    step = pl.program_id(0)
    chunks = (kv0, kv1, kv2, kv3)

    @pl.when(step == 0)
    def _():
        fill_keys(chunks, bias_ref, ka_ref)

    qa = query_wide(pair_ref[:, :HEAD], step * (TILE // SPAN))
    g = g_ref[...]
    lse = lse_ref[...]
    delta = row_delta(g, pair_ref[:, HEAD:])
    own = pl.ds(pl.multiple_of(step * TILE, TILE), TILE)
    s_ref[...] = dot(ka_ref[pl.ds(0, ROWS), :], qa, NT)
    s_ref[own, :] = jnp.where(later_in_span(), LOW, s_ref[own, :])
    total = jnp.zeros((HEAD, TILE), F32)
    for c, kv_ref in enumerate(chunks):
        scores = dot(ka_ref[pl.ds(c * ROWS, ROWS), :], qa, NT) if c else s_ref[...]
        prob = jnp.exp(scores - lse)
        dprob = dot(kv_ref[:, HEAD:], g, NT)
        ds = (prob * (dprob - delta)).astype(BF16)
        total += dot(kv_ref[:, :HEAD], ds, TN)
    dq_ref[...] = (total * SCALE).T.astype(BF16)


def query_grad(pair, g, lse, kvs, bias):
    return pl.pallas_call(
        query_body,
        out_shape=jax.ShapeDtypeStruct((ROWS, HEAD), BF16),
        grid=(ROWS // TILE,),
        in_specs=[
            tile_spec(2 * HEAD),
            tile_spec(HEAD),
            row_spec(1),
            *[once(ROWS, 2 * HEAD)] * 4,
            once(4 * UNITS, HEAD),
        ],
        out_specs=tile_spec(HEAD),
        scratch_shapes=[
            pltpu.VMEM((4 * ROWS, 2 * HEAD), BF16),
            pltpu.VMEM((ROWS, TILE), F32),
        ],
        cost_estimate=cost(3, 4 * ROWS * ROWS),
        compiler_params=pltpu.CompilerParams(vmem_limit_bytes=WIDE_GRANT),
        name="query_grad",
    )(pair, g, lse, *kvs, bias)


def key_body(*refs):
    kv_ref, bias_ref = refs[:2]
    pairs, gs, lses = refs[2:6], refs[6:10], refs[10]
    dk_ref, dv_ref, ka_ref, s_ref, dk_acc, dv_acc = refs[11:]
    ka_ref[:, :HEAD] = kv_ref[:, :HEAD]
    ka_ref[:, HEAD:] = spread_bias(bias_ref[:UNITS, :])
    dk_acc[...] = jnp.zeros_like(dk_acc)
    dv_acc[...] = jnp.zeros_like(dv_acc)

    def tile(i, _):
        rows = pl.ds(pl.multiple_of(i * TILE, TILE), TILE)
        dk = jnp.zeros((ROWS, HEAD), F32)
        dv = jnp.zeros((ROWS, HEAD), F32)
        for c in range(4):
            q = pairs[c][rows, :HEAD]
            g = gs[c][rows, :]
            lse = lses[c : c + 1, rows]
            delta = row_delta(g, pairs[c][rows, HEAD:])
            qa = query_wide(q, i * (TILE // SPAN) + c * UNITS)
            scores = dot(ka_ref[...], qa, NT)
            if c == 0:
                s_ref[...] = scores
                s_ref[rows, :] = jnp.where(later_in_span(), LOW, s_ref[rows, :])
                scores = s_ref[...]
            prob = jnp.exp(scores - lse)
            dprob = dot(kv_ref[:, HEAD:], g, NT)
            ds = (prob * (dprob - delta)).astype(BF16)
            dv += dot(prob.astype(BF16), g, NN)
            dk += dot(ds, q, NN)
        dk_acc[...] += dk
        dv_acc[...] += dv
        return 0

    lax.fori_loop(0, ROWS // TILE, tile, 0)
    dk_ref[...] = (dk_acc[...] * SCALE).astype(BF16)
    dv_ref[...] = dv_acc[...].astype(BF16)


def key_grad(kv, bias, pairs, gs, lses):
    return pl.pallas_call(
        key_body,
        out_shape=[jax.ShapeDtypeStruct((ROWS, HEAD), BF16)] * 2,
        grid=(1,),
        in_specs=[
            once(ROWS, 2 * HEAD),
            once(4 * UNITS, HEAD),
            *[once(ROWS, 2 * HEAD)] * 4,
            *[once(ROWS, HEAD)] * 4,
            once(4, ROWS),
        ],
        out_specs=[once(ROWS, HEAD)] * 2,
        scratch_shapes=[
            pltpu.VMEM((ROWS, 2 * HEAD), BF16),
            pltpu.VMEM((ROWS, TILE), F32),
            pltpu.VMEM((ROWS, HEAD), F32),
            pltpu.VMEM((ROWS, HEAD), F32),
        ],
        cost_estimate=cost(4, 4 * ROWS * ROWS),
        compiler_params=pltpu.CompilerParams(vmem_limit_bytes=WIDE_GRANT),
        name="key_grad",
    )(kv, bias, *pairs, *gs, lses)


ZY = ("z", "y")
CHIPS = ("z", "y", "xl", "xh")
SWAP = [(0, 1), (1, 0)]


def other_core(x):
    return lax.ppermute(x, "core", SWAP)


def other_chip(x):
    return lax.ppermute(x, "xl", SWAP)


def everyone(x):
    far = other_chip(x)
    return x, other_core(x), far, other_core(far)


def exchange(x, axes):
    return lax.all_to_all(x, axes, 0, 0, tiled=True)


def in_order(first, own, peer):
    return jnp.stack([jnp.where(first, own, peer), jnp.where(first, peer, own)])


def span_bias(span_order, block_mask, xl, core):
    count = span_order.shape[0]
    row = jnp.arange(count, dtype=jnp.int32)
    owner, unit = row // UNITS, row % UNITS
    row_xl = xl ^ (owner // 2)
    half = core ^ (owner % 2) ^ ((unit // 4 + unit % 4) % 2)
    storage = 2 * (2 * unit + row_xl) + half
    held = (storage[:, None] == jnp.arange(count, dtype=jnp.int32)[None, :]).astype(jnp.int32)
    position = jnp.sum(held * span_order[None, :], axis=1)
    hot = (position[:, None] == jnp.arange(count, dtype=jnp.int32)[None, :]).astype(F32)
    pairs = jnp.dot(hot, jnp.dot(block_mask.astype(F32).T, hot.T))
    allowed = (pairs > 0.5) & (position[:, None] <= position[None, :])
    bias = jnp.where(allowed, 0.0, LOW).astype(F32)
    return jnp.pad(bias, ((0, 0), (0, HEAD - count)))


def side_by_side(first, own, peer):
    return jnp.concatenate([jnp.where(first, own, peer), jnp.where(first, peer, own)], axis=-1)


def across(x):
    return lax.ppermute(x, ("xl", "xh"), [(k, k ^ 3) for k in range(4)])


def weight_body(xl_ref, own0, own1, other0, other1, up_ref, out_ref, keep_ref, send_ref, w_ref):
    for flip, pieces in enumerate(((own0, own1), (other0, other1))):
        for units, part in zip((slice(0, MANY), slice(MANY, UNITS)), pieces):
            for c in range(2):
                rows = part[:, c * 32 : (c + 1) * 32, :]
                w_ref[units, xl_ref[0] ^ flip, :, c * 512 : (c + 1) * 512] = rows
    weight = w_ref[...].reshape(1024, 1024)
    out_ref[...] = weight
    for rows, out in ((slice(0, 128), keep_ref), (slice(128, 256), send_ref)):
        out[...] = dot(up_ref[rows, :], weight, NT)


def weight_whole(xl, own, other, up):
    return pl.pallas_call(
        weight_body,
        out_shape=[
            pltpu.HBM((1024, 1024), BF16),
            jax.ShapeDtypeStruct((128, 1024), F32),
            jax.ShapeDtypeStruct((128, 1024), F32),
        ],
        grid=(1,),
        in_specs=[pl.BlockSpec(memory_space=pltpu.SMEM)]
        + [once(*x.shape) for x in (*own, *other, up)],
        out_specs=[once(1024, 1024), once(128, 1024), once(128, 1024)],
        scratch_shapes=[pltpu.VMEM((UNITS, 2, 32, 1024), BF16)],
        cost_estimate=pl.CostEstimate(
            flops=2 * 256 * 1024 * 1024, bytes_accessed=4 << 20, transcendentals=0
        ),
        compiler_params=pltpu.CompilerParams(vmem_limit_bytes=GRANT),
        name="weight_whole",
    )(xl, *own, *other, up)


def term_body(own_ref, peer_ref, up_ref, out_ref, token_ref):
    token_ref[...] = jnp.zeros_like(token_ref)
    att = jnp.concatenate([own_ref[...], peer_ref[...]], axis=0)
    for c in range(2):
        cols = slice(c * 512, (c + 1) * 512)
        out_ref[:, cols] = dot(att, up_ref[:, cols], TN).astype(BF16)


def weight_terms(own, peer, up):
    return pl.pallas_call(
        term_body,
        out_shape=[pltpu.HBM((1024, 1024), BF16), jax.ShapeDtypeStruct((8, HEAD), F32)],
        grid=(1,),
        in_specs=[once(128, 1024), once(128, 1024), once(256, 1024)],
        out_specs=[once(1024, 1024), once(8, HEAD)],
        cost_estimate=pl.CostEstimate(
            flops=2 * 256 * 1024 * 1024, bytes_accessed=4 << 20, transcendentals=0
        ),
        compiler_params=pltpu.CompilerParams(vmem_limit_bytes=GRANT),
        name="weight_terms",
    )(own, peer, up)


IN_SMEM = pl.BlockSpec(memory_space=pltpu.SMEM)


def move(body, name, outs, scalars, *arrays, space=jax.ShapeDtypeStruct, after=()):
    spaces = space if isinstance(space, list) else [space] * len(outs)
    read = len(scalars) + len(arrays)

    def run(*refs):
        body(*refs[:read], *refs[read + len(after) :])

    return pl.pallas_call(
        run,
        out_shape=[make(shape, BF16) for make, shape in zip(spaces, outs)],
        grid=(1,),
        in_specs=[IN_SMEM] * len(scalars)
        + [once(*x.shape) for x in arrays]
        + [pl.BlockSpec(memory_space=pl.ANY)] * len(after),
        out_specs=[once(*shape) for shape in outs],
        cost_estimate=pl.CostEstimate(flops=0, bytes_accessed=4 << 20, transcendentals=0),
        compiler_params=pltpu.CompilerParams(vmem_limit_bytes=GRANT),
        name=name,
    )(*scalars, *arrays, *after)


def head_cols(h):
    return slice(h * HEAD, (h + 1) * HEAD)


def span_rows(half):
    return pl.ds(pl.multiple_of(half * SPAN, SPAN), SPAN)


def cut_body(half_ref, q_ref, k_ref, v_ref, own_ref, sent_ref):
    for side, out in enumerate((own_ref, sent_ref)):
        rows = span_rows(half_ref[0] ^ side)
        for t, x in enumerate((q_ref, k_ref, v_ref)):
            for h in range(HEADS):
                out[h, :, head_cols(t)] = x[rows, head_cols(h)]


def fill_body(core_ref, xh_ref, xl_ref, own_ref, peer_ref, w0, w1, w2, w3, out_ref):
    core, xh = core_ref[0], xh_ref[0]
    out_ref[pl.ds(core * HEADS, HEADS), :, : 3 * HEAD] = own_ref[...]
    out_ref[pl.ds((1 - core) * HEADS, HEADS), :, : 3 * HEAD] = peer_ref[...]
    first, mine_first = core == 0, xh == 0
    w = [jnp.where(first, x[:, :1024], x[:, 1024:]).astype(F32) for x in (w0, w1, w2, w3)]
    near = [jnp.where(first, w[0], w[1]), jnp.where(first, w[1], w[0])]
    far = [jnp.where(first, w[2], w[3]), jnp.where(first, w[3], w[2])]
    front = [jnp.where(mine_first, a, b) for a, b in zip(near, far)]
    back = [jnp.where(mine_first, b, a) for a, b in zip(near, far)]
    rows = jnp.concatenate(front + back, axis=0).astype(BF16)
    for c in range(2):
        part = rows[:, c * 512 : (c + 1) * 512]
        for unit in range(UNITS):
            out_ref[unit, c * 32 : (c + 1) * 32, 3 * HEAD :] = part


def up_body(core_ref, half_ref, own_ref, peer_ref, out_ref):
    core, half = core_ref[0], half_ref[0]
    for side in range(2):
        rows = span_rows(half ^ side)
        wide = own_ref[rows, :]
        mine = jnp.where(core == 0, wide[:, :1024], wide[:, 1024:])
        out_ref[span_rows(2 * side + core), :] = mine
        out_ref[span_rows(2 * side + 1 - core), :] = peer_ref[rows, :]


def split_body(x_ref, q_ref, kv_ref, w0_ref, w1_ref):
    x = x_ref[...]
    q_ref[...] = x[:, :, :HEAD].reshape(ROWS, HEAD)
    kv_ref[...] = x[:, :, HEAD : 3 * HEAD].reshape(ROWS, 2 * HEAD)
    w0_ref[...] = x[:MANY, :, 3 * HEAD :]
    w1_ref[...] = x[MANY:, :, 3 * HEAD :]


def cross_body(pair_ref, own_ref, peer_ref, out_ref):
    for s in range(2):
        for h in range(HEADS):
            unit, rows = s * HEADS + h, slice(s * SPAN, (s + 1) * SPAN)
            out_ref[unit, :, :HEAD] = pair_ref[unit * SPAN : (unit + 1) * SPAN, HEAD:]
            total = own_ref[rows, head_cols(h)] + peer_ref[rows, head_cols(h)]
            out_ref[unit, :, HEAD:] = total.astype(BF16)


def land_body(x_ref, att_ref, g_ref):
    g_ref[...] = x_ref[:, :, HEAD:].reshape(ROWS, HEAD)
    for s in range(2):
        for h in range(HEADS):
            att_ref[s * SPAN : (s + 1) * SPAN, head_cols(h)] = x_ref[s * HEADS + h, :, :HEAD]


def final_body(core_ref, half_ref, own_ref, peer_ref, dq_ref, dk_ref, dv_ref):
    core, half = core_ref[0], half_ref[0]
    for t, out in enumerate((dq_ref, dk_ref, dv_ref)):
        for h in range(HEADS):
            out[span_rows(half), head_cols(h)] = own_ref[core * HEADS + h, :, head_cols(t)]
            out[span_rows(1 - half), head_cols(h)] = peer_ref[h, :, head_cols(t)]


def local(query_states, key_states, value_states, span_order, block_mask, output_weight, upstream):
    z, y, xl, xh, core = (lax.axis_index(a) for a in ("z", "y", "xl", "xh", "core"))
    half = core ^ ((z + y) % 2)
    core_1, xl_1, xh_1, half_1 = (x.reshape(1) for x in (core, xl, xh, half))
    cols = output_weight.shape[1] // 2

    weight_far = lax.ppermute(output_weight, "xh", SWAP)
    weight_rows = [in_hbm(output_weight), other_core(output_weight), weight_far, other_core(weight_far)]
    unit_rows = (HEADS, SPAN, 3 * HEAD)
    own, sent = move(
        cut_body,
        "cut",
        [unit_rows] * 2,
        [half_1],
        in_hbm(query_states[0]),
        in_hbm(key_states[0]),
        in_hbm(value_states[0]),
        space=pltpu.HBM,
    )
    (blocks,) = move(
        fill_body,
        "fill",
        [(UNITS, SPAN, 3 * HEAD + 512)],
        [core_1, xh_1, xl_1],
        in_hbm(own),
        other_core(sent),
        *weight_rows,
    )
    blocks = exchange(blocks, ZY)
    q, own_kv, *weight_own = move(
        split_body,
        "split",
        [(ROWS, HEAD), (ROWS, 2 * HEAD), (MANY, SPAN, 512), (UNITS - MANY, SPAN, 512)],
        [],
        blocks,
        space=pltpu.HBM,
    )
    far_kv = other_chip(own_kv)
    weight_other = [across(weight_own[0]), other_chip(weight_own[1])]
    near_kv = other_core(own_kv)
    own_kv, span_order, wide, side, which = lax.optimization_barrier(
        (own_kv, span_order, upstream[0], xl, core)
    )
    first_core = which == 0
    bias = span_bias(span_order, block_mask, side, which)

    up_sent = jnp.where(first_core, wide[:, cols:], wide[:, :cols])
    (up,) = move(
        up_body,
        "up",
        [(4 * SPAN, cols)],
        [core_1, half_1],
        in_hbm(wide),
        other_core(up_sent),
        space=pltpu.HBM,
    )

    out, top, total = forward(True, in_hbm(q), (in_hbm(own_kv), near_kv), bias)
    far_kv, total, up = lax.optimization_barrier((far_kv, total, up))
    kvs = (own_kv, near_kv, far_kv, other_core(far_kv))
    pair, lse = forward(False, in_hbm(q), kvs[2:], bias, in_hbm(out), top, total)
    lses = jnp.concatenate([lse, other_core(lse)], axis=0)
    lses = jnp.concatenate([lses, other_chip(lses)], axis=0)

    place, lse = lax.optimization_barrier((xl_1, lse))
    weight, grad_own, grad_sent = weight_whole(
        place, [in_hbm(x) for x in weight_own], weight_other, in_hbm(up)
    )
    (crossing,) = move(
        cross_body,
        "cross",
        [(UNITS, SPAN, 2 * HEAD)],
        [],
        in_hbm(pair),
        grad_own,
        other_core(grad_sent),
    )
    crossed = exchange(crossing, ZY)
    pair_sent, lses = lax.optimization_barrier((pair, lses))
    pair_far = other_chip(pair_sent)

    att_own, g = move(
        land_body,
        "land",
        [(2 * SPAN, HEADS * HEAD), (ROWS, HEAD)],
        [],
        crossed,
        after=(lses,),
        space=[jax.ShapeDtypeStruct, pltpu.HBM],
    )
    gs = everyone(g)
    att_peer = other_core(att_own)
    term, token = weight_terms(att_own, att_peer, in_hbm(up))
    term = exchange(term.reshape(UNITS, SPAN, cols), ZY)
    weight, pair_far, token = lax.optimization_barrier((weight, pair_far, token))
    pairs = (pair_sent, other_core(pair_sent), pair_far, other_core(pair_far))

    query_out = query_grad(in_hbm(pair), in_hbm(g), lse, [in_hbm(x) for x in kvs], bias)
    key_out, value_out = key_grad(in_hbm(own_kv), bias, pairs, gs, lses)
    grads = [x.reshape(UNITS, SPAN, HEAD) for x in (query_out, key_out, value_out)]
    grads = exchange(jnp.concatenate(grads, axis=2), ZY)

    def project(att):
        return dot(att, weight, NN).astype(BF16).reshape(2, SPAN, cols)

    own, peer = project(att_own), project(att_peer)
    kept = [lax.dynamic_index_in_dim(x, core, 0, False) for x in (own, peer)]
    gone = jnp.stack([lax.dynamic_index_in_dim(x, 1 - core, 0, False) for x in (own, peer)])
    gone = other_core(gone)
    own = in_order(half == 0, kept[0], kept[1]).reshape(2 * SPAN, cols)
    peer = in_order(half == 0, gone[1], gone[0]).reshape(2 * SPAN, cols)
    projected = side_by_side(first_core, own, peer)

    summed = jnp.sum(term.astype(F32), axis=0).reshape(4, 16, cols)
    chip = 2 * xl + xh
    total = lax.dynamic_index_in_dim(summed, chip, 0, False)
    for step in (1, 2, 3):
        part = lax.dynamic_index_in_dim(summed, chip ^ step, 0, False)
        total = total + lax.ppermute(part, ("xl", "xh"), [(k, k ^ step) for k in range(4)])
    total = total.reshape(2, -1, cols)
    own = lax.dynamic_index_in_dim(total, core, 0, False)
    peer = other_core(lax.dynamic_index_in_dim(total, 1 - core, 0, False))
    weight_gradient = side_by_side(first_core, own, peer)

    peer = other_core(lax.dynamic_slice_in_dim(grads, (1 - core) * HEADS, HEADS, 0))
    own_rows = (2 * SPAN, HEADS * HEAD)
    query_gradient, key_gradient, value_gradient = move(
        final_body, "final", [own_rows] * 3, [core_1, half_1], grads, peer, after=(token,)
    )
    return (
        projected[None],
        query_gradient[None],
        key_gradient[None],
        value_gradient[None],
        weight_gradient,
    )


def solution(mesh):
    axes = ("z", "y", "xl", "xh", "core")
    fine = Mesh(mesh.devices.reshape(4, 4, 2, 2, 2), axes)
    rows = P(("xh", "core"), ("z", "y", "xl"), None)
    return jax.shard_map(
        local,
        mesh=fine,
        in_specs=(rows, rows, rows, P(), P(), P(axes, None), rows),
        out_specs=(rows, rows, rows, rows, P(axes, None)),
        check_vma=False,
    )
```

```python
import functools

import jax
import jax.numpy as jnp
from jax import lax
from jax.experimental import pallas as pl
from jax.experimental.pallas import tpu as pltpu
from jax.sharding import Mesh, PartitionSpec as P

HEADS = 8
HEAD = 128
SPAN = 64
UNITS = 16
MANY = 12
ROWS = UNITS * SPAN
TILE = 256
LOW = -1e30
GRANT = 16 << 20
WIDE_GRANT = 32 << 20
SCALE = 1.0 / HEAD
F32 = jnp.float32
BF16 = jnp.bfloat16
NT = (((1,), (1,)), ((), ()))
NN = (((1,), (0,)), ((), ()))
TN = (((0,), (0,)), ((), ()))


def in_hbm(x):
    return pltpu.with_memory_space_constraint(x, pltpu.HBM)


def dot(a, b, dims):
    return lax.dot_general(a, b, dims, preferred_element_type=F32)


def span_hot(first_span):
    span = lax.broadcasted_iota(jnp.int32, (TILE, HEAD), 0) // SPAN + first_span
    lane = lax.broadcasted_iota(jnp.int32, (TILE, HEAD), 1)
    return (span == lane).astype(F32).astype(BF16)


def query_wide(query, first_span):
    return jnp.concatenate([query * BF16(SCALE), span_hot(first_span)], axis=1)


def spread_bias(bias):
    return jnp.broadcast_to(bias[:, None, :], (UNITS, SPAN, HEAD)).reshape(ROWS, HEAD).astype(BF16)


def fill_keys(chunks, bias_ref, ka_ref, first_chunk=0):
    for c, kv_ref in enumerate(chunks):
        rows = pl.ds(c * ROWS, ROWS)
        spans = slice((first_chunk + c) * UNITS, (first_chunk + c + 1) * UNITS)
        ka_ref[rows, :HEAD] = kv_ref[:, :HEAD]
        ka_ref[rows, HEAD:] = spread_bias(bias_ref[spans, :])


def later_in_span():
    key = lax.broadcasted_iota(jnp.int32, (TILE, TILE), 0)
    query = lax.broadcasted_iota(jnp.int32, (TILE, TILE), 1)
    return (key // SPAN == query // SPAN) & (key > query)


def forward_body(first, *refs):
    if first:
        q_ref, kv0, kv1, bias_ref, o_ref, m_ref, l_ref, ka_ref, s_ref = refs
    else:
        q_ref, kv0, kv1, bias_ref, o0_ref, m0_ref, l0_ref, pair_ref, lse_ref, ka_ref, s_ref = refs
    step = pl.program_id(0)
    chunks = (kv0, kv1)

    @pl.when(step == 0)
    def _():
        fill_keys(chunks, bias_ref, ka_ref, 0 if first else 2)

    q = q_ref[...]
    qa = query_wide(q, step * (TILE // SPAN))
    top = None if first else m0_ref[...]
    for c in range(2):
        rows = pl.ds(c * ROWS, ROWS)
        s_ref[rows, :] = dot(ka_ref[rows, :], qa, NT)
        if first and c == 0:
            own = pl.ds(pl.multiple_of(step * TILE, TILE), TILE)
            s_ref[own, :] = jnp.where(later_in_span(), LOW, s_ref[own, :])
        chunk_top = jnp.max(s_ref[rows, :], axis=0, keepdims=True)
        top = chunk_top if top is None else jnp.maximum(top, chunk_top)
    total = jnp.zeros((1, TILE), F32)
    out = jnp.zeros((HEAD, TILE), F32)
    for c, kv_ref in enumerate(chunks):
        weights = jnp.exp(s_ref[pl.ds(c * ROWS, ROWS), :] - top)
        total += jnp.sum(weights, axis=0, keepdims=True)
        out += dot(kv_ref[:, HEAD:], weights.astype(BF16), TN)
    if first:
        o_ref[...] = out
        m_ref[...] = top
        l_ref[...] = total
    else:
        fade = jnp.exp(m0_ref[...] - top)
        total += l0_ref[...] * fade
        out = (out + o0_ref[...] * fade) / total
        pair_ref[:, :HEAD] = q
        pair_ref[:, HEAD:] = out.T.astype(BF16)
        lse_ref[...] = top + jnp.log(total)


def tile_spec(cols):
    return pl.BlockSpec((TILE, cols), lambda i: (i, 0))


def row_spec(rows):
    return pl.BlockSpec((rows, TILE), lambda i: (0, i))


def cost(matmuls, pairs):
    return pl.CostEstimate(
        flops=matmuls * 2 * pairs * 2 * HEAD, bytes_accessed=4 << 20, transcendentals=pairs
    )


def once(*shape):
    return pl.BlockSpec(shape, lambda i: (0,) * len(shape), pipeline_mode=pl.Buffered(1))


def forward(first, q, kvs, bias, *carry):
    stat = jax.ShapeDtypeStruct((1, ROWS), F32)
    if first:
        outs = [pltpu.HBM((HEAD, ROWS), F32), stat, stat]
        out_specs = [row_spec(HEAD), row_spec(1), row_spec(1)]
    else:
        outs = [pltpu.HBM((ROWS, 2 * HEAD), BF16), stat]
        out_specs = [tile_spec(2 * HEAD), row_spec(1)]
    return pl.pallas_call(
        functools.partial(forward_body, first),
        out_shape=outs,
        grid=(ROWS // TILE,),
        in_specs=[
            tile_spec(HEAD),
            *[once(ROWS, 2 * HEAD)] * 2,
            once(4 * UNITS, HEAD),
            *[row_spec(x.shape[0]) for x in carry],
        ],
        out_specs=out_specs,
        scratch_shapes=[
            pltpu.VMEM((2 * ROWS, 2 * HEAD), BF16),
            pltpu.VMEM((2 * ROWS, TILE), F32),
        ],
        cost_estimate=cost(2, 2 * ROWS * ROWS),
        compiler_params=pltpu.CompilerParams(vmem_limit_bytes=GRANT),
        name="forward_near" if first else "forward_far",
    )(q, *kvs, bias, *carry)


def row_delta(g, att):
    return jnp.sum((g.astype(F32) * att.astype(F32)).T, axis=0, keepdims=True)


def query_body(pair_ref, g_ref, lse_ref, kv0, kv1, kv2, kv3, bias_ref, dq_ref, ka_ref, s_ref):
    step = pl.program_id(0)
    chunks = (kv0, kv1, kv2, kv3)

    @pl.when(step == 0)
    def _():
        fill_keys(chunks, bias_ref, ka_ref)

    qa = query_wide(pair_ref[:, :HEAD], step * (TILE // SPAN))
    g = g_ref[...]
    lse = lse_ref[...]
    delta = row_delta(g, pair_ref[:, HEAD:])
    own = pl.ds(pl.multiple_of(step * TILE, TILE), TILE)
    s_ref[...] = dot(ka_ref[pl.ds(0, ROWS), :], qa, NT)
    s_ref[own, :] = jnp.where(later_in_span(), LOW, s_ref[own, :])
    total = jnp.zeros((HEAD, TILE), F32)
    for c, kv_ref in enumerate(chunks):
        scores = dot(ka_ref[pl.ds(c * ROWS, ROWS), :], qa, NT) if c else s_ref[...]
        prob = jnp.exp(scores - lse)
        dprob = dot(kv_ref[:, HEAD:], g, NT)
        ds = (prob * (dprob - delta)).astype(BF16)
        total += dot(kv_ref[:, :HEAD], ds, TN)
    dq_ref[...] = (total * SCALE).T.astype(BF16)


def query_grad(pair, g, lse, kvs, bias):
    return pl.pallas_call(
        query_body,
        out_shape=jax.ShapeDtypeStruct((ROWS, HEAD), BF16),
        grid=(ROWS // TILE,),
        in_specs=[
            tile_spec(2 * HEAD),
            tile_spec(HEAD),
            row_spec(1),
            *[once(ROWS, 2 * HEAD)] * 4,
            once(4 * UNITS, HEAD),
        ],
        out_specs=tile_spec(HEAD),
        scratch_shapes=[
            pltpu.VMEM((4 * ROWS, 2 * HEAD), BF16),
            pltpu.VMEM((ROWS, TILE), F32),
        ],
        cost_estimate=cost(3, 4 * ROWS * ROWS),
        compiler_params=pltpu.CompilerParams(vmem_limit_bytes=WIDE_GRANT),
        name="query_grad",
    )(pair, g, lse, *kvs, bias)


def key_body(*refs):
    kv_ref, bias_ref = refs[:2]
    pairs, gs, lses = refs[2:6], refs[6:10], refs[10]
    dk_ref, dv_ref, ka_ref, s_ref, dk_acc, dv_acc = refs[11:]
    ka_ref[:, :HEAD] = kv_ref[:, :HEAD]
    ka_ref[:, HEAD:] = spread_bias(bias_ref[:UNITS, :])
    dk_acc[...] = jnp.zeros_like(dk_acc)
    dv_acc[...] = jnp.zeros_like(dv_acc)

    def tile(i, _):
        rows = pl.ds(pl.multiple_of(i * TILE, TILE), TILE)
        dk = jnp.zeros((ROWS, HEAD), F32)
        dv = jnp.zeros((ROWS, HEAD), F32)
        for c in range(4):
            q = pairs[c][rows, :HEAD]
            g = gs[c][rows, :]
            lse = lses[c : c + 1, rows]
            delta = row_delta(g, pairs[c][rows, HEAD:])
            qa = query_wide(q, i * (TILE // SPAN) + c * UNITS)
            scores = dot(ka_ref[...], qa, NT)
            if c == 0:
                s_ref[...] = scores
                s_ref[rows, :] = jnp.where(later_in_span(), LOW, s_ref[rows, :])
                scores = s_ref[...]
            prob = jnp.exp(scores - lse)
            dprob = dot(kv_ref[:, HEAD:], g, NT)
            ds = (prob * (dprob - delta)).astype(BF16)
            dv += dot(prob.astype(BF16), g, NN)
            dk += dot(ds, q, NN)
        dk_acc[...] += dk
        dv_acc[...] += dv
        return 0

    lax.fori_loop(0, ROWS // TILE, tile, 0)
    dk_ref[...] = (dk_acc[...] * SCALE).astype(BF16)
    dv_ref[...] = dv_acc[...].astype(BF16)


def key_grad(kv, bias, pairs, gs, lses):
    return pl.pallas_call(
        key_body,
        out_shape=[jax.ShapeDtypeStruct((ROWS, HEAD), BF16)] * 2,
        grid=(1,),
        in_specs=[
            once(ROWS, 2 * HEAD),
            once(4 * UNITS, HEAD),
            *[once(ROWS, 2 * HEAD)] * 4,
            *[once(ROWS, HEAD)] * 4,
            once(4, ROWS),
        ],
        out_specs=[once(ROWS, HEAD)] * 2,
        scratch_shapes=[
            pltpu.VMEM((ROWS, 2 * HEAD), BF16),
            pltpu.VMEM((ROWS, TILE), F32),
            pltpu.VMEM((ROWS, HEAD), F32),
            pltpu.VMEM((ROWS, HEAD), F32),
        ],
        cost_estimate=cost(4, 4 * ROWS * ROWS),
        compiler_params=pltpu.CompilerParams(vmem_limit_bytes=WIDE_GRANT),
        name="key_grad",
    )(kv, bias, *pairs, *gs, lses)


ZY = ("z", "y")
CHIPS = ("z", "y", "xl", "xh")
SWAP = [(0, 1), (1, 0)]


def other_core(x):
    return lax.ppermute(x, "core", SWAP)


def other_chip(x):
    return lax.ppermute(x, "xl", SWAP)


def everyone(x):
    far = other_chip(x)
    return x, other_core(x), far, other_core(far)


def exchange(x, axes):
    return lax.all_to_all(x, axes, 0, 0, tiled=True)


def in_order(first, own, peer):
    return jnp.stack([jnp.where(first, own, peer), jnp.where(first, peer, own)])


def span_bias(span_order, block_mask, xl, core):
    count = span_order.shape[0]
    row = jnp.arange(count, dtype=jnp.int32)
    owner, unit = row // UNITS, row % UNITS
    row_xl = xl ^ (owner // 2)
    half = core ^ (owner % 2) ^ ((unit // 4 + unit % 4) % 2)
    storage = 2 * (2 * unit + row_xl) + half
    held = (storage[:, None] == jnp.arange(count, dtype=jnp.int32)[None, :]).astype(jnp.int32)
    position = jnp.sum(held * span_order[None, :], axis=1)
    hot = (position[:, None] == jnp.arange(count, dtype=jnp.int32)[None, :]).astype(F32)
    pairs = jnp.dot(hot, jnp.dot(block_mask.astype(F32).T, hot.T))
    allowed = (pairs > 0.5) & (position[:, None] <= position[None, :])
    bias = jnp.where(allowed, 0.0, LOW).astype(F32)
    return jnp.pad(bias, ((0, 0), (0, HEAD - count)))


def side_by_side(first, own, peer):
    return jnp.concatenate([jnp.where(first, own, peer), jnp.where(first, peer, own)], axis=-1)


def across(x):
    return lax.ppermute(x, ("xl", "xh"), [(k, k ^ 3) for k in range(4)])


def weight_body(xl_ref, own0, own1, other0, other1, up_ref, out_ref, keep_ref, send_ref, w_ref):
    for flip, pieces in enumerate(((own0, own1), (other0, other1))):
        for units, part in zip((slice(0, MANY), slice(MANY, UNITS)), pieces):
            for c in range(2):
                rows = part[:, c * 32 : (c + 1) * 32, :]
                w_ref[units, xl_ref[0] ^ flip, :, c * 512 : (c + 1) * 512] = rows
    weight = w_ref[...].reshape(1024, 1024)
    out_ref[...] = weight
    for rows, out in ((slice(0, 128), keep_ref), (slice(128, 256), send_ref)):
        out[...] = dot(up_ref[rows, :], weight, NT)


def weight_whole(xl, own, other, up):
    return pl.pallas_call(
        weight_body,
        out_shape=[
            pltpu.HBM((1024, 1024), BF16),
            jax.ShapeDtypeStruct((128, 1024), F32),
            jax.ShapeDtypeStruct((128, 1024), F32),
        ],
        grid=(1,),
        in_specs=[pl.BlockSpec(memory_space=pltpu.SMEM)]
        + [once(*x.shape) for x in (*own, *other, up)],
        out_specs=[once(1024, 1024), once(128, 1024), once(128, 1024)],
        scratch_shapes=[pltpu.VMEM((UNITS, 2, 32, 1024), BF16)],
        cost_estimate=pl.CostEstimate(
            flops=2 * 256 * 1024 * 1024, bytes_accessed=4 << 20, transcendentals=0
        ),
        compiler_params=pltpu.CompilerParams(vmem_limit_bytes=GRANT),
        name="weight_whole",
    )(xl, *own, *other, up)


def term_body(own_ref, peer_ref, up_ref, out_ref, token_ref):
    token_ref[...] = jnp.zeros_like(token_ref)
    att = jnp.concatenate([own_ref[...], peer_ref[...]], axis=0)
    for c in range(2):
        cols = slice(c * 512, (c + 1) * 512)
        out_ref[:, cols] = dot(att, up_ref[:, cols], TN).astype(BF16)


def weight_terms(own, peer, up):
    return pl.pallas_call(
        term_body,
        out_shape=[pltpu.HBM((1024, 1024), BF16), jax.ShapeDtypeStruct((8, HEAD), F32)],
        grid=(1,),
        in_specs=[once(128, 1024), once(128, 1024), once(256, 1024)],
        out_specs=[once(1024, 1024), once(8, HEAD)],
        cost_estimate=pl.CostEstimate(
            flops=2 * 256 * 1024 * 1024, bytes_accessed=4 << 20, transcendentals=0
        ),
        compiler_params=pltpu.CompilerParams(vmem_limit_bytes=GRANT),
        name="weight_terms",
    )(own, peer, up)


IN_SMEM = pl.BlockSpec(memory_space=pltpu.SMEM)


def move(body, name, outs, scalars, *arrays, space=jax.ShapeDtypeStruct, after=()):
    spaces = space if isinstance(space, list) else [space] * len(outs)
    read = len(scalars) + len(arrays)

    def run(*refs):
        body(*refs[:read], *refs[read + len(after) :])

    return pl.pallas_call(
        run,
        out_shape=[make(shape, BF16) for make, shape in zip(spaces, outs)],
        grid=(1,),
        in_specs=[IN_SMEM] * len(scalars)
        + [once(*x.shape) for x in arrays]
        + [pl.BlockSpec(memory_space=pl.ANY)] * len(after),
        out_specs=[once(*shape) for shape in outs],
        cost_estimate=pl.CostEstimate(flops=0, bytes_accessed=4 << 20, transcendentals=0),
        compiler_params=pltpu.CompilerParams(vmem_limit_bytes=GRANT),
        name=name,
    )(*scalars, *arrays, *after)


def head_cols(h):
    return slice(h * HEAD, (h + 1) * HEAD)


def span_rows(half):
    return pl.ds(pl.multiple_of(half * SPAN, SPAN), SPAN)


def cut_body(half_ref, q_ref, k_ref, v_ref, own_ref, sent_ref):
    for side, out in enumerate((own_ref, sent_ref)):
        rows = span_rows(half_ref[0] ^ side)
        for t, x in enumerate((q_ref, k_ref, v_ref)):
            for h in range(HEADS):
                out[h, :, head_cols(t)] = x[rows, head_cols(h)]


def fill_body(core_ref, xh_ref, xl_ref, own_ref, peer_ref, w0, w1, w2, w3, out_ref):
    core, xh = core_ref[0], xh_ref[0]
    out_ref[pl.ds(core * HEADS, HEADS), :, : 3 * HEAD] = own_ref[...]
    out_ref[pl.ds((1 - core) * HEADS, HEADS), :, : 3 * HEAD] = peer_ref[...]
    first, mine_first = core == 0, xh == 0
    w = [jnp.where(first, x[:, :1024], x[:, 1024:]).astype(F32) for x in (w0, w1, w2, w3)]
    near = [jnp.where(first, w[0], w[1]), jnp.where(first, w[1], w[0])]
    far = [jnp.where(first, w[2], w[3]), jnp.where(first, w[3], w[2])]
    front = [jnp.where(mine_first, a, b) for a, b in zip(near, far)]
    back = [jnp.where(mine_first, b, a) for a, b in zip(near, far)]
    rows = jnp.concatenate(front + back, axis=0).astype(BF16)
    for c in range(2):
        part = rows[:, c * 512 : (c + 1) * 512]
        for unit in range(UNITS):
            out_ref[unit, c * 32 : (c + 1) * 32, 3 * HEAD :] = part


def up_body(core_ref, half_ref, own_ref, peer_ref, out_ref):
    core, half = core_ref[0], half_ref[0]
    for side in range(2):
        rows = span_rows(half ^ side)
        wide = own_ref[rows, :]
        mine = jnp.where(core == 0, wide[:, :1024], wide[:, 1024:])
        out_ref[span_rows(2 * side + core), :] = mine
        out_ref[span_rows(2 * side + 1 - core), :] = peer_ref[rows, :]


def split_body(x_ref, q_ref, kv_ref, w0_ref, w1_ref):
    x = x_ref[...]
    q_ref[...] = x[:, :, :HEAD].reshape(ROWS, HEAD)
    kv_ref[...] = x[:, :, HEAD : 3 * HEAD].reshape(ROWS, 2 * HEAD)
    w0_ref[...] = x[:MANY, :, 3 * HEAD :]
    w1_ref[...] = x[MANY:, :, 3 * HEAD :]


def cross_body(pair_ref, own_ref, peer_ref, out_ref):
    for s in range(2):
        for h in range(HEADS):
            unit, rows = s * HEADS + h, slice(s * SPAN, (s + 1) * SPAN)
            out_ref[unit, :, :HEAD] = pair_ref[unit * SPAN : (unit + 1) * SPAN, HEAD:]
            total = own_ref[rows, head_cols(h)] + peer_ref[rows, head_cols(h)]
            out_ref[unit, :, HEAD:] = total.astype(BF16)


def land_body(x_ref, att_ref, g_ref):
    g_ref[...] = x_ref[:, :, HEAD:].reshape(ROWS, HEAD)
    for s in range(2):
        for h in range(HEADS):
            att_ref[s * SPAN : (s + 1) * SPAN, head_cols(h)] = x_ref[s * HEADS + h, :, :HEAD]


def final_body(core_ref, half_ref, own_ref, peer_ref, dq_ref, dk_ref, dv_ref):
    core, half = core_ref[0], half_ref[0]
    for t, out in enumerate((dq_ref, dk_ref, dv_ref)):
        for h in range(HEADS):
            out[span_rows(half), head_cols(h)] = own_ref[core * HEADS + h, :, head_cols(t)]
            out[span_rows(1 - half), head_cols(h)] = peer_ref[h, :, head_cols(t)]


def local(query_states, key_states, value_states, span_order, block_mask, output_weight, upstream):
    z, y, xl, xh, core = (lax.axis_index(a) for a in ("z", "y", "xl", "xh", "core"))
    half = core ^ ((z + y) % 2)
    core_1, xl_1, xh_1, half_1 = (x.reshape(1) for x in (core, xl, xh, half))
    cols = output_weight.shape[1] // 2

    wide = upstream[0]
    up_sent = jnp.where(core == 0, wide[:, cols:], wide[:, :cols])
    (up,) = move(
        up_body,
        "up",
        [(4 * SPAN, cols)],
        [core_1, half_1],
        in_hbm(wide),
        other_core(up_sent),
        space=pltpu.HBM,
    )

    weight_far = lax.ppermute(output_weight, "xh", SWAP)
    weight_rows = [in_hbm(output_weight), other_core(output_weight), weight_far, other_core(weight_far)]
    unit_rows = (HEADS, SPAN, 3 * HEAD)
    own, sent = move(
        cut_body,
        "cut",
        [unit_rows] * 2,
        [half_1],
        in_hbm(query_states[0]),
        in_hbm(key_states[0]),
        in_hbm(value_states[0]),
        space=pltpu.HBM,
    )
    (blocks,) = move(
        fill_body,
        "fill",
        [(UNITS, SPAN, 3 * HEAD + 512)],
        [core_1, xh_1, xl_1],
        in_hbm(own),
        other_core(sent),
        *weight_rows,
        after=(in_hbm(up),),
    )
    blocks = exchange(blocks, ZY)
    q, own_kv, *weight_own = move(
        split_body,
        "split",
        [(ROWS, HEAD), (ROWS, 2 * HEAD), (MANY, SPAN, 512), (UNITS - MANY, SPAN, 512)],
        [],
        blocks,
        space=pltpu.HBM,
    )
    far_kv = other_chip(own_kv)
    weight_other = [across(weight_own[0]), other_chip(weight_own[1])]
    near_kv = other_core(own_kv)
    own_kv, span_order, side, which = lax.optimization_barrier((own_kv, span_order, xl, core))
    first_core = which == 0
    bias = span_bias(span_order, block_mask, side, which)


    out, top, total = forward(True, in_hbm(q), (in_hbm(own_kv), near_kv), bias)
    far_kv, total = lax.optimization_barrier((far_kv, total))
    kvs = (own_kv, near_kv, far_kv, other_core(far_kv))
    pair, lse = forward(False, in_hbm(q), kvs[2:], bias, in_hbm(out), top, total)
    lses = jnp.concatenate([lse, other_core(lse)], axis=0)
    lses = jnp.concatenate([lses, other_chip(lses)], axis=0)

    place, lse = lax.optimization_barrier((xl_1, lse))
    weight, grad_own, grad_sent = weight_whole(
        place, [in_hbm(x) for x in weight_own], weight_other, in_hbm(up)
    )
    (crossing,) = move(
        cross_body,
        "cross",
        [(UNITS, SPAN, 2 * HEAD)],
        [],
        in_hbm(pair),
        grad_own,
        other_core(grad_sent),
    )
    crossed = exchange(crossing, ZY)
    pair_sent, lses = lax.optimization_barrier((pair, lses))
    pair_far = other_chip(pair_sent)

    att_own, g = move(
        land_body,
        "land",
        [(2 * SPAN, HEADS * HEAD), (ROWS, HEAD)],
        [],
        crossed,
        after=(lses,),
        space=[jax.ShapeDtypeStruct, pltpu.HBM],
    )
    gs = everyone(g)
    att_peer = other_core(att_own)
    term, token = weight_terms(att_own, att_peer, in_hbm(up))
    term = exchange(term.reshape(UNITS, SPAN, cols), ZY)
    weight, pair_far, token = lax.optimization_barrier((weight, pair_far, token))
    pairs = (pair_sent, other_core(pair_sent), pair_far, other_core(pair_far))

    query_out = query_grad(in_hbm(pair), in_hbm(g), lse, [in_hbm(x) for x in kvs], bias)
    key_out, value_out = key_grad(in_hbm(own_kv), bias, pairs, gs, lses)
    grads = [x.reshape(UNITS, SPAN, HEAD) for x in (query_out, key_out, value_out)]
    grads = exchange(jnp.concatenate(grads, axis=2), ZY)

    def project(att):
        return dot(att, weight, NN).astype(BF16).reshape(2, SPAN, cols)

    own, peer = project(att_own), project(att_peer)
    kept = [lax.dynamic_index_in_dim(x, core, 0, False) for x in (own, peer)]
    gone = jnp.stack([lax.dynamic_index_in_dim(x, 1 - core, 0, False) for x in (own, peer)])
    gone = other_core(gone)
    own = in_order(half == 0, kept[0], kept[1]).reshape(2 * SPAN, cols)
    peer = in_order(half == 0, gone[1], gone[0]).reshape(2 * SPAN, cols)
    projected = side_by_side(first_core, own, peer)

    summed = jnp.sum(term.astype(F32), axis=0).reshape(4, 16, cols)
    chip = 2 * xl + xh
    total = lax.dynamic_index_in_dim(summed, chip, 0, False)
    for step in (1, 2, 3):
        part = lax.dynamic_index_in_dim(summed, chip ^ step, 0, False)
        total = total + lax.ppermute(part, ("xl", "xh"), [(k, k ^ step) for k in range(4)])
    total = total.reshape(2, -1, cols)
    own = lax.dynamic_index_in_dim(total, core, 0, False)
    peer = other_core(lax.dynamic_index_in_dim(total, 1 - core, 0, False))
    weight_gradient = side_by_side(first_core, own, peer)

    peer = other_core(lax.dynamic_slice_in_dim(grads, (1 - core) * HEADS, HEADS, 0))
    own_rows = (2 * SPAN, HEADS * HEAD)
    query_gradient, key_gradient, value_gradient = move(
        final_body, "final", [own_rows] * 3, [core_1, half_1], grads, peer, after=(token,)
    )
    return (
        projected[None],
        query_gradient[None],
        key_gradient[None],
        value_gradient[None],
        weight_gradient,
    )


def solution(mesh):
    axes = ("z", "y", "xl", "xh", "core")
    fine = Mesh(mesh.devices.reshape(4, 4, 2, 2, 2), axes)
    rows = P(("xh", "core"), ("z", "y", "xl"), None)
    return jax.shard_map(
        local,
        mesh=fine,
        in_specs=(rows, rows, rows, P(), P(), P(axes, None), rows),
        out_specs=(rows, rows, rows, rows, P(axes, None)),
        check_vma=False,
    )
```

```python
import functools

import jax
import jax.numpy as jnp
from jax import lax
from jax.experimental import pallas as pl
from jax.experimental.pallas import tpu as pltpu
from jax.sharding import Mesh, PartitionSpec as P

HEADS = 8
HEAD = 128
SPAN = 64
UNITS = 16
MANY = 12
ROWS = UNITS * SPAN
TILE = 256
LOW = -1e30
GRANT = 16 << 20
WIDE_GRANT = 32 << 20
SCALE = 1.0 / HEAD
F32 = jnp.float32
BF16 = jnp.bfloat16
NT = (((1,), (1,)), ((), ()))
NN = (((1,), (0,)), ((), ()))
TN = (((0,), (0,)), ((), ()))


def in_hbm(x):
    return pltpu.with_memory_space_constraint(x, pltpu.HBM)


def dot(a, b, dims):
    return lax.dot_general(a, b, dims, preferred_element_type=F32)


def span_hot(first_span):
    span = lax.broadcasted_iota(jnp.int32, (TILE, HEAD), 0) // SPAN + first_span
    lane = lax.broadcasted_iota(jnp.int32, (TILE, HEAD), 1)
    return (span == lane).astype(F32).astype(BF16)


def query_wide(query, first_span):
    return jnp.concatenate([query * BF16(SCALE), span_hot(first_span)], axis=1)


def spread_bias(bias):
    return jnp.broadcast_to(bias[:, None, :], (UNITS, SPAN, HEAD)).reshape(ROWS, HEAD).astype(BF16)


def fill_keys(chunks, bias_ref, ka_ref, first_chunk=0):
    for c, kv_ref in enumerate(chunks):
        rows = pl.ds(c * ROWS, ROWS)
        spans = slice((first_chunk + c) * UNITS, (first_chunk + c + 1) * UNITS)
        ka_ref[rows, :HEAD] = kv_ref[:, :HEAD]
        ka_ref[rows, HEAD:] = spread_bias(bias_ref[spans, :])


def later_in_span():
    key = lax.broadcasted_iota(jnp.int32, (TILE, TILE), 0)
    query = lax.broadcasted_iota(jnp.int32, (TILE, TILE), 1)
    return (key // SPAN == query // SPAN) & (key > query)


def forward_body(first, *refs):
    if first:
        q_ref, kv0, kv1, bias_ref, o_ref, m_ref, l_ref, ka_ref, s_ref = refs
    else:
        q_ref, kv0, kv1, bias_ref, o0_ref, m0_ref, l0_ref, pair_ref, lse_ref, ka_ref, s_ref = refs
    step = pl.program_id(0)
    chunks = (kv0, kv1)

    @pl.when(step == 0)
    def _():
        fill_keys(chunks, bias_ref, ka_ref, 0 if first else 2)

    q = q_ref[...]
    qa = query_wide(q, step * (TILE // SPAN))
    top = None if first else m0_ref[...]
    for c in range(2):
        rows = pl.ds(c * ROWS, ROWS)
        s_ref[rows, :] = dot(ka_ref[rows, :], qa, NT)
        if first and c == 0:
            own = pl.ds(pl.multiple_of(step * TILE, TILE), TILE)
            s_ref[own, :] = jnp.where(later_in_span(), LOW, s_ref[own, :])
        chunk_top = jnp.max(s_ref[rows, :], axis=0, keepdims=True)
        top = chunk_top if top is None else jnp.maximum(top, chunk_top)
    total = jnp.zeros((1, TILE), F32)
    out = jnp.zeros((HEAD, TILE), F32)
    for c, kv_ref in enumerate(chunks):
        weights = jnp.exp(s_ref[pl.ds(c * ROWS, ROWS), :] - top)
        total += jnp.sum(weights, axis=0, keepdims=True)
        out += dot(kv_ref[:, HEAD:], weights.astype(BF16), TN)
    if first:
        o_ref[...] = out
        m_ref[...] = top
        l_ref[...] = total
    else:
        fade = jnp.exp(m0_ref[...] - top)
        total += l0_ref[...] * fade
        out = (out + o0_ref[...] * fade) / total
        pair_ref[:, :HEAD] = q
        pair_ref[:, HEAD:] = out.T.astype(BF16)
        lse_ref[...] = top + jnp.log(total)


def tile_spec(cols):
    return pl.BlockSpec((TILE, cols), lambda i: (i, 0))


def row_spec(rows):
    return pl.BlockSpec((rows, TILE), lambda i: (0, i))


def cost(matmuls, pairs):
    return pl.CostEstimate(
        flops=matmuls * 2 * pairs * 2 * HEAD, bytes_accessed=4 << 20, transcendentals=pairs
    )


def once(*shape):
    return pl.BlockSpec(shape, lambda i: (0,) * len(shape), pipeline_mode=pl.Buffered(1))


def forward(first, q, kvs, bias, *carry):
    stat = jax.ShapeDtypeStruct((1, ROWS), F32)
    if first:
        outs = [pltpu.HBM((HEAD, ROWS), F32), stat, stat]
        out_specs = [row_spec(HEAD), row_spec(1), row_spec(1)]
    else:
        outs = [pltpu.HBM((ROWS, 2 * HEAD), BF16), stat]
        out_specs = [tile_spec(2 * HEAD), row_spec(1)]
    return pl.pallas_call(
        functools.partial(forward_body, first),
        out_shape=outs,
        grid=(ROWS // TILE,),
        in_specs=[
            tile_spec(HEAD),
            *[once(ROWS, 2 * HEAD)] * 2,
            once(4 * UNITS, HEAD),
            *[row_spec(x.shape[0]) for x in carry],
        ],
        out_specs=out_specs,
        scratch_shapes=[
            pltpu.VMEM((2 * ROWS, 2 * HEAD), BF16),
            pltpu.VMEM((2 * ROWS, TILE), F32),
        ],
        cost_estimate=cost(2, 2 * ROWS * ROWS),
        compiler_params=pltpu.CompilerParams(vmem_limit_bytes=GRANT),
        name="forward_near" if first else "forward_far",
    )(q, *kvs, bias, *carry)


def row_delta(g, att):
    return jnp.sum((g.astype(F32) * att.astype(F32)).T, axis=0, keepdims=True)


def query_body(pair_ref, g_ref, lse_ref, kv0, kv1, kv2, kv3, bias_ref, dq_ref, ka_ref, s_ref):
    step = pl.program_id(0)
    chunks = (kv0, kv1, kv2, kv3)

    @pl.when(step == 0)
    def _():
        fill_keys(chunks, bias_ref, ka_ref)

    qa = query_wide(pair_ref[:, :HEAD], step * (TILE // SPAN))
    g = g_ref[...]
    lse = lse_ref[...]
    delta = row_delta(g, pair_ref[:, HEAD:])
    own = pl.ds(pl.multiple_of(step * TILE, TILE), TILE)
    s_ref[...] = dot(ka_ref[pl.ds(0, ROWS), :], qa, NT)
    s_ref[own, :] = jnp.where(later_in_span(), LOW, s_ref[own, :])
    total = jnp.zeros((HEAD, TILE), F32)
    for c, kv_ref in enumerate(chunks):
        scores = dot(ka_ref[pl.ds(c * ROWS, ROWS), :], qa, NT) if c else s_ref[...]
        prob = jnp.exp(scores - lse)
        dprob = dot(kv_ref[:, HEAD:], g, NT)
        ds = (prob * (dprob - delta)).astype(BF16)
        total += dot(kv_ref[:, :HEAD], ds, TN)
    dq_ref[...] = (total * SCALE).T.astype(BF16)


def query_grad(pair, g, lse, kvs, bias):
    return pl.pallas_call(
        query_body,
        out_shape=jax.ShapeDtypeStruct((ROWS, HEAD), BF16),
        grid=(ROWS // TILE,),
        in_specs=[
            tile_spec(2 * HEAD),
            tile_spec(HEAD),
            row_spec(1),
            *[once(ROWS, 2 * HEAD)] * 4,
            once(4 * UNITS, HEAD),
        ],
        out_specs=tile_spec(HEAD),
        scratch_shapes=[
            pltpu.VMEM((4 * ROWS, 2 * HEAD), BF16),
            pltpu.VMEM((ROWS, TILE), F32),
        ],
        cost_estimate=cost(3, 4 * ROWS * ROWS),
        compiler_params=pltpu.CompilerParams(vmem_limit_bytes=WIDE_GRANT),
        name="query_grad",
    )(pair, g, lse, *kvs, bias)


def key_body(*refs):
    kv_ref, bias_ref = refs[:2]
    pairs, gs, lses = refs[2:6], refs[6:10], refs[10]
    dk_ref, dv_ref, ka_ref, s_ref, dk_acc, dv_acc = refs[11:]
    ka_ref[:, :HEAD] = kv_ref[:, :HEAD]
    ka_ref[:, HEAD:] = spread_bias(bias_ref[:UNITS, :])
    dk_acc[...] = jnp.zeros_like(dk_acc)
    dv_acc[...] = jnp.zeros_like(dv_acc)

    def tile(i, _):
        rows = pl.ds(pl.multiple_of(i * TILE, TILE), TILE)
        dk = jnp.zeros((ROWS, HEAD), F32)
        dv = jnp.zeros((ROWS, HEAD), F32)
        for c in range(4):
            q = pairs[c][rows, :HEAD]
            g = gs[c][rows, :]
            lse = lses[c : c + 1, rows]
            delta = row_delta(g, pairs[c][rows, HEAD:])
            qa = query_wide(q, i * (TILE // SPAN) + c * UNITS)
            scores = dot(ka_ref[...], qa, NT)
            if c == 0:
                s_ref[...] = scores
                s_ref[rows, :] = jnp.where(later_in_span(), LOW, s_ref[rows, :])
                scores = s_ref[...]
            prob = jnp.exp(scores - lse)
            dprob = dot(kv_ref[:, HEAD:], g, NT)
            ds = (prob * (dprob - delta)).astype(BF16)
            dv += dot(prob.astype(BF16), g, NN)
            dk += dot(ds, q, NN)
        dk_acc[...] += dk
        dv_acc[...] += dv
        return 0

    lax.fori_loop(0, ROWS // TILE, tile, 0)
    dk_ref[...] = (dk_acc[...] * SCALE).astype(BF16)
    dv_ref[...] = dv_acc[...].astype(BF16)


def key_grad(kv, bias, pairs, gs, lses):
    return pl.pallas_call(
        key_body,
        out_shape=[jax.ShapeDtypeStruct((ROWS, HEAD), BF16)] * 2,
        grid=(1,),
        in_specs=[
            once(ROWS, 2 * HEAD),
            once(4 * UNITS, HEAD),
            *[once(ROWS, 2 * HEAD)] * 4,
            *[once(ROWS, HEAD)] * 4,
            once(4, ROWS),
        ],
        out_specs=[once(ROWS, HEAD)] * 2,
        scratch_shapes=[
            pltpu.VMEM((ROWS, 2 * HEAD), BF16),
            pltpu.VMEM((ROWS, TILE), F32),
            pltpu.VMEM((ROWS, HEAD), F32),
            pltpu.VMEM((ROWS, HEAD), F32),
        ],
        cost_estimate=cost(4, 4 * ROWS * ROWS),
        compiler_params=pltpu.CompilerParams(vmem_limit_bytes=WIDE_GRANT),
        name="key_grad",
    )(kv, bias, *pairs, *gs, lses)


ZY = ("z", "y")
CHIPS = ("z", "y", "xl", "xh")
SWAP = [(0, 1), (1, 0)]


def other_core(x):
    return lax.ppermute(x, "core", SWAP)


def other_chip(x):
    return lax.ppermute(x, "xl", SWAP)


def everyone(x):
    far = other_chip(x)
    return x, other_core(x), far, other_core(far)


def exchange(x, axes):
    return lax.all_to_all(x, axes, 0, 0, tiled=True)


def in_order(first, own, peer):
    return jnp.stack([jnp.where(first, own, peer), jnp.where(first, peer, own)])


def span_bias(span_order, block_mask, xl, core):
    count = span_order.shape[0]
    row = jnp.arange(count, dtype=jnp.int32)
    owner, unit = row // UNITS, row % UNITS
    row_xl = xl ^ (owner // 2)
    half = core ^ (owner % 2) ^ ((unit // 4 + unit % 4) % 2)
    storage = 2 * (2 * unit + row_xl) + half
    held = (storage[:, None] == jnp.arange(count, dtype=jnp.int32)[None, :]).astype(jnp.int32)
    position = jnp.sum(held * span_order[None, :], axis=1)
    hot = (position[:, None] == jnp.arange(count, dtype=jnp.int32)[None, :]).astype(F32)
    pairs = jnp.dot(hot, jnp.dot(block_mask.astype(F32).T, hot.T))
    allowed = (pairs > 0.5) & (position[:, None] <= position[None, :])
    bias = jnp.where(allowed, 0.0, LOW).astype(F32)
    return jnp.pad(bias, ((0, 0), (0, HEAD - count)))


def side_by_side(first, own, peer):
    return jnp.concatenate([jnp.where(first, own, peer), jnp.where(first, peer, own)], axis=-1)


def across(x):
    return lax.ppermute(x, ("xl", "xh"), [(k, k ^ 3) for k in range(4)])


def weight_body(xl_ref, own0, own1, other0, other1, up_ref, out_ref, keep_ref, send_ref, w_ref):
    for flip, pieces in enumerate(((own0, own1), (other0, other1))):
        for units, part in zip((slice(0, MANY), slice(MANY, UNITS)), pieces):
            for c in range(2):
                rows = part[:, c * 32 : (c + 1) * 32, :]
                w_ref[units, xl_ref[0] ^ flip, :, c * 512 : (c + 1) * 512] = rows
    weight = w_ref[...].reshape(1024, 1024)
    out_ref[...] = weight
    for rows, out in ((slice(0, 128), keep_ref), (slice(128, 256), send_ref)):
        out[...] = dot(up_ref[rows, :], weight, NT)


def weight_whole(xl, own, other, up):
    return pl.pallas_call(
        weight_body,
        out_shape=[
            pltpu.HBM((1024, 1024), BF16),
            jax.ShapeDtypeStruct((128, 1024), F32),
            jax.ShapeDtypeStruct((128, 1024), F32),
        ],
        grid=(1,),
        in_specs=[pl.BlockSpec(memory_space=pltpu.SMEM)]
        + [once(*x.shape) for x in (*own, *other, up)],
        out_specs=[once(1024, 1024), once(128, 1024), once(128, 1024)],
        scratch_shapes=[pltpu.VMEM((UNITS, 2, 32, 1024), BF16)],
        cost_estimate=pl.CostEstimate(
            flops=2 * 256 * 1024 * 1024, bytes_accessed=4 << 20, transcendentals=0
        ),
        compiler_params=pltpu.CompilerParams(vmem_limit_bytes=GRANT),
        name="weight_whole",
    )(xl, *own, *other, up)


def term_body(own_ref, peer_ref, up_ref, out_ref, token_ref):
    token_ref[...] = jnp.zeros_like(token_ref)
    att = jnp.concatenate([own_ref[...], peer_ref[...]], axis=0)
    for c in range(2):
        cols = slice(c * 512, (c + 1) * 512)
        out_ref[:, cols] = dot(att, up_ref[:, cols], TN).astype(BF16)


def weight_terms(own, peer, up):
    return pl.pallas_call(
        term_body,
        out_shape=[pltpu.HBM((1024, 1024), BF16), jax.ShapeDtypeStruct((8, HEAD), F32)],
        grid=(1,),
        in_specs=[once(128, 1024), once(128, 1024), once(256, 1024)],
        out_specs=[once(1024, 1024), once(8, HEAD)],
        cost_estimate=pl.CostEstimate(
            flops=2 * 256 * 1024 * 1024, bytes_accessed=4 << 20, transcendentals=0
        ),
        compiler_params=pltpu.CompilerParams(vmem_limit_bytes=GRANT),
        name="weight_terms",
    )(own, peer, up)


IN_SMEM = pl.BlockSpec(memory_space=pltpu.SMEM)


def move(body, name, outs, scalars, *arrays, space=jax.ShapeDtypeStruct, after=()):
    spaces = space if isinstance(space, list) else [space] * len(outs)
    read = len(scalars) + len(arrays)

    def run(*refs):
        body(*refs[:read], *refs[read + len(after) :])

    return pl.pallas_call(
        run,
        out_shape=[make(shape, BF16) for make, shape in zip(spaces, outs)],
        grid=(1,),
        in_specs=[IN_SMEM] * len(scalars)
        + [once(*x.shape) for x in arrays]
        + [pl.BlockSpec(memory_space=pl.ANY)] * len(after),
        out_specs=[once(*shape) for shape in outs],
        cost_estimate=pl.CostEstimate(flops=0, bytes_accessed=4 << 20, transcendentals=0),
        compiler_params=pltpu.CompilerParams(vmem_limit_bytes=GRANT),
        name=name,
    )(*scalars, *arrays, *after)


def head_cols(h):
    return slice(h * HEAD, (h + 1) * HEAD)


def span_rows(half):
    return pl.ds(pl.multiple_of(half * SPAN, SPAN), SPAN)


def cut_body(half_ref, q_ref, k_ref, v_ref, own_ref, sent_ref):
    for side, out in enumerate((own_ref, sent_ref)):
        rows = span_rows(half_ref[0] ^ side)
        for t, x in enumerate((q_ref, k_ref, v_ref)):
            for h in range(HEADS):
                out[h, :, head_cols(t)] = x[rows, head_cols(h)]


def fill_body(core_ref, xh_ref, xl_ref, own_ref, peer_ref, w0, w1, w2, w3, out_ref):
    core, xh = core_ref[0], xh_ref[0]
    out_ref[pl.ds(core * HEADS, HEADS), :, : 3 * HEAD] = own_ref[...]
    out_ref[pl.ds((1 - core) * HEADS, HEADS), :, : 3 * HEAD] = peer_ref[...]
    first, mine_first = core == 0, xh == 0
    w = [jnp.where(first, x[:, :1024], x[:, 1024:]).astype(F32) for x in (w0, w1, w2, w3)]
    near = [jnp.where(first, w[0], w[1]), jnp.where(first, w[1], w[0])]
    far = [jnp.where(first, w[2], w[3]), jnp.where(first, w[3], w[2])]
    front = [jnp.where(mine_first, a, b) for a, b in zip(near, far)]
    back = [jnp.where(mine_first, b, a) for a, b in zip(near, far)]
    rows = jnp.concatenate(front + back, axis=0).astype(BF16)
    for c in range(2):
        part = rows[:, c * 512 : (c + 1) * 512]
        for unit in range(UNITS):
            out_ref[unit, c * 32 : (c + 1) * 32, 3 * HEAD :] = part


def up_body(core_ref, half_ref, own_ref, peer_ref, out_ref):
    core, half = core_ref[0], half_ref[0]
    for side in range(2):
        rows = span_rows(half ^ side)
        wide = own_ref[rows, :]
        mine = jnp.where(core == 0, wide[:, :1024], wide[:, 1024:])
        out_ref[span_rows(2 * side + core), :] = mine
        out_ref[span_rows(2 * side + 1 - core), :] = peer_ref[rows, :]


def split_body(x_ref, q_ref, kv_ref, w0_ref, w1_ref):
    x = x_ref[...]
    q_ref[...] = x[:, :, :HEAD].reshape(ROWS, HEAD)
    kv_ref[...] = x[:, :, HEAD : 3 * HEAD].reshape(ROWS, 2 * HEAD)
    w0_ref[...] = x[:MANY, :, 3 * HEAD :]
    w1_ref[...] = x[MANY:, :, 3 * HEAD :]


def cross_body(pair_ref, own_ref, peer_ref, out_ref):
    for s in range(2):
        for h in range(HEADS):
            unit, rows = s * HEADS + h, slice(s * SPAN, (s + 1) * SPAN)
            out_ref[unit, :, :HEAD] = pair_ref[unit * SPAN : (unit + 1) * SPAN, HEAD:]
            total = own_ref[rows, head_cols(h)] + peer_ref[rows, head_cols(h)]
            out_ref[unit, :, HEAD:] = total.astype(BF16)


def land_body(x_ref, att_ref, g_ref):
    g_ref[...] = x_ref[:, :, HEAD:].reshape(ROWS, HEAD)
    for s in range(2):
        for h in range(HEADS):
            att_ref[s * SPAN : (s + 1) * SPAN, head_cols(h)] = x_ref[s * HEADS + h, :, :HEAD]


def final_body(core_ref, half_ref, own_ref, peer_ref, dq_ref, dk_ref, dv_ref):
    core, half = core_ref[0], half_ref[0]
    for t, out in enumerate((dq_ref, dk_ref, dv_ref)):
        for h in range(HEADS):
            out[span_rows(half), head_cols(h)] = own_ref[core * HEADS + h, :, head_cols(t)]
            out[span_rows(1 - half), head_cols(h)] = peer_ref[h, :, head_cols(t)]


def local(query_states, key_states, value_states, span_order, block_mask, output_weight, upstream):
    z, y, xl, xh, core = (lax.axis_index(a) for a in ("z", "y", "xl", "xh", "core"))
    half = core ^ ((z + y) % 2)
    core_1, xl_1, xh_1, half_1 = (x.reshape(1) for x in (core, xl, xh, half))
    cols = output_weight.shape[1] // 2

    weight_far = lax.ppermute(output_weight, "xh", SWAP)
    weight_rows = [in_hbm(output_weight), other_core(output_weight), weight_far, other_core(weight_far)]
    unit_rows = (HEADS, SPAN, 3 * HEAD)
    own, sent = move(
        cut_body,
        "cut",
        [unit_rows] * 2,
        [half_1],
        in_hbm(query_states[0]),
        in_hbm(key_states[0]),
        in_hbm(value_states[0]),
        space=pltpu.HBM,
    )
    (blocks,) = move(
        fill_body,
        "fill",
        [(UNITS, SPAN, 3 * HEAD + 512)],
        [core_1, xh_1, xl_1],
        in_hbm(own),
        other_core(sent),
        *weight_rows,
    )
    blocks = exchange(blocks, ZY)
    q, own_kv, *weight_own = move(
        split_body,
        "split",
        [(ROWS, HEAD), (ROWS, 2 * HEAD), (MANY, SPAN, 512), (UNITS - MANY, SPAN, 512)],
        [],
        blocks,
        space=pltpu.HBM,
    )
    far_kv = other_chip(own_kv)
    weight_other = [across(weight_own[0]), other_chip(weight_own[1])]
    near_kv = other_core(own_kv)
    own_kv, span_order, wide, side, which = lax.optimization_barrier(
        (own_kv, span_order, upstream[0], xl, core)
    )
    first_core = which == 0
    bias = span_bias(span_order, block_mask, side, which)

    up_sent = jnp.where(first_core, wide[:, cols:], wide[:, :cols])

    out, top, total = forward(True, in_hbm(q), (in_hbm(own_kv), near_kv), bias)
    (up,) = move(
        up_body,
        "up",
        [(4 * SPAN, cols)],
        [core_1, half_1],
        in_hbm(wide),
        other_core(up_sent),
        space=pltpu.HBM,
        after=(total,),
    )
    far_kv, total, up = lax.optimization_barrier((far_kv, total, up))
    kvs = (own_kv, near_kv, far_kv, other_core(far_kv))
    pair, lse = forward(False, in_hbm(q), kvs[2:], bias, in_hbm(out), top, total)
    lses = jnp.concatenate([lse, other_core(lse)], axis=0)
    lses = jnp.concatenate([lses, other_chip(lses)], axis=0)

    place, lse = lax.optimization_barrier((xl_1, lse))
    weight, grad_own, grad_sent = weight_whole(
        place, [in_hbm(x) for x in weight_own], weight_other, in_hbm(up)
    )
    (crossing,) = move(
        cross_body,
        "cross",
        [(UNITS, SPAN, 2 * HEAD)],
        [],
        in_hbm(pair),
        grad_own,
        other_core(grad_sent),
    )
    crossed = exchange(crossing, ZY)
    pair_sent, lses = lax.optimization_barrier((pair, lses))
    pair_far = other_chip(pair_sent)

    att_own, g = move(
        land_body,
        "land",
        [(2 * SPAN, HEADS * HEAD), (ROWS, HEAD)],
        [],
        crossed,
        after=(lses,),
        space=[jax.ShapeDtypeStruct, pltpu.HBM],
    )
    gs = everyone(g)
    att_peer = other_core(att_own)
    term, token = weight_terms(att_own, att_peer, in_hbm(up))
    term = exchange(term.reshape(UNITS, SPAN, cols), ZY)
    weight, pair_far, token = lax.optimization_barrier((weight, pair_far, token))
    pairs = (pair_sent, other_core(pair_sent), pair_far, other_core(pair_far))

    query_out = query_grad(in_hbm(pair), in_hbm(g), lse, [in_hbm(x) for x in kvs], bias)
    key_out, value_out = key_grad(in_hbm(own_kv), bias, pairs, gs, lses)
    grads = [x.reshape(UNITS, SPAN, HEAD) for x in (query_out, key_out, value_out)]
    grads = exchange(jnp.concatenate(grads, axis=2), ZY)

    def project(att):
        return dot(att, weight, NN).astype(BF16).reshape(2, SPAN, cols)

    own, peer = project(att_own), project(att_peer)
    kept = [lax.dynamic_index_in_dim(x, core, 0, False) for x in (own, peer)]
    gone = jnp.stack([lax.dynamic_index_in_dim(x, 1 - core, 0, False) for x in (own, peer)])
    gone = other_core(gone)
    own = in_order(half == 0, kept[0], kept[1]).reshape(2 * SPAN, cols)
    peer = in_order(half == 0, gone[1], gone[0]).reshape(2 * SPAN, cols)
    projected = side_by_side(first_core, own, peer)

    summed = jnp.sum(term.astype(F32), axis=0).reshape(4, 16, cols)
    chip = 2 * xl + xh
    total = lax.dynamic_index_in_dim(summed, chip, 0, False)
    for step in (1, 2, 3):
        part = lax.dynamic_index_in_dim(summed, chip ^ step, 0, False)
        total = total + lax.ppermute(part, ("xl", "xh"), [(k, k ^ step) for k in range(4)])
    total = total.reshape(2, -1, cols)
    own = lax.dynamic_index_in_dim(total, core, 0, False)
    peer = other_core(lax.dynamic_index_in_dim(total, 1 - core, 0, False))
    weight_gradient = side_by_side(first_core, own, peer)

    peer = other_core(lax.dynamic_slice_in_dim(grads, (1 - core) * HEADS, HEADS, 0))
    own_rows = (2 * SPAN, HEADS * HEAD)
    query_gradient, key_gradient, value_gradient = move(
        final_body, "final", [own_rows] * 3, [core_1, half_1], grads, peer, after=(token,)
    )
    return (
        projected[None],
        query_gradient[None],
        key_gradient[None],
        value_gradient[None],
        weight_gradient,
    )


def solution(mesh):
    axes = ("z", "y", "xl", "xh", "core")
    fine = Mesh(mesh.devices.reshape(4, 4, 2, 2, 2), axes)
    rows = P(("xh", "core"), ("z", "y", "xl"), None)
    return jax.shard_map(
        local,
        mesh=fine,
        in_specs=(rows, rows, rows, P(), P(), P(axes, None), rows),
        out_specs=(rows, rows, rows, rows, P(axes, None)),
        check_vma=False,
    )
```
